32 devices in a mesh: groups: 2 (over y), wide: 4 (over z), expert: 2 (over x), inner: 2 (over core).
Axes of the slice: x: 2, y: 2, z: 4, core: 2. Of those that a mesh axis runs over, the one named last changes fastest.
Arguments:
- candidates: bfloat16 [4096, 1024], P(('groups', 'wide')), parts along dimension 0, may hold values from -6 to 6
- gate_weight: bfloat16 [1024, 128], replicated
- expert_in: bfloat16 [32, 1024, 2048], P('expert', None, ('wide', 'inner')), may hold values from -0.1875 to 0.1875
- expert_out: bfloat16 [32, 256, 2048], P('expert', None, ('wide', 'inner')), may hold values from -0.125 to 0.125
- norm_gain: bfloat16 [1024], replicated, may hold values from 0.099609375 to 1.8984375
- query_weight: bfloat16 [1024, 1024], P(None, ('expert', 'inner'))
- key_weight: bfloat16 [1024, 1024], P(None, ('expert', 'inner'))
- value_weight: bfloat16 [1024, 1024], P(None, ('expert', 'inner')), may hold values from -0.1875 to 0.1875
- task_weight: bfloat16 [1024, 4], replicated, may hold values from -0.1875 to 0.1875
- attn_weight: bfloat16 [1024, 4], P(('expert', 'inner')), may hold values from -0.75 to 0.75
- request_of: int32 [4096], P(('groups', 'wide')), parts along dimension 0, may hold values from 0 to 7, as said below
Outputs:
- scores: float32 [4096, 4], P(('groups', 'wide')), parts along dimension 0
The draws below stay inside these ranges and needn't reach their ends.
There are 2 independent parts, one for each index of `groups`. The reference program is written for one: setup_inputs(seed, part) draws one part's arguments, and reference() takes and returns one part's arrays. A program takes and returns all parts, laid end to end along the dimension named above; an argument that names none is the same for every part. Nothing has to cross between parts.
Inputs may be any that keep to these rules, and one draw needn't show every extreme that they name: `request_of`: candidates of a request arrive in any order over the shards. Among the 512 candidates of one shard of wide, no request has more than 128; one request has exactly 128 in every shard.
All inputs are finite; a program needn't handle non-finite values.
Results may differ from the reference program's by a relative error of at most 0.0051.
Values may be sent and summed in bfloat16 or wider, within the bound.
A program may use at most 128 MiB of HBM per device.

```python
import math
import jax
import jax.numpy as jnp
from jax import lax

D = 1024
EXPERTS = 32
FF = 2048
DE = 256
TASKS = 4
HEADS = 16
HD = 64
ROW_DEV = 512
ROWS = 2048
REQUEST_TOTAL = 8
CAP = 128
MODEL = 1024
N_WIDE = 4


def draw_gate_weight(key, part):
    first = jax.random.fold_in(key, 0)
    base = jax.random.normal(first, (D, TASKS * EXPERTS), jnp.float32) * D ** (-0.5)
    factors = jnp.full((1, TASKS * EXPERTS), 3.0, jnp.float32)
    return (base * factors).astype(jnp.bfloat16)


def paired_parts(key):
    shared = jax.random.fold_in(key, 7)
    first, second = jax.random.split(shared, 2)
    key_part = jax.random.normal(first, (MODEL, HEADS * HD), jnp.float32) * MODEL ** (-0.5)
    jitter_sample = jax.random.normal(second, (MODEL, HEADS * HD), jnp.float32) * MODEL ** (-0.5)
    return (key_part, jitter_sample)


def draw_query_weight(key, part):
    key_part, jitter_sample = paired_parts(key)
    result = jitter_sample
    return result.astype(jnp.bfloat16)


def draw_key_weight(key, part):
    key_part, jitter_sample = paired_parts(key)
    return key_part.astype(jnp.bfloat16)


def draw_request_of(key, part):
    first, second, third, fourth = jax.random.split(key, 4)
    blocks = ROWS // ROW_DEV
    place_entries = REQUEST_TOTAL * CAP
    tier_value = jax.random.randint(first, (REQUEST_TOTAL,), 0, 4)
    selected_experts = jax.random.randint(second, (), 0, REQUEST_TOTAL)
    extra_credit = jnp.where(jnp.arange(REQUEST_TOTAL) == selected_experts, 131072, tier_value * 16384)
    request_per_place = jnp.arange(place_entries, dtype=jnp.int32) // CAP
    jitter_sample = jax.random.randint(third, (blocks, place_entries), 0, 65536)
    ranking_weight = (extra_credit[request_per_place][None, :] + jitter_sample) * place_entries + jnp.arange(place_entries, dtype=jnp.int32)[None, :]
    picked = lax.top_k(ranking_weight.astype(jnp.int32), ROW_DEV)[1]
    requests = request_per_place[picked]
    shuffles = jax.vmap(lambda sub: jax.random.permutation(sub, ROW_DEV))(jax.random.split(fourth, blocks))
    mixed = jnp.take_along_axis(requests, shuffles, axis=1)
    return mixed.reshape(-1).astype(jnp.int32)


def steps_of(stream_key, dims, cuts, low, top_value):
    def one(dim, parts):
        steps = jax.random.uniform(jax.random.fold_in(jax.random.fold_in(stream_key, 6), dim), (parts,), jnp.float32, low / len(cuts), top_value / len(cuts))
        return jnp.repeat(jnp.exp(steps), dims[dim] // parts).reshape((-1,) + (1,) * (len(dims) - dim - 1))

    level = one(*cuts[0])
    for cut in cuts[1:]:
        level = level * one(*cut)
    return level


def gaussian(own_key, shape, width, limit, pieces=(), held_as=jnp.bfloat16):
    values = width * jax.random.normal(own_key, shape, jnp.float32)
    if pieces:
        values = values * steps_of(own_key, shape, pieces, -0.22, 0.18)
    return jnp.clip(values, -limit, limit).astype(held_as)


def setup_inputs(seed: int = 0, part: int = 0) -> dict:
    arg_keys = jax.random.split(jax.random.key(seed), 12)
    part_keys = jax.random.split(jax.random.fold_in(arg_keys[11], part), 12)
    return {
        "candidates": gaussian(part_keys[0], (ROWS, D), 1.0, 6.0, ((0, 4),)),
        "gate_weight": draw_gate_weight(jax.random.fold_in(arg_keys[11], 71), part),
        "expert_in": gaussian(arg_keys[2], (EXPERTS, D, FF), D ** -0.5, 0.1875, ((0, 2), (2, 8))),
        "expert_out": gaussian(arg_keys[3], (EXPERTS, DE, FF), FF ** -0.5, 0.125, ((0, 2), (2, 8))),
        "norm_gain": jnp.clip(1.0 + 0.18 * jax.random.normal(arg_keys[4], (MODEL,), jnp.float32), 0.099609375, 1.8984375).astype(jnp.bfloat16),
        "query_weight": draw_query_weight(jax.random.fold_in(arg_keys[11], 71), part),
        "key_weight": draw_key_weight(jax.random.fold_in(arg_keys[11], 71), part),
        "value_weight": gaussian(arg_keys[7], (MODEL, HEADS * HD), MODEL ** -0.5, 0.1875, ((1, 4),)),
        "task_weight": gaussian(arg_keys[8], (MODEL, TASKS), MODEL ** -0.5, 0.1875),
        "attn_weight": gaussian(arg_keys[9], (HEADS * HD, TASKS), (HEADS * HD // 16) ** -0.5, 0.75, ((0, 4),)),
        "request_of": draw_request_of(jax.random.fold_in(jax.random.fold_in(arg_keys[11], part), 71), part),
    }


def reference(candidates, gate_weight, expert_in, expert_out, norm_gain, query_weight, key_weight, value_weight, task_weight, attn_weight, request_of):
    logits = jnp.dot(candidates, gate_weight, preferred_element_type=jnp.float32).reshape(ROWS, TASKS, EXPERTS)
    gates = jax.nn.softmax(logits, axis=-1)

    def one_expert(total, index):
        w_in = expert_in[index]
        w_out = expert_out[index]
        hidden = jax.nn.relu(jnp.dot(candidates, w_in, preferred_element_type=jnp.float32)).astype(jnp.bfloat16)
        output = jnp.dot(hidden, w_out.T, preferred_element_type=jnp.float32)
        weight = lax.dynamic_index_in_dim(gates, index, 2, keepdims=False)
        return (total + weight[:, :, None] * output[:, None, :], None)
    mixed, _ = lax.scan(one_expert, jnp.zeros((ROWS, TASKS, DE), jnp.float32), jnp.arange(EXPERTS, dtype=jnp.int32))
    rep = mixed.reshape(ROWS, MODEL)
    center = lax.optimization_barrier(jnp.mean(rep, axis=1, keepdims=True))
    spread = lax.optimization_barrier(jnp.mean(jnp.square(rep - center), axis=1, keepdims=True))
    normed = ((rep - center) * lax.rsqrt(spread + 1e-05) * norm_gain.astype(jnp.float32)).astype(jnp.bfloat16)
    queries = jnp.dot(normed, query_weight, preferred_element_type=jnp.float32).astype(jnp.bfloat16)
    keys = jnp.dot(normed, key_weight, preferred_element_type=jnp.float32).astype(jnp.bfloat16)
    values = jnp.dot(normed, value_weight, preferred_element_type=jnp.float32).astype(jnp.bfloat16)
    order = jnp.argsort(request_of, stable=True).astype(jnp.int32)
    counts = lax.optimization_barrier(jnp.sum((request_of[None, :] == jnp.arange(REQUEST_TOTAL, dtype=jnp.int32)[:, None]).astype(jnp.int32), axis=1))
    offsets = (jnp.cumsum(counts) - counts).astype(jnp.int32)
    span = N_WIDE * CAP
    position = jnp.arange(span, dtype=jnp.int32)
    factor = 1.0 / math.sqrt(HD)

    def one_request(index):
        rows_at = jnp.take(order, jnp.minimum(offsets[index] + position, ROWS - 1).astype(jnp.int32))
        live = position < counts[index]
        query = jnp.take(queries, rows_at, axis=0).astype(jnp.float32).reshape(span, HEADS, HD)
        key = jnp.take(keys, rows_at, axis=0).astype(jnp.float32).reshape(span, HEADS, HD)
        value = jnp.take(values, rows_at, axis=0).astype(jnp.float32).reshape(span, HEADS, HD)
        affinity = jnp.einsum('qhd,khd->hqk', query, key) * factor
        affinity = jnp.where(live[None, None, :], affinity, -1e+30)
        probs = jax.nn.softmax(affinity, axis=-1).astype(jnp.bfloat16)
        context = jnp.einsum('hqk,khd->qhd', probs.astype(jnp.float32), value).astype(jnp.bfloat16).reshape(span, HEADS * HD)
        return (jnp.dot(context, attn_weight, preferred_element_type=jnp.float32), rows_at, live)
    terms, rows_all, live_all = lax.map(one_request, jnp.arange(REQUEST_TOTAL, dtype=jnp.int32))
    target = jnp.where(live_all, rows_all, ROWS).reshape(-1).astype(jnp.int32)
    attention = jnp.zeros((ROWS, TASKS), jnp.float32).at[target].set(terms.reshape(-1, TASKS), mode='drop')
    return jnp.dot(normed, task_weight, preferred_element_type=jnp.float32) + attention
```

```python
import functools
import math

import jax
import jax.numpy as jnp
from jax import lax
from jax.experimental import pallas as pl
from jax.experimental.pallas import tpu as pltpu
from jax.sharding import PartitionSpec as P

HD = 64
ALL = ("wide", "expert", "inner")
VMEM_LIMIT = 60 * 1024 * 1024


MESH = pl.DeviceIdType.MESH


def place():
    return tuple(lax.axis_index(a) for a in ALL), tuple(lax.axis_size(a) for a in ALL)


def turn(start, step, size):
    return lax.rem(start + step, size)


def greet():
    mine, sizes = place()
    barrier = pltpu.get_barrier_semaphore()
    for axis, here, size in zip(ALL, mine, sizes):
        for step in range(1, size):
            pl.semaphore_signal(
                barrier, inc=1, device_id={axis: turn(here, step, size)}, device_id_type=MESH
            )
    pl.semaphore_wait(barrier, sum(sizes) - len(sizes))


def gather_kernel(with_ids, *refs):
    if with_ids:
        own_ref, id_ref, out_ref, ids_ref, recv, send_z, send_x, send_c, local_sem, id_r, id_s = refs
    else:
        own_ref, out_ref, recv, send_z, send_x, send_c, local_sem = refs
    (z, x, c), (nz, nx, nc) = place()
    greet()

    def copy(src, zs, xs, cs, sem, axis, target):
        return pltpu.make_async_remote_copy(
            src_ref=src,
            dst_ref=out_ref.at[zs, cs, xs],
            send_sem=sem,
            recv_sem=recv.at[zs, cs, xs],
            device_id={axis: target},
            device_id_type=MESH,
        )

    def arrived(zs, xs, cs):
        copy(out_ref.at[zs, cs, xs], zs, xs, cs, send_z.at[0], "inner", turn(c, 1, nc)).wait_recv()

    sent = []

    def push(*what):
        item = copy(*what)
        item.start()
        sent.append(item)

    def spread_x(src, k, zs):
        for step in range(1, nx):
            push(src, zs, x, c, send_x.at[k, step - 1], "expert", turn(x, step, nx))

    def spread_c(src, k, j, zs, xs):
        for step in range(1, nc):
            push(src, zs, xs, c, send_c.at[k, j, step - 1], "inner", turn(c, step, nc))

    for step in range(1, nz):
        push(own_ref, z, x, c, send_z.at[step - 1], "wide", turn(z, step, nz))
    spread_x(own_ref, 0, z)
    spread_c(own_ref, 0, 0, z, x)
    keep = pltpu.make_async_copy(own_ref, out_ref.at[z, c, x], local_sem.at[0])
    keep.start()
    if with_ids:
        id_copies = []
        for step in range(1, nz):
            item = pltpu.make_async_remote_copy(
                src_ref=id_ref,
                dst_ref=ids_ref.at[z],
                send_sem=id_s.at[step - 1],
                recv_sem=id_r.at[z],
                device_id={"wide": turn(z, step, nz)},
                device_id_type=MESH,
            )
            item.start()
            id_copies.append(item)
        ids_ref[z] = id_ref[...]

    def pass_x(k):
        zs = turn(z, k, nz)
        for step in range(1, nx):
            xs = turn(x, step, nx)
            arrived(zs, xs, c)
            spread_c(out_ref.at[zs, c, xs], k, step, zs, xs)

    for k in range(1, nz):
        zs = turn(z, k, nz)
        arrived(zs, x, c)
        spread_x(out_ref.at[zs, c, x], k, zs)
        spread_c(out_ref.at[zs, c, x], k, 0, zs, x)
        pass_x(k - 1)
    pass_x(nz - 1)
    for k in range(nz):
        for j in range(nx):
            for step in range(1, nc):
                arrived(turn(z, k, nz), turn(x, j, nx), turn(c, step, nc))
    for item in sent:
        item.wait_send()
    keep.wait()
    if with_ids:
        for step in range(1, nz):
            zs = turn(z, step, nz)
            pltpu.make_async_remote_copy(
                src_ref=id_ref,
                dst_ref=ids_ref.at[zs],
                send_sem=id_s.at[step - 1],
                recv_sem=id_r.at[zs],
                device_id={"wide": zs},
                device_id_type=MESH,
            ).wait_recv()
        for item in id_copies:
            item.wait_send()


def run_gather(own, ids, collective):
    nz, nx, nc = (lax.axis_size(a) for a in ALL)
    dma = pltpu.SemaphoreType.DMA
    with_ids = ids is not None
    shape = jax.ShapeDtypeStruct((nz, nc, nx) + own.shape, own.dtype)
    vmem = pl.BlockSpec(memory_space=pltpu.VMEM)
    anywhere = pl.BlockSpec(memory_space=pl.ANY)
    scratch = [
        dma((nz, nc, nx)),
        dma((max(nz - 1, 1),)),
        dma((nz, max(nx - 1, 1))),
        dma((nz, nx, max(nc - 1, 1))),
        dma((1,)),
    ]
    if with_ids:
        scratch += [dma((nz,)), dma((max(nz - 1, 1),))]
    out = pl.pallas_call(
        functools.partial(gather_kernel, with_ids),
        in_specs=[vmem, vmem] if with_ids else [vmem],
        out_specs=[anywhere, vmem] if with_ids else anywhere,
        out_shape=[shape, jax.ShapeDtypeStruct((nz,) + ids.shape, ids.dtype)] if with_ids else shape,
        scratch_shapes=scratch,
        compiler_params=pltpu.CompilerParams(collective_id=collective, has_side_effects=True),
    )(*([own, ids] if with_ids else [own]))
    depth = own.shape[1]
    if with_ids:
        return out[0].reshape(-1, depth), out[1].reshape(1, -1)
    return out.reshape(-1, depth)


def reduce_kernel(
    part_ref, gain_ref, out_ref, mine, core_in, x_out, x_in, z_out, z_in,
    local_sem, core_s, core_r, x_s, x_r, z_s, z_r,
):
    (z, x, c), (nz, nx, nc) = place()
    f32 = jnp.float32
    greet()
    other = turn(c, 1, nc)
    core, kept = [], []
    for k in range(nz):
        s = turn(z, k + 1, nz)
        item = pltpu.make_async_remote_copy(
            src_ref=part_ref.at[s, other],
            dst_ref=core_in.at[k],
            send_sem=core_s.at[k],
            recv_sem=core_r.at[k],
            device_id={"inner": other},
            device_id_type=MESH,
        )
        item.start()
        core.append(item)
        stay = pltpu.make_async_copy(part_ref.at[s, c], mine.at[k], local_sem.at[k])
        stay.start()
        kept.append(stay)

    def pair(k, xs):
        return mine[k, xs].astype(f32) + core_in[k, xs].astype(f32)

    across, along = [], []

    def finish(k):
        total = pair(k, x)
        for step in range(1, nx):
            across[k][step - 1].wait_recv()
            total = total + x_in[k, step - 1].astype(f32)
        if k == nz - 1:
            return total
        z_out[k] = total.astype(z_out.dtype)
        item = pltpu.make_async_remote_copy(
            src_ref=z_out.at[k],
            dst_ref=z_in.at[k],
            send_sem=z_s.at[k],
            recv_sem=z_r.at[k],
            device_id={"wide": turn(z, k + 1, nz)},
            device_id_type=MESH,
        )
        item.start()
        along.append(item)

    for k in range(nz):
        kept[k].wait()
        core[k].wait_recv()
        items = []
        for step in range(1, nx):
            xs = turn(x, step, nx)
            x_out[k, step - 1] = pair(k, xs).astype(x_out.dtype)
            item = pltpu.make_async_remote_copy(
                src_ref=x_out.at[k, step - 1],
                dst_ref=x_in.at[k, step - 1],
                send_sem=x_s.at[k, step - 1],
                recv_sem=x_r.at[k, step - 1],
                device_id={"expert": xs},
                device_id_type=MESH,
            )
            item.start()
            items.append(item)
        across.append(items)
        if k > 0:
            finish(k - 1)
    total = finish(nz - 1)
    for k in range(nz - 1):
        along[k].wait_recv()
        total = total + z_in[k].astype(f32)
    center = jnp.mean(total, axis=1, keepdims=True)
    spread = jnp.mean(jnp.square(total - center), axis=1, keepdims=True)
    normed = (total - center) * lax.rsqrt(spread + 1e-05) * gain_ref[...].astype(f32)
    out_ref[...] = normed.astype(out_ref.dtype)
    for item in core + along + [i for items in across for i in items]:
        item.wait_send()


def run_reduce(part, gain, share, collective):
    nz, nx, nc = (lax.axis_size(a) for a in ALL)
    width = part.shape[1]
    dma = pltpu.SemaphoreType.DMA
    kind = part.dtype
    part = part.reshape(nz, nc, nx, share, width)
    few = max(nx - 1, 1)
    vmem = pl.BlockSpec(memory_space=pltpu.VMEM)
    return pl.pallas_call(
        reduce_kernel,
        in_specs=[pl.BlockSpec(memory_space=pl.ANY), vmem],
        out_specs=vmem,
        out_shape=jax.ShapeDtypeStruct((share, width), kind),
        scratch_shapes=[
            pltpu.VMEM((nz, nx, share, width), kind),
            pltpu.VMEM((nz, nx, share, width), kind),
            pltpu.VMEM((nz, few, share, width), kind),
            pltpu.VMEM((nz, few, share, width), kind),
            pltpu.VMEM((nz, share, width), kind),
            pltpu.VMEM((nz, share, width), kind),
            dma((nz,)),
            dma((nz,)),
            dma((nz,)),
            dma((nz, few)),
            dma((nz, few)),
            dma((nz,)),
            dma((nz,)),
        ],
        compiler_params=pltpu.CompilerParams(
            collective_id=collective, has_side_effects=True, vmem_limit_bytes=VMEM_LIMIT
        ),
    )(part, gain)


def expert_kernel(tasks, x_ref, gate_ref, win_ref, wout_ref, out_ref, acc_ref):
    rows = x_ref.shape[0]
    columns = gate_ref.shape[1]
    experts_all = columns // tasks
    held, _, _ = win_ref.shape
    width = wout_ref.shape[1]
    x = x_ref[...]
    logits = jnp.dot(x, gate_ref[...], preferred_element_type=jnp.float32)
    task = lax.broadcasted_iota(jnp.int32, (rows, columns), 1) // experts_all
    top = jnp.zeros_like(logits)
    for t in range(tasks):
        high = jnp.max(jnp.where(task == t, logits, -jnp.inf), axis=1, keepdims=True)
        top = jnp.where(task == t, high, top)
    powers = jnp.exp(logits - top)
    total = jnp.ones_like(logits)
    for t in range(tasks):
        part = jnp.sum(jnp.where(task == t, powers, 0.0), axis=1, keepdims=True)
        total = jnp.where(task == t, part, total)
    gates = powers / total
    shift = lax.rem(columns - lax.axis_index("expert") * held, columns)
    gates = pltpu.roll(gates, shift, 1)
    together = min(4, held)
    for first in range(0, held, together):
        made = []
        for e in range(first, first + together):
            hidden = jnp.maximum(
                jnp.dot(x, win_ref[e], preferred_element_type=jnp.float32), 0.0
            ).astype(jnp.bfloat16)
            made.append(
                lax.dot_general(
                    hidden,
                    wout_ref[e],
                    (((1,), (1,)), ((), ())),
                    preferred_element_type=jnp.float32,
                )
            )
        for t in range(tasks):
            piece = None
            for j, output in enumerate(made):
                lane = t * experts_all + first + j
                term = gates[:, lane : lane + 1] * output
                piece = term if piece is None else piece + term
            span = slice(t * width, (t + 1) * width)
            if first > 0:
                piece = piece + acc_ref[:, span]
            if first + together < held:
                acc_ref[:, span] = piece
            else:
                out_ref[:, span] = piece.astype(out_ref.dtype)


def run_experts(x, gate_weight, expert_in, expert_out, tasks):
    rows, depth = x.shape
    held, _, units = expert_in.shape
    width = expert_out.shape[1]
    block = min(512, rows)
    return pl.pallas_call(
        functools.partial(expert_kernel, tasks),
        grid=(rows // block,),
        in_specs=[
            pl.BlockSpec((block, depth), lambda i: (i, 0)),
            pl.BlockSpec(gate_weight.shape, lambda i: (0, 0)),
            pl.BlockSpec(expert_in.shape, lambda i: (0, 0, 0), pipeline_mode=pl.Buffered(1)),
            pl.BlockSpec(expert_out.shape, lambda i: (0, 0, 0), pipeline_mode=pl.Buffered(1)),
        ],
        out_specs=pl.BlockSpec((block, tasks * width), lambda i: (i, 0)),
        out_shape=jax.ShapeDtypeStruct((rows, tasks * width), jnp.bfloat16),
        scratch_shapes=[pltpu.VMEM((block, tasks * width), jnp.float32)],
        compiler_params=pltpu.CompilerParams(vmem_limit_bytes=VMEM_LIMIT),
    )(x, gate_weight, expert_in, expert_out)


def attention_kernel(q_ref, k_ref, v_ref, own_ref, all_ref, weight_ref, out_ref):
    same = own_ref[...] == all_ref[...]
    factor = 1.0 / math.sqrt(HD)
    result = None
    for first in range(0, q_ref.shape[1], HD):
        span = slice(first, first + HD)
        affinity = (
            lax.dot_general(
                q_ref[:, span],
                k_ref[:, span],
                (((1,), (1,)), ((), ())),
                preferred_element_type=jnp.float32,
            )
            * factor
        )
        affinity = jnp.where(same, affinity, -1e30)
        highest = jnp.max(affinity, axis=1, keepdims=True)
        powers = jnp.exp(affinity - highest)
        total = jnp.sum(powers, axis=1, keepdims=True)
        context = jnp.dot(
            powers.astype(jnp.bfloat16), v_ref[:, span], preferred_element_type=jnp.float32
        )
        context = (context / total).astype(jnp.bfloat16)
        term = jnp.dot(context, weight_ref[span, :], preferred_element_type=jnp.float32)
        result = term if result is None else result + term
    out_ref[...] = result


def run_attention(q, k, v, own, every, weight):
    rows, width = q.shape
    keys = k.shape[0]
    tasks = weight.shape[1]
    block = min(128, rows)
    return pl.pallas_call(
        attention_kernel,
        grid=(rows // block,),
        in_specs=[
            pl.BlockSpec((block, width), lambda i: (i, 0)),
            pl.BlockSpec((keys, width), lambda i: (0, 0)),
            pl.BlockSpec((keys, width), lambda i: (0, 0)),
            pl.BlockSpec((block, 1), lambda i: (i, 0)),
            pl.BlockSpec((1, keys), lambda i: (0, 0)),
            pl.BlockSpec((width, tasks), lambda i: (0, 0)),
        ],
        out_specs=pl.BlockSpec((block, tasks), lambda i: (i, 0)),
        out_shape=jax.ShapeDtypeStruct((rows, tasks), jnp.float32),
        compiler_params=pltpu.CompilerParams(vmem_limit_bytes=VMEM_LIMIT),
    )(q, k, v, own, every, weight)


def flip(position, step):
    low = lax.rem(position, 2)
    high = position // 2
    return (high + (step // 2) * (1 - 2 * high)) * 2 + low + lax.rem(step, 2) * (1 - 2 * low)


def remote(src, dst, send, recv, **where):
    return pltpu.make_async_remote_copy(
        src_ref=src, dst_ref=dst, send_sem=send, recv_sem=recv, device_id=where,
        device_id_type=MESH,
    )


TOGETHER = 4


def mix_kernel(
    tasks, cand_ref, gate_ref, win_hbm, wout_hbm, gain_ref, out_ref,
    xbuf, win, wout, gates_all, gates, hidden, made, acc, part, core_in, x_out, x_in, z_out, z_in,
    load_sem, up_s, down_s, z_r, x_s, x_r, c_s, c_r, core_s, core_r, rx_s, rx_r, rz_s, rz_r,
):
    (z, x, c), (nz, nx, nc) = place()
    f32, bf = jnp.float32, jnp.bfloat16
    other_x, other_c = 1 - x, 1 - c
    held = win.shape[0]
    quarters, share, depth = xbuf.shape[1:]
    rows = quarters * share
    width = wout.shape[1]
    spot = c * nx + x
    loads = [
        pltpu.make_async_copy(cand_ref, xbuf.at[z], load_sem.at[0]),
        pltpu.make_async_copy(win_hbm, win, load_sem.at[1]),
        pltpu.make_async_copy(wout_hbm, wout, load_sem.at[2]),
    ]
    for item in loads:
        item.start()
    greet()

    def upward(src, slab, d):
        return remote(src, xbuf.at[slab, spot], up_s.at[d], z_r.at[slab], wide=z + 1)

    def downward(src, slab, d):
        return remote(src, xbuf.at[slab, spot], down_s.at[d], z_r.at[slab], wide=z - 1)

    def sideways(slab):
        piece = xbuf.at[slab, spot]
        return remote(piece, piece, x_s.at[slab], x_r.at[slab], expert=other_x)

    def corewise(slab, j, q):
        piece = xbuf.at[slab, q]
        return remote(piece, piece, c_s.at[slab, j], c_r.at[slab, j], inner=other_c)

    @pl.when(z < nz - 1)
    def _():
        upward(cand_ref.at[spot], z, 0).start()

    @pl.when(z > 0)
    def _():
        downward(cand_ref.at[spot], z, 0).start()

    for item in loads:
        item.wait()

    def arrive_z(d):
        below, above = z - d, z + d

        @pl.when(below >= 0)
        def _():
            remote(
                xbuf.at[below, spot], xbuf.at[below, spot], up_s.at[0], z_r.at[below], wide=z - 1
            ).wait_recv()

            @pl.when(z < nz - 1)
            def _():
                upward(xbuf.at[below, spot], below, d).start()

            sideways(below).start()
            corewise(below, 0, spot).start()

        @pl.when(above < nz)
        def _():
            remote(
                xbuf.at[above, spot], xbuf.at[above, spot], down_s.at[0], z_r.at[above], wide=z + 1
            ).wait_recv()

            @pl.when(z > 0)
            def _():
                downward(xbuf.at[above, spot], above, d).start()

            sideways(above).start()
            corewise(above, 0, spot).start()

    def arrive_x(d):
        for slab, here in ((z - d, z - d >= 0), (z + d, z + d < nz)):

            @pl.when(here)
            def _():
                piece = xbuf.at[slab, c * nx + other_x]
                remote(piece, piece, x_s.at[slab], x_r.at[slab], expert=other_x).wait_recv()
                corewise(slab, 1, c * nx + other_x).start()

    def arrive_c(slab):
        for j, q in ((0, other_c * nx + x), (1, other_c * nx + other_x)):
            piece = xbuf.at[slab, q]
            remote(piece, piece, c_s.at[slab, j], c_r.at[slab, j], inner=other_c).wait_recv()

    def to_core(k):
        return remote(
            part.at[k, pl.ds(other_c * nx, nx)], core_in.at[k], core_s.at[k], core_r.at[k],
            inner=other_c,
        )

    def to_x(k):
        return remote(x_out.at[k], x_in.at[k], rx_s.at[k], rx_r.at[k], expert=other_x)

    def to_z(k):
        return remote(z_out.at[k], z_in.at[k], rz_s.at[k], rz_r.at[k], wide=flip(z, k))

    def reduce_core(k):
        to_core(k).wait_recv()
        x_out[k] = (
            part[k, c * nx + other_x].astype(f32) + core_in[k, other_x].astype(f32)
        ).astype(bf)
        to_x(k).start()

    def total_of(k):
        return (
            part[k, c * nx + x].astype(f32)
            + core_in[k, x].astype(f32)
            + x_in[k].astype(f32)
        )

    def reduce_x(k):
        to_x(k).wait_recv()

        @pl.when(k > 0)
        def _():
            z_out[k] = total_of(k).astype(bf)
            to_z(k).start()

    groups = held // TOGETHER

    def gating(i, k):
        side = (i % 2) * TOGETHER
        for q in range(quarters):
            lanes = slice(q * share, (q + 1) * share)
            weights = [
                [
                    gates[t * held + i * TOGETHER + j : t * held + i * TOGETHER + j + 1, lanes]
                    for j in range(TOGETHER)
                ]
                for t in range(tasks)
            ]
            for f in range(0, width, 16):
                outs = [made[side + j, f : f + 16, lanes] for j in range(TOGETHER)]
                for t in range(tasks):
                    span = slice(t * width + f, t * width + f + 16)
                    piece = weights[t][0] * outs[0]
                    for j in range(1, TOGETHER):
                        piece = piece + weights[t][j] * outs[j]
                    if i > 0:
                        piece = piece + acc[q, span, :]
                    if i < groups - 1:
                        acc[q, span, :] = piece
                    else:
                        part[k, q, span, :] = piece.astype(bf)

    def stage(i, data, k):
        if i < groups:
            for j in range(TOGETHER):
                e = i * TOGETHER + j
                hidden[(i % 2) * TOGETHER + j] = jnp.maximum(
                    jnp.dot(data, win[e], preferred_element_type=f32), 0.0
                ).astype(bf)
        if 0 < i <= groups:
            side = ((i - 1) % 2) * TOGETHER
            for j in range(TOGETHER):
                e = (i - 1) * TOGETHER + j
                made[side + j] = lax.dot_general(
                    wout[e], hidden[side + j], (((1,), (1,)), ((), ())),
                    preferred_element_type=f32,
                )
        if i > 1:
            gating(i - 2, k)

    def step(k, carry):
        slab = flip(z, k)
        data = xbuf[slab].reshape(rows, depth)
        logits = lax.dot_general(
            gate_ref[...], data, (((0,), (1,)), ((), ())), preferred_element_type=f32
        )
        logits = logits.reshape(tasks, logits.shape[0] // tasks, rows)
        powers = jnp.exp(logits - jnp.max(logits, axis=1, keepdims=True))
        gates_all[...] = powers / jnp.sum(powers, axis=1, keepdims=True)
        for t in range(tasks):
            gates[t * held : (t + 1) * held, :] = gates_all[
                t, pl.ds(pl.multiple_of(x * held, held), held), :
            ]
        half = (groups + 2) // 2
        for i in range(half):
            stage(i, data, k)

        @pl.when(k < nz - 1)
        def _():
            arrive_z(k + 1)

        @pl.when(k > 0)
        def _():
            reduce_core(k - 1)

        data = xbuf[slab].reshape(rows, depth)
        for i in range(half, groups + 2):
            stage(i, data, k)
        to_core(k).start()

        @pl.when(k < nz - 1)
        def _():
            arrive_x(k + 1)

        @pl.when(k > 0)
        def _():
            reduce_x(k - 1)

        @pl.when(k < nz - 1)
        def _():
            arrive_c(flip(z, k + 1))

        return carry

    lax.fori_loop(0, nz, step, 0)
    reduce_core(nz - 1)
    reduce_x(nz - 1)
    total = total_of(0)
    for k in range(1, nz):
        to_z(k).wait_recv()
        total = total + z_in[k].astype(f32)
    total = total.T
    center = jnp.mean(total, axis=1, keepdims=True)
    spread = jnp.mean(jnp.square(total - center), axis=1, keepdims=True)
    normed = (total - center) * lax.rsqrt(spread + 1e-05) * gain_ref[...].astype(f32)
    out_ref[...] = normed.astype(bf)

    for d in range(nz - 1):

        @pl.when((z < nz - 1) & (z - d >= 0))
        def _():
            upward(xbuf.at[z, spot], z, d).wait_send()

        @pl.when((z > 0) & (z + d < nz))
        def _():
            downward(xbuf.at[z, spot], z, d).wait_send()

    for k in range(1, nz):
        slab = flip(z, k)
        sideways(slab).wait_send()
        corewise(slab, 0, spot).wait_send()
        corewise(slab, 1, spot).wait_send()
        to_z(k).wait_send()
    for k in range(nz):
        to_core(k).wait_send()
        to_x(k).wait_send()


def run_mix(cand, gate_weight, expert_in, expert_out, gain, tasks, collective):
    nz, nx, nc = (lax.axis_size(a) for a in ALL)
    rows, depth = cand.shape
    quarters = nx * nc
    share = rows // quarters
    held, _, units = expert_in.shape
    width = expert_out.shape[1]
    dma = pltpu.SemaphoreType.DMA
    f32, bf = jnp.float32, jnp.bfloat16
    vmem = pl.BlockSpec(memory_space=pltpu.VMEM)
    anywhere = pl.BlockSpec(memory_space=pl.ANY)
    model = tasks * width
    experts_all = gate_weight.shape[1] // tasks
    return pl.pallas_call(
        functools.partial(mix_kernel, tasks),
        in_specs=[anywhere, vmem, anywhere, anywhere, vmem],
        out_specs=vmem,
        out_shape=jax.ShapeDtypeStruct((share, model), bf),
        scratch_shapes=[
            pltpu.VMEM((nz, quarters, share, depth), bf),
            pltpu.VMEM(expert_in.shape, bf),
            pltpu.VMEM(expert_out.shape, bf),
            pltpu.VMEM((tasks, experts_all, rows), f32),
            pltpu.VMEM((tasks * held, rows), f32),
            pltpu.VMEM((2 * TOGETHER, rows, units), bf),
            pltpu.VMEM((2 * TOGETHER, width, rows), f32),
            pltpu.VMEM((quarters, model, share), f32),
            pltpu.VMEM((nz, quarters, model, share), bf),
            pltpu.VMEM((nz, nx, model, share), bf),
            pltpu.VMEM((nz, model, share), bf),
            pltpu.VMEM((nz, model, share), bf),
            pltpu.VMEM((nz, model, share), bf),
            pltpu.VMEM((nz, model, share), bf),
            dma((3,)),
            dma((nz,)),
            dma((nz,)),
            dma((nz,)),
            dma((nz,)),
            dma((nz,)),
            dma((nz, 2)),
            dma((nz, 2)),
            dma((nz,)),
            dma((nz,)),
            dma((nz,)),
            dma((nz,)),
            dma((nz,)),
            dma((nz,)),
        ],
        compiler_params=pltpu.CompilerParams(
            collective_id=collective, has_side_effects=True, vmem_limit_bytes=VMEM_LIMIT
        ),
    )(cand.reshape(quarters, share, depth), gate_weight, expert_in, expert_out, gain)


def score_kernel(
    norm_ref, q_ref, k_ref, v_ref, task_ref, attn_ref, own_ref, id_ref, out_ref,
    nb, keys, extra, ids, queries, powers, high, sums, partial,
    n_s, n_r, id_s, id_r, up_s, down_s, key_r, p_s, p_r,
):
    (z, x, c), (nz, nx, nc) = place()
    f32, bf = jnp.float32, jnp.bfloat16
    other_x, other_c = 1 - x, 1 - c
    spot = c * nx + x
    quarters, share, depth = nb.shape
    rows = quarters * share
    heads = queries.shape[1] // HD
    tasks = task_ref.shape[1]
    barrier = pltpu.get_barrier_semaphore()
    pl.semaphore_signal(
        barrier, inc=1, device_id={"expert": other_x, "inner": other_c}, device_id_type=MESH
    )
    for axis, here, size in zip(ALL, (z, x, c), (nz, nx, nc)):
        for turned in range(1, size):
            pl.semaphore_signal(
                barrier, inc=1, device_id={axis: turn(here, turned, size)}, device_id_type=MESH
            )
    pl.semaphore_wait(barrier, nz + nx + nc - 2)

    def give(q, j, **where):
        return remote(nb.at[q], nb.at[q], n_s.at[j], n_r.at[j], **where)

    first = remote(norm_ref, nb.at[spot], n_s.at[0], n_r.at[0], expert=other_x)
    second = remote(norm_ref, nb.at[spot], n_s.at[1], n_r.at[1], inner=other_c)
    first.start()
    second.start()
    id_copies = []
    for turned in range(1, nz):
        target = turn(z, turned, nz)
        item = remote(id_ref, ids.at[z], id_s.at[turned], id_r.at[z], wide=target)
        item.start()
        id_copies.append(item)
    ids[z] = id_ref[...]
    nb[spot] = norm_ref[...]
    across = c * nx + other_x
    give(across, 0, expert=other_x).wait_recv()
    third = give(across, 2, inner=other_c)
    third.start()
    give(other_c * nx + x, 1, inner=other_c).wait_recv()
    give(other_c * nx + other_x, 2, inner=other_c).wait_recv()
    data = nb[...].reshape(rows, depth)
    half = heads // 2 * HD
    keys_own = jnp.dot(data, k_ref[...], preferred_element_type=f32).astype(bf)
    values = jnp.dot(data, v_ref[...], preferred_element_type=f32).astype(bf)
    for j in range(2):
        keys[z, j] = keys_own[:, j * half : (j + 1) * half]
    lift = lax.dot_general(
        attn_ref[...], values, (((0,), (1,)), ((), ())), preferred_element_type=f32
    )
    coarse = lift.astype(bf)
    fine = (lift - coarse.astype(f32)).astype(bf).astype(f32)
    coarse = coarse.astype(f32)
    ones = jnp.ones((1, rows), f32)
    blank = jnp.zeros((16 - 2 * tasks - 1, rows), f32)
    for h in range(heads):
        piece = slice(h * tasks, (h + 1) * tasks)
        extra[z, h * 16 : (h + 1) * 16, :] = jnp.concatenate(
            [coarse[piece], fine[piece], ones, blank], axis=0
        ).astype(bf)

    def parts(slab):
        return [keys.at[slab, 0], keys.at[slab, 1], extra.at[slab]]

    def upward(slab, d, j):
        piece = parts(slab)[j]
        return remote(piece, piece, up_s.at[d, j], key_r.at[slab, j], wide=z + 1)

    def downward(slab, d, j):
        piece = parts(slab)[j]
        return remote(piece, piece, down_s.at[d, j], key_r.at[slab, j], wide=z - 1)

    order = (2, 0, 1)

    @pl.when(z < nz - 1)
    def _():
        for j in order:
            upward(z, 0, j).start()

    @pl.when(z > 0)
    def _():
        for j in order:
            downward(z, 0, j).start()

    queries[...] = (
        jnp.dot(data, q_ref[...], preferred_element_type=f32) * (1.0 / math.sqrt(HD))
    ).astype(bf)
    for item in id_copies:
        item.wait_send()
    for turned in range(1, nz):
        source = turn(z, turned, nz)
        remote(id_ref, ids.at[source], id_s.at[turned], id_r.at[source], wide=source).wait_recv()

    def attend(slab, fresh):
        same = own_ref[...] == ids[slab]
        tops = []
        for h in range(heads):
            span = slice(h * HD, (h + 1) * HD)
            inside = (h * HD) % half
            affinity = lax.dot_general(
                queries[:, span],
                keys[slab, h * HD // half][:, inside : inside + HD],
                (((1,), (1,)), ((), ())),
                preferred_element_type=f32,
            )
            affinity = jnp.where(same, affinity, -1e30)
            top = jnp.max(affinity, axis=1, keepdims=True)
            powers[h] = jnp.exp(affinity - top).astype(bf)
            tops.append(top)
        for h in range(heads):
            got = lax.dot_general(
                powers[h], extra[slab, h * 16 : (h + 1) * 16, :], (((1,), (1,)), ((), ())),
                preferred_element_type=f32,
            )
            if fresh:
                high[h] = tops[h]
                sums[h] = got
            else:
                peak = jnp.maximum(high[h], tops[h])
                sums[h] = sums[h] * jnp.exp(high[h] - peak) + got * jnp.exp(tops[h] - peak)
                high[h] = peak

    attend(z, True)

    def step(d, carry):
        below, above = z - d, z + d

        @pl.when(below >= 0)
        def _():
            for j in order:
                piece = parts(below)[j]
                remote(piece, piece, up_s.at[0, j], key_r.at[below, j], wide=z - 1).wait_recv()

                @pl.when(z < nz - 1)
                def _():
                    upward(below, d, j).start()

        @pl.when(above < nz)
        def _():
            for j in order:
                piece = parts(above)[j]
                remote(piece, piece, down_s.at[0, j], key_r.at[above, j], wide=z + 1).wait_recv()

                @pl.when(z > 0)
                def _():
                    downward(above, d, j).start()

        @pl.when(below >= 0)
        def _():
            attend(below, False)

        @pl.when(above < nz)
        def _():
            attend(above, False)

        return carry

    lax.fori_loop(1, nz, step, 0)
    result = None
    for h in range(heads):
        got = sums[h]
        term = (got[:, :tasks] + got[:, tasks : 2 * tasks]) / got[:, 2 * tasks : 2 * tasks + 1]
        result = term if result is None else result + term
    lanes = partial.shape[2]
    result = jnp.concatenate([result, jnp.zeros((rows, 128 - tasks), f32)], axis=1)
    partial[0] = result.T[:8, :]
    sends = []
    for j, where in enumerate(
        ({"inner": other_c}, {"expert": other_x}, {"expert": other_x, "inner": other_c})
    ):
        item = remote(partial.at[0], partial.at[j + 1], p_s.at[j], p_r.at[j], **where)
        item.start()
        sends.append(item)
    base = lax.dot_general(
        task_ref[...], data, (((0,), (1,)), ((), ())), preferred_element_type=f32
    )
    for item in sends:
        item.wait()
    everything = (partial[0] + partial[1]) + (partial[2] + partial[3])
    everything = everything[:tasks, :] + base
    padded = jnp.concatenate([everything, jnp.zeros((8 - tasks, rows), f32)], axis=0)
    out_ref[...] = padded.T[:, :tasks]
    first.wait_send()
    second.wait_send()
    third.wait_send()
    for d in range(nz - 1):
        for j in order:

            @pl.when((z < nz - 1) & (z - d >= 0))
            def _():
                upward(z, d, j).wait_send()

            @pl.when((z > 0) & (z + d < nz))
            def _():
                downward(z, d, j).wait_send()


def run_scores(normed, query, key, value, task, attn, request_of, collective):
    nz, nx, nc = (lax.axis_size(a) for a in ALL)
    share, depth = normed.shape
    quarters = nx * nc
    rows = share * quarters
    width = query.shape[1]
    heads = width // HD
    tasks = task.shape[1]
    dma = pltpu.SemaphoreType.DMA
    f32, bf = jnp.float32, jnp.bfloat16
    vmem = pl.BlockSpec(memory_space=pltpu.VMEM)
    lane = jnp.arange(heads * tasks)[None, :]
    row = jnp.arange(width)[:, None]
    spread = jnp.where(row // HD == lane // tasks, jnp.tile(attn, (1, heads)), 0).astype(bf)
    return pl.pallas_call(
        score_kernel,
        in_specs=[vmem] * 8,
        out_specs=vmem,
        out_shape=jax.ShapeDtypeStruct((rows, tasks), f32),
        scratch_shapes=[
            pltpu.VMEM((quarters, share, depth), bf),
            pltpu.VMEM((nz, 2, rows, width // 2), bf),
            pltpu.VMEM((nz, heads * 16, rows), bf),
            pltpu.VMEM((nz, 1, rows), jnp.int32),
            pltpu.VMEM((rows, width), bf),
            pltpu.VMEM((heads, rows, rows), bf),
            pltpu.VMEM((heads, rows, 1), f32),
            pltpu.VMEM((heads, rows, 16), f32),
            pltpu.VMEM((nx * nc, 8, rows), f32),
            dma((3,)),
            dma((3,)),
            dma((nz,)),
            dma((nz,)),
            dma((nz, 3)),
            dma((nz, 3)),
            dma((nz, 3)),
            dma((3,)),
            dma((3,)),
        ],
        compiler_params=pltpu.CompilerParams(
            collective_id=collective, has_side_effects=True, vmem_limit_bytes=VMEM_LIMIT
        ),
    )(normed, query, key, value, task, spread, request_of[:, None], request_of[None, :])


def fused(sizes, rows, heads, held):
    return sizes == (4, 2, 2) and rows % 512 == 0 and heads == 4 and held % (2 * TOGETHER) == 0


def local(
    candidates,
    gate_weight,
    expert_in,
    expert_out,
    norm_gain,
    query_weight,
    key_weight,
    value_weight,
    task_weight,
    attn_weight,
    request_of,
):
    rows = candidates.shape[0]
    tasks = task_weight.shape[1]
    nz, nx, nc = (lax.axis_size(a) for a in ALL)
    if fused((nz, nx, nc), rows, query_weight.shape[1] // HD, expert_in.shape[0]):
        normed = run_mix(
            candidates, gate_weight, expert_in, expert_out, norm_gain[None, :], tasks, 3
        )
        return run_scores(
            normed, query_weight, key_weight, value_weight, task_weight, attn_weight, request_of, 4
        )
    share = rows // (nx * nc)
    spot = lax.axis_index("inner") * nx + lax.axis_index("expert")
    wide = lax.axis_index("wide")
    quarter = lax.dynamic_slice_in_dim(candidates, spot * share, share, 0)
    everyone, requests = run_gather(quarter, request_of[None, :], 0)
    partial_mix = run_experts(everyone, gate_weight, expert_in, expert_out, tasks)
    normed = run_reduce(partial_mix, norm_gain[None, :], share, 1)
    normed_all = run_gather(normed, None, 2)
    own = lax.dynamic_slice_in_dim(normed_all, wide * rows, rows, 0)
    queries = jnp.dot(own, query_weight, preferred_element_type=jnp.float32).astype(jnp.bfloat16)
    keys = jnp.dot(normed_all, key_weight, preferred_element_type=jnp.float32).astype(jnp.bfloat16)
    values = jnp.dot(normed_all, value_weight, preferred_element_type=jnp.float32).astype(
        jnp.bfloat16
    )
    term = run_attention(
        queries, keys, values, request_of[:, None], requests, attn_weight
    )
    attention = lax.psum(term.T, ("expert", "inner")).T
    return jnp.dot(own, task_weight, preferred_element_type=jnp.float32) + attention


def solution(mesh):
    return jax.shard_map(
        local,
        mesh=mesh,
        in_specs=(
            P(("groups", "wide"), None),
            P(),
            P("expert", None, ("wide", "inner")),
            P("expert", None, ("wide", "inner")),
            P(),
            P(None, ("expert", "inner")),
            P(None, ("expert", "inner")),
            P(None, ("expert", "inner")),
            P(),
            P(("expert", "inner"), None),
            P(("groups", "wide")),
        ),
        out_specs=P(("groups", "wide"), None),
        check_vma=False,
    )
```

```python
import functools
import math

import jax
import jax.numpy as jnp
from jax import lax
from jax.experimental import pallas as pl
from jax.experimental.pallas import tpu as pltpu
from jax.sharding import PartitionSpec as P

HD = 64
ALL = ("wide", "expert", "inner")
VMEM_LIMIT = 60 * 1024 * 1024


MESH = pl.DeviceIdType.MESH


def place():
    return tuple(lax.axis_index(a) for a in ALL), tuple(lax.axis_size(a) for a in ALL)


def turn(start, step, size):
    return lax.rem(start + step, size)


def greet():
    mine, sizes = place()
    barrier = pltpu.get_barrier_semaphore()
    for axis, here, size in zip(ALL, mine, sizes):
        for step in range(1, size):
            pl.semaphore_signal(
                barrier, inc=1, device_id={axis: turn(here, step, size)}, device_id_type=MESH
            )
    pl.semaphore_wait(barrier, sum(sizes) - len(sizes))


def gather_kernel(with_ids, *refs):
    if with_ids:
        own_ref, id_ref, out_ref, ids_ref, recv, send_z, send_x, send_c, local_sem, id_r, id_s = refs
    else:
        own_ref, out_ref, recv, send_z, send_x, send_c, local_sem = refs
    (z, x, c), (nz, nx, nc) = place()
    greet()

    def copy(src, zs, xs, cs, sem, axis, target):
        return pltpu.make_async_remote_copy(
            src_ref=src,
            dst_ref=out_ref.at[zs, cs, xs],
            send_sem=sem,
            recv_sem=recv.at[zs, cs, xs],
            device_id={axis: target},
            device_id_type=MESH,
        )

    def arrived(zs, xs, cs):
        copy(out_ref.at[zs, cs, xs], zs, xs, cs, send_z.at[0], "inner", turn(c, 1, nc)).wait_recv()

    sent = []

    def push(*what):
        item = copy(*what)
        item.start()
        sent.append(item)

    def spread_x(src, k, zs):
        for step in range(1, nx):
            push(src, zs, x, c, send_x.at[k, step - 1], "expert", turn(x, step, nx))

    def spread_c(src, k, j, zs, xs):
        for step in range(1, nc):
            push(src, zs, xs, c, send_c.at[k, j, step - 1], "inner", turn(c, step, nc))

    for step in range(1, nz):
        push(own_ref, z, x, c, send_z.at[step - 1], "wide", turn(z, step, nz))
    spread_x(own_ref, 0, z)
    spread_c(own_ref, 0, 0, z, x)
    keep = pltpu.make_async_copy(own_ref, out_ref.at[z, c, x], local_sem.at[0])
    keep.start()
    if with_ids:
        id_copies = []
        for step in range(1, nz):
            item = pltpu.make_async_remote_copy(
                src_ref=id_ref,
                dst_ref=ids_ref.at[z],
                send_sem=id_s.at[step - 1],
                recv_sem=id_r.at[z],
                device_id={"wide": turn(z, step, nz)},
                device_id_type=MESH,
            )
            item.start()
            id_copies.append(item)
        ids_ref[z] = id_ref[...]

    def pass_x(k):
        zs = turn(z, k, nz)
        for step in range(1, nx):
            xs = turn(x, step, nx)
            arrived(zs, xs, c)
            spread_c(out_ref.at[zs, c, xs], k, step, zs, xs)

    for k in range(1, nz):
        zs = turn(z, k, nz)
        arrived(zs, x, c)
        spread_x(out_ref.at[zs, c, x], k, zs)
        spread_c(out_ref.at[zs, c, x], k, 0, zs, x)
        pass_x(k - 1)
    pass_x(nz - 1)
    for k in range(nz):
        for j in range(nx):
            for step in range(1, nc):
                arrived(turn(z, k, nz), turn(x, j, nx), turn(c, step, nc))
    for item in sent:
        item.wait_send()
    keep.wait()
    if with_ids:
        for step in range(1, nz):
            zs = turn(z, step, nz)
            pltpu.make_async_remote_copy(
                src_ref=id_ref,
                dst_ref=ids_ref.at[zs],
                send_sem=id_s.at[step - 1],
                recv_sem=id_r.at[zs],
                device_id={"wide": zs},
                device_id_type=MESH,
            ).wait_recv()
        for item in id_copies:
            item.wait_send()


def run_gather(own, ids, collective):
    nz, nx, nc = (lax.axis_size(a) for a in ALL)
    dma = pltpu.SemaphoreType.DMA
    with_ids = ids is not None
    shape = jax.ShapeDtypeStruct((nz, nc, nx) + own.shape, own.dtype)
    vmem = pl.BlockSpec(memory_space=pltpu.VMEM)
    anywhere = pl.BlockSpec(memory_space=pl.ANY)
    scratch = [
        dma((nz, nc, nx)),
        dma((max(nz - 1, 1),)),
        dma((nz, max(nx - 1, 1))),
        dma((nz, nx, max(nc - 1, 1))),
        dma((1,)),
    ]
    if with_ids:
        scratch += [dma((nz,)), dma((max(nz - 1, 1),))]
    out = pl.pallas_call(
        functools.partial(gather_kernel, with_ids),
        in_specs=[vmem, vmem] if with_ids else [vmem],
        out_specs=[anywhere, vmem] if with_ids else anywhere,
        out_shape=[shape, jax.ShapeDtypeStruct((nz,) + ids.shape, ids.dtype)] if with_ids else shape,
        scratch_shapes=scratch,
        compiler_params=pltpu.CompilerParams(collective_id=collective, has_side_effects=True),
    )(*([own, ids] if with_ids else [own]))
    depth = own.shape[1]
    if with_ids:
        return out[0].reshape(-1, depth), out[1].reshape(1, -1)
    return out.reshape(-1, depth)


def reduce_kernel(
    part_ref, gain_ref, out_ref, mine, core_in, x_out, x_in, z_out, z_in,
    local_sem, core_s, core_r, x_s, x_r, z_s, z_r,
):
    (z, x, c), (nz, nx, nc) = place()
    f32 = jnp.float32
    greet()
    other = turn(c, 1, nc)
    core, kept = [], []
    for k in range(nz):
        s = turn(z, k + 1, nz)
        item = pltpu.make_async_remote_copy(
            src_ref=part_ref.at[s, other],
            dst_ref=core_in.at[k],
            send_sem=core_s.at[k],
            recv_sem=core_r.at[k],
            device_id={"inner": other},
            device_id_type=MESH,
        )
        item.start()
        core.append(item)
        stay = pltpu.make_async_copy(part_ref.at[s, c], mine.at[k], local_sem.at[k])
        stay.start()
        kept.append(stay)

    def pair(k, xs):
        return mine[k, xs].astype(f32) + core_in[k, xs].astype(f32)

    across, along = [], []

    def finish(k):
        total = pair(k, x)
        for step in range(1, nx):
            across[k][step - 1].wait_recv()
            total = total + x_in[k, step - 1].astype(f32)
        if k == nz - 1:
            return total
        z_out[k] = total.astype(z_out.dtype)
        item = pltpu.make_async_remote_copy(
            src_ref=z_out.at[k],
            dst_ref=z_in.at[k],
            send_sem=z_s.at[k],
            recv_sem=z_r.at[k],
            device_id={"wide": turn(z, k + 1, nz)},
            device_id_type=MESH,
        )
        item.start()
        along.append(item)

    for k in range(nz):
        kept[k].wait()
        core[k].wait_recv()
        items = []
        for step in range(1, nx):
            xs = turn(x, step, nx)
            x_out[k, step - 1] = pair(k, xs).astype(x_out.dtype)
            item = pltpu.make_async_remote_copy(
                src_ref=x_out.at[k, step - 1],
                dst_ref=x_in.at[k, step - 1],
                send_sem=x_s.at[k, step - 1],
                recv_sem=x_r.at[k, step - 1],
                device_id={"expert": xs},
                device_id_type=MESH,
            )
            item.start()
            items.append(item)
        across.append(items)
        if k > 0:
            finish(k - 1)
    total = finish(nz - 1)
    for k in range(nz - 1):
        along[k].wait_recv()
        total = total + z_in[k].astype(f32)
    center = jnp.mean(total, axis=1, keepdims=True)
    spread = jnp.mean(jnp.square(total - center), axis=1, keepdims=True)
    normed = (total - center) * lax.rsqrt(spread + 1e-05) * gain_ref[...].astype(f32)
    out_ref[...] = normed.astype(out_ref.dtype)
    for item in core + along + [i for items in across for i in items]:
        item.wait_send()


def run_reduce(part, gain, share, collective):
    nz, nx, nc = (lax.axis_size(a) for a in ALL)
    width = part.shape[1]
    dma = pltpu.SemaphoreType.DMA
    kind = part.dtype
    part = part.reshape(nz, nc, nx, share, width)
    few = max(nx - 1, 1)
    vmem = pl.BlockSpec(memory_space=pltpu.VMEM)
    return pl.pallas_call(
        reduce_kernel,
        in_specs=[pl.BlockSpec(memory_space=pl.ANY), vmem],
        out_specs=vmem,
        out_shape=jax.ShapeDtypeStruct((share, width), kind),
        scratch_shapes=[
            pltpu.VMEM((nz, nx, share, width), kind),
            pltpu.VMEM((nz, nx, share, width), kind),
            pltpu.VMEM((nz, few, share, width), kind),
            pltpu.VMEM((nz, few, share, width), kind),
            pltpu.VMEM((nz, share, width), kind),
            pltpu.VMEM((nz, share, width), kind),
            dma((nz,)),
            dma((nz,)),
            dma((nz,)),
            dma((nz, few)),
            dma((nz, few)),
            dma((nz,)),
            dma((nz,)),
        ],
        compiler_params=pltpu.CompilerParams(
            collective_id=collective, has_side_effects=True, vmem_limit_bytes=VMEM_LIMIT
        ),
    )(part, gain)


def expert_kernel(tasks, x_ref, gate_ref, win_ref, wout_ref, out_ref, acc_ref):
    rows = x_ref.shape[0]
    columns = gate_ref.shape[1]
    experts_all = columns // tasks
    held, _, _ = win_ref.shape
    width = wout_ref.shape[1]
    x = x_ref[...]
    logits = jnp.dot(x, gate_ref[...], preferred_element_type=jnp.float32)
    task = lax.broadcasted_iota(jnp.int32, (rows, columns), 1) // experts_all
    top = jnp.zeros_like(logits)
    for t in range(tasks):
        high = jnp.max(jnp.where(task == t, logits, -jnp.inf), axis=1, keepdims=True)
        top = jnp.where(task == t, high, top)
    powers = jnp.exp(logits - top)
    total = jnp.ones_like(logits)
    for t in range(tasks):
        part = jnp.sum(jnp.where(task == t, powers, 0.0), axis=1, keepdims=True)
        total = jnp.where(task == t, part, total)
    gates = powers / total
    shift = lax.rem(columns - lax.axis_index("expert") * held, columns)
    gates = pltpu.roll(gates, shift, 1)
    together = min(4, held)
    for first in range(0, held, together):
        made = []
        for e in range(first, first + together):
            hidden = jnp.maximum(
                jnp.dot(x, win_ref[e], preferred_element_type=jnp.float32), 0.0
            ).astype(jnp.bfloat16)
            made.append(
                lax.dot_general(
                    hidden,
                    wout_ref[e],
                    (((1,), (1,)), ((), ())),
                    preferred_element_type=jnp.float32,
                )
            )
        for t in range(tasks):
            piece = None
            for j, output in enumerate(made):
                lane = t * experts_all + first + j
                term = gates[:, lane : lane + 1] * output
                piece = term if piece is None else piece + term
            span = slice(t * width, (t + 1) * width)
            if first > 0:
                piece = piece + acc_ref[:, span]
            if first + together < held:
                acc_ref[:, span] = piece
            else:
                out_ref[:, span] = piece.astype(out_ref.dtype)


def run_experts(x, gate_weight, expert_in, expert_out, tasks):
    rows, depth = x.shape
    held, _, units = expert_in.shape
    width = expert_out.shape[1]
    block = min(512, rows)
    return pl.pallas_call(
        functools.partial(expert_kernel, tasks),
        grid=(rows // block,),
        in_specs=[
            pl.BlockSpec((block, depth), lambda i: (i, 0)),
            pl.BlockSpec(gate_weight.shape, lambda i: (0, 0)),
            pl.BlockSpec(expert_in.shape, lambda i: (0, 0, 0), pipeline_mode=pl.Buffered(1)),
            pl.BlockSpec(expert_out.shape, lambda i: (0, 0, 0), pipeline_mode=pl.Buffered(1)),
        ],
        out_specs=pl.BlockSpec((block, tasks * width), lambda i: (i, 0)),
        out_shape=jax.ShapeDtypeStruct((rows, tasks * width), jnp.bfloat16),
        scratch_shapes=[pltpu.VMEM((block, tasks * width), jnp.float32)],
        compiler_params=pltpu.CompilerParams(vmem_limit_bytes=VMEM_LIMIT),
    )(x, gate_weight, expert_in, expert_out)


def attention_kernel(q_ref, k_ref, v_ref, own_ref, all_ref, weight_ref, out_ref):
    same = own_ref[...] == all_ref[...]
    factor = 1.0 / math.sqrt(HD)
    result = None
    for first in range(0, q_ref.shape[1], HD):
        span = slice(first, first + HD)
        affinity = (
            lax.dot_general(
                q_ref[:, span],
                k_ref[:, span],
                (((1,), (1,)), ((), ())),
                preferred_element_type=jnp.float32,
            )
            * factor
        )
        affinity = jnp.where(same, affinity, -1e30)
        highest = jnp.max(affinity, axis=1, keepdims=True)
        powers = jnp.exp(affinity - highest)
        total = jnp.sum(powers, axis=1, keepdims=True)
        context = jnp.dot(
            powers.astype(jnp.bfloat16), v_ref[:, span], preferred_element_type=jnp.float32
        )
        context = (context / total).astype(jnp.bfloat16)
        term = jnp.dot(context, weight_ref[span, :], preferred_element_type=jnp.float32)
        result = term if result is None else result + term
    out_ref[...] = result


def run_attention(q, k, v, own, every, weight):
    rows, width = q.shape
    keys = k.shape[0]
    tasks = weight.shape[1]
    block = min(128, rows)
    return pl.pallas_call(
        attention_kernel,
        grid=(rows // block,),
        in_specs=[
            pl.BlockSpec((block, width), lambda i: (i, 0)),
            pl.BlockSpec((keys, width), lambda i: (0, 0)),
            pl.BlockSpec((keys, width), lambda i: (0, 0)),
            pl.BlockSpec((block, 1), lambda i: (i, 0)),
            pl.BlockSpec((1, keys), lambda i: (0, 0)),
            pl.BlockSpec((width, tasks), lambda i: (0, 0)),
        ],
        out_specs=pl.BlockSpec((block, tasks), lambda i: (i, 0)),
        out_shape=jax.ShapeDtypeStruct((rows, tasks), jnp.float32),
        compiler_params=pltpu.CompilerParams(vmem_limit_bytes=VMEM_LIMIT),
    )(q, k, v, own, every, weight)


def flip(position, step):
    low = lax.rem(position, 2)
    high = position // 2
    return (high + (step // 2) * (1 - 2 * high)) * 2 + low + lax.rem(step, 2) * (1 - 2 * low)


def remote(src, dst, send, recv, **where):
    return pltpu.make_async_remote_copy(
        src_ref=src, dst_ref=dst, send_sem=send, recv_sem=recv, device_id=where,
        device_id_type=MESH,
    )


TOGETHER = 4


def mix_kernel(
    tasks, cand_ref, gate_ref, win_hbm, wout_hbm, gain_ref, out_ref,
    xbuf, win, wout, gates_all, gates, hidden, made, acc, part, core_in, x_out, x_in, z_out, z_in,
    load_sem, up_s, down_s, z_r, x_s, x_r, c_s, c_r, core_s, core_r, rx_s, rx_r, rz_s, rz_r,
):
    (z, x, c), (nz, nx, nc) = place()
    f32, bf = jnp.float32, jnp.bfloat16
    other_x, other_c = 1 - x, 1 - c
    held = win.shape[0]
    quarters, share, depth = xbuf.shape[1:]
    rows = quarters * share
    width = wout.shape[1]
    spot = c * nx + x
    loads = [
        pltpu.make_async_copy(cand_ref, xbuf.at[z], load_sem.at[0]),
        pltpu.make_async_copy(win_hbm, win, load_sem.at[1]),
        pltpu.make_async_copy(wout_hbm, wout, load_sem.at[2]),
    ]
    for item in loads:
        item.start()
    greet()

    def upward(src, slab, d):
        return remote(src, xbuf.at[slab, spot], up_s.at[d], z_r.at[slab], wide=z + 1)

    def downward(src, slab, d):
        return remote(src, xbuf.at[slab, spot], down_s.at[d], z_r.at[slab], wide=z - 1)

    def sideways(slab):
        piece = xbuf.at[slab, spot]
        return remote(piece, piece, x_s.at[slab], x_r.at[slab], expert=other_x)

    def corewise(slab, j, q):
        piece = xbuf.at[slab, q]
        return remote(piece, piece, c_s.at[slab, j], c_r.at[slab, j], inner=other_c)

    @pl.when(z < nz - 1)
    def _():
        upward(cand_ref.at[spot], z, 0).start()

    @pl.when(z > 0)
    def _():
        downward(cand_ref.at[spot], z, 0).start()

    for item in loads:
        item.wait()

    def arrive_z(d):
        below, above = z - d, z + d

        @pl.when(below >= 0)
        def _():
            remote(
                xbuf.at[below, spot], xbuf.at[below, spot], up_s.at[0], z_r.at[below], wide=z - 1
            ).wait_recv()

            @pl.when(z < nz - 1)
            def _():
                upward(xbuf.at[below, spot], below, d).start()

        @pl.when(above < nz)
        def _():
            remote(
                xbuf.at[above, spot], xbuf.at[above, spot], down_s.at[0], z_r.at[above], wide=z + 1
            ).wait_recv()

            @pl.when(z > 0)
            def _():
                downward(xbuf.at[above, spot], above, d).start()

    def spread(slab):
        sideways(slab).start()
        corewise(slab, 0, spot).start()

    def arrive_x(slab):
        piece = xbuf.at[slab, c * nx + other_x]
        remote(piece, piece, x_s.at[slab], x_r.at[slab], expert=other_x).wait_recv()
        corewise(slab, 1, c * nx + other_x).start()

    def arrive_c(slab):
        for j, q in ((0, other_c * nx + x), (1, other_c * nx + other_x)):
            piece = xbuf.at[slab, q]
            remote(piece, piece, c_s.at[slab, j], c_r.at[slab, j], inner=other_c).wait_recv()

    def to_core(k):
        return remote(
            part.at[k, pl.ds(other_c * nx, nx)], core_in.at[k], core_s.at[k], core_r.at[k],
            inner=other_c,
        )

    def to_x(k):
        return remote(x_out.at[k], x_in.at[k], rx_s.at[k], rx_r.at[k], expert=other_x)

    def to_z(k):
        return remote(z_out.at[k], z_in.at[k], rz_s.at[k], rz_r.at[k], wide=flip(z, k))

    def reduce_core(k):
        to_core(k).wait_recv()
        x_out[k] = (
            part[k, c * nx + other_x].astype(f32) + core_in[k, other_x].astype(f32)
        ).astype(bf)
        to_x(k).start()

    def total_of(k):
        return (
            part[k, c * nx + x].astype(f32)
            + core_in[k, x].astype(f32)
            + x_in[k].astype(f32)
        )

    def reduce_x(k):
        to_x(k).wait_recv()

        @pl.when(k > 0)
        def _():
            z_out[k] = total_of(k).astype(bf)
            to_z(k).start()

    groups = held // TOGETHER

    def gating(i, k):
        side = (i % 2) * TOGETHER
        for q in range(quarters):
            lanes = slice(q * share, (q + 1) * share)
            weights = [
                [
                    gates[t * held + i * TOGETHER + j : t * held + i * TOGETHER + j + 1, lanes]
                    for j in range(TOGETHER)
                ]
                for t in range(tasks)
            ]
            for f in range(0, width, 16):
                outs = [made[side + j, f : f + 16, lanes] for j in range(TOGETHER)]
                for t in range(tasks):
                    span = slice(t * width + f, t * width + f + 16)
                    piece = weights[t][0] * outs[0]
                    for j in range(1, TOGETHER):
                        piece = piece + weights[t][j] * outs[j]
                    if i > 0:
                        piece = piece + acc[q, span, :]
                    if i < groups - 1:
                        acc[q, span, :] = piece
                    else:
                        part[k, q, span, :] = piece.astype(bf)

    def stage(i, data, k):
        if i < groups:
            for j in range(TOGETHER):
                e = i * TOGETHER + j
                hidden[(i % 2) * TOGETHER + j] = jnp.maximum(
                    jnp.dot(data, win[e], preferred_element_type=f32), 0.0
                ).astype(bf)
        if 0 < i <= groups:
            side = ((i - 1) % 2) * TOGETHER
            for j in range(TOGETHER):
                e = (i - 1) * TOGETHER + j
                made[side + j] = lax.dot_general(
                    wout[e], hidden[side + j], (((1,), (1,)), ((), ())),
                    preferred_element_type=f32,
                )
        if i > 1:
            gating(i - 2, k)

    def step(k, carry):
        slab = flip(z, k)
        data = xbuf[slab].reshape(rows, depth)
        logits = lax.dot_general(
            gate_ref[...], data, (((0,), (1,)), ((), ())), preferred_element_type=f32
        )
        logits = logits.reshape(tasks, logits.shape[0] // tasks, rows)
        powers = jnp.exp(logits - jnp.max(logits, axis=1, keepdims=True))
        gates_all[...] = powers / jnp.sum(powers, axis=1, keepdims=True)
        for t in range(tasks):
            gates[t * held : (t + 1) * held, :] = gates_all[
                t, pl.ds(pl.multiple_of(x * held, held), held), :
            ]
        after = flip(z, k + 1)

        @pl.when((k > 0) & (k < nz - 1))
        def _():
            arrive_z(k + 1)
            spread(after)

        for i in range(2):
            stage(i, data, k)

        @pl.when(k == 0)
        def _():
            arrive_z(1)
            spread(after)

        @pl.when(k > 1)
        def _():
            reduce_x(k - 2)

        @pl.when(k > 0)
        def _():
            reduce_core(k - 1)

        data = xbuf[slab].reshape(rows, depth)
        for i in range(2, groups + 2):
            stage(i, data, k)
        to_core(k).start()

        @pl.when(k < nz - 1)
        def _():
            arrive_x(after)
            arrive_c(after)

        return carry

    lax.fori_loop(0, nz, step, 0)
    reduce_core(nz - 1)
    reduce_x(nz - 2)
    reduce_x(nz - 1)
    total = total_of(0)
    for k in range(1, nz):
        to_z(k).wait_recv()
        total = total + z_in[k].astype(f32)
    total = total.T
    center = jnp.mean(total, axis=1, keepdims=True)
    spread = jnp.mean(jnp.square(total - center), axis=1, keepdims=True)
    normed = (total - center) * lax.rsqrt(spread + 1e-05) * gain_ref[...].astype(f32)
    out_ref[...] = normed.astype(bf)

    for d in range(nz - 1):

        @pl.when((z < nz - 1) & (z - d >= 0))
        def _():
            upward(xbuf.at[z, spot], z, d).wait_send()

        @pl.when((z > 0) & (z + d < nz))
        def _():
            downward(xbuf.at[z, spot], z, d).wait_send()

    for k in range(1, nz):
        slab = flip(z, k)
        sideways(slab).wait_send()
        corewise(slab, 0, spot).wait_send()
        corewise(slab, 1, spot).wait_send()
        to_z(k).wait_send()
    for k in range(nz):
        to_core(k).wait_send()
        to_x(k).wait_send()


def run_mix(cand, gate_weight, expert_in, expert_out, gain, tasks, collective):
    nz, nx, nc = (lax.axis_size(a) for a in ALL)
    rows, depth = cand.shape
    quarters = nx * nc
    share = rows // quarters
    held, _, units = expert_in.shape
    width = expert_out.shape[1]
    dma = pltpu.SemaphoreType.DMA
    f32, bf = jnp.float32, jnp.bfloat16
    vmem = pl.BlockSpec(memory_space=pltpu.VMEM)
    anywhere = pl.BlockSpec(memory_space=pl.ANY)
    model = tasks * width
    experts_all = gate_weight.shape[1] // tasks
    return pl.pallas_call(
        functools.partial(mix_kernel, tasks),
        in_specs=[anywhere, vmem, anywhere, anywhere, vmem],
        out_specs=vmem,
        out_shape=jax.ShapeDtypeStruct((share, model), bf),
        scratch_shapes=[
            pltpu.VMEM((nz, quarters, share, depth), bf),
            pltpu.VMEM(expert_in.shape, bf),
            pltpu.VMEM(expert_out.shape, bf),
            pltpu.VMEM((tasks, experts_all, rows), f32),
            pltpu.VMEM((tasks * held, rows), f32),
            pltpu.VMEM((2 * TOGETHER, rows, units), bf),
            pltpu.VMEM((2 * TOGETHER, width, rows), f32),
            pltpu.VMEM((quarters, model, share), f32),
            pltpu.VMEM((nz, quarters, model, share), bf),
            pltpu.VMEM((nz, nx, model, share), bf),
            pltpu.VMEM((nz, model, share), bf),
            pltpu.VMEM((nz, model, share), bf),
            pltpu.VMEM((nz, model, share), bf),
            pltpu.VMEM((nz, model, share), bf),
            dma((3,)),
            dma((nz,)),
            dma((nz,)),
            dma((nz,)),
            dma((nz,)),
            dma((nz,)),
            dma((nz, 2)),
            dma((nz, 2)),
            dma((nz,)),
            dma((nz,)),
            dma((nz,)),
            dma((nz,)),
            dma((nz,)),
            dma((nz,)),
        ],
        compiler_params=pltpu.CompilerParams(
            collective_id=collective, has_side_effects=True, vmem_limit_bytes=VMEM_LIMIT
        ),
    )(cand.reshape(quarters, share, depth), gate_weight, expert_in, expert_out, gain)


def score_kernel(
    norm_ref, q_ref, k_ref, v_ref, task_ref, attn_ref, id_ref, out_ref,
    nb, keys, extra, ids, queries, powers, high, sums, partial,
    n_s, n_r, id_s, id_r, up_s, down_s, key_r, p_s, p_r,
):
    (z, x, c), (nz, nx, nc) = place()
    f32, bf = jnp.float32, jnp.bfloat16
    other_x, other_c = 1 - x, 1 - c
    spot = c * nx + x
    quarters, share, depth = nb.shape
    rows = quarters * share
    heads = queries.shape[1] // HD
    tasks = task_ref.shape[0]
    barrier = pltpu.get_barrier_semaphore()
    pl.semaphore_signal(
        barrier, inc=1, device_id={"expert": other_x, "inner": other_c}, device_id_type=MESH
    )
    for axis, here, size in zip(ALL, (z, x, c), (nz, nx, nc)):
        for turned in range(1, size):
            pl.semaphore_signal(
                barrier, inc=1, device_id={axis: turn(here, turned, size)}, device_id_type=MESH
            )
    pl.semaphore_wait(barrier, nz + nx + nc - 2)

    def give(q, j, **where):
        return remote(nb.at[q], nb.at[q], n_s.at[j], n_r.at[j], **where)

    first = remote(norm_ref, nb.at[spot], n_s.at[0], n_r.at[0], expert=other_x)
    second = remote(norm_ref, nb.at[spot], n_s.at[1], n_r.at[1], inner=other_c)
    first.start()
    second.start()
    id_copies = []
    for turned in range(1, nz):
        target = turn(z, turned, nz)
        item = remote(id_ref, ids.at[z], id_s.at[turned], id_r.at[z], wide=target)
        item.start()
        id_copies.append(item)
    ids[z] = id_ref[...]
    nb[spot] = norm_ref[...]
    across = c * nx + other_x
    give(across, 0, expert=other_x).wait_recv()
    third = give(across, 2, inner=other_c)
    third.start()
    give(other_c * nx + x, 1, inner=other_c).wait_recv()
    give(other_c * nx + other_x, 2, inner=other_c).wait_recv()
    data = nb[...].reshape(rows, depth)
    half = heads // 2 * HD
    keys_own = jnp.dot(data, k_ref[...], preferred_element_type=f32).astype(bf)
    values = jnp.dot(data, v_ref[...], preferred_element_type=f32).astype(bf)
    for j in range(2):
        keys[z, j] = keys_own[:, j * half : (j + 1) * half]
    shape = (heads * tasks, heads * HD)
    row = lax.broadcasted_iota(jnp.int32, shape, 0) // tasks
    column = lax.broadcasted_iota(jnp.int32, shape, 1) // HD
    stacked = jnp.concatenate([attn_ref[...].astype(f32)] * heads, axis=0)
    lift = lax.dot_general(
        jnp.where(row == column, stacked, 0.0).astype(bf), values, (((1,), (1,)), ((), ())),
        preferred_element_type=f32,
    )
    coarse = lift.astype(bf)
    fine = (lift - coarse.astype(f32)).astype(bf).astype(f32)
    coarse = coarse.astype(f32)
    ones = jnp.ones((1, rows), f32)
    blank = jnp.zeros((16 - 2 * tasks - 1, rows), f32)
    for h in range(heads):
        piece = slice(h * tasks, (h + 1) * tasks)
        extra[z, h * 16 : (h + 1) * 16, :] = jnp.concatenate(
            [coarse[piece], fine[piece], ones, blank], axis=0
        ).astype(bf)

    def parts(slab):
        return [keys.at[slab, 0], keys.at[slab, 1], extra.at[slab]]

    def upward(slab, d, j):
        piece = parts(slab)[j]
        return remote(piece, piece, up_s.at[d, j], key_r.at[slab, j], wide=z + 1)

    def downward(slab, d, j):
        piece = parts(slab)[j]
        return remote(piece, piece, down_s.at[d, j], key_r.at[slab, j], wide=z - 1)

    order = (2, 0, 1)

    @pl.when(z < nz - 1)
    def _():
        for j in order:
            upward(z, 0, j).start()

    @pl.when(z > 0)
    def _():
        for j in order:
            downward(z, 0, j).start()

    queries[...] = (
        jnp.dot(data, q_ref[...], preferred_element_type=f32) * (1.0 / math.sqrt(HD))
    ).astype(bf)
    for item in id_copies:
        item.wait_send()
    for turned in range(1, nz):
        source = turn(z, turned, nz)
        remote(id_ref, ids.at[source], id_s.at[turned], id_r.at[source], wide=source).wait_recv()

    own = jnp.broadcast_to(id_ref[...].astype(f32), (8, rows)).T[:, :1]

    def attend(slab, fresh):
        same = own == ids[slab].astype(f32)
        tops = []
        for h in range(heads):
            span = slice(h * HD, (h + 1) * HD)
            inside = (h * HD) % half
            affinity = lax.dot_general(
                queries[:, span],
                keys[slab, h * HD // half][:, inside : inside + HD],
                (((1,), (1,)), ((), ())),
                preferred_element_type=f32,
            )
            affinity = jnp.where(same, affinity, -1e30)
            top = jnp.max(affinity, axis=1, keepdims=True)
            powers[h] = jnp.exp(affinity - top).astype(bf)
            tops.append(top)
        for h in range(heads):
            got = lax.dot_general(
                powers[h], extra[slab, h * 16 : (h + 1) * 16, :], (((1,), (1,)), ((), ())),
                preferred_element_type=f32,
            )
            if fresh:
                high[h] = tops[h]
                sums[h] = got
            else:
                peak = jnp.maximum(high[h], tops[h])
                sums[h] = sums[h] * jnp.exp(high[h] - peak) + got * jnp.exp(tops[h] - peak)
                high[h] = peak

    attend(z, True)

    def step(d, carry):
        below, above = z - d, z + d

        @pl.when(below >= 0)
        def _():
            for j in order:
                piece = parts(below)[j]
                remote(piece, piece, up_s.at[0, j], key_r.at[below, j], wide=z - 1).wait_recv()

                @pl.when(z < nz - 1)
                def _():
                    upward(below, d, j).start()

        @pl.when(above < nz)
        def _():
            for j in order:
                piece = parts(above)[j]
                remote(piece, piece, down_s.at[0, j], key_r.at[above, j], wide=z + 1).wait_recv()

                @pl.when(z > 0)
                def _():
                    downward(above, d, j).start()

        attend(flip(z, d), False)
        return carry

    lax.fori_loop(1, nz, step, 0)
    result = None
    for h in range(heads):
        got = sums[h]
        term = (got[:, :tasks] + got[:, tasks : 2 * tasks]) / got[:, 2 * tasks : 2 * tasks + 1]
        result = term if result is None else result + term
    lanes = partial.shape[2]
    result = jnp.concatenate([result, jnp.zeros((rows, 128 - tasks), f32)], axis=1)
    partial[0] = result.T[:8, :]
    sends = []
    for j, where in enumerate(
        ({"inner": other_c}, {"expert": other_x}, {"expert": other_x, "inner": other_c})
    ):
        item = remote(partial.at[0], partial.at[j + 1], p_s.at[j], p_r.at[j], **where)
        item.start()
        sends.append(item)
    base = lax.dot_general(
        task_ref[...], data, (((1,), (1,)), ((), ())), preferred_element_type=f32
    )
    for item in sends:
        item.wait()
    everything = (partial[0] + partial[1]) + (partial[2] + partial[3])
    out_ref[...] = everything[:tasks, :] + base
    first.wait_send()
    second.wait_send()
    third.wait_send()
    for d in range(nz - 1):
        for j in order:

            @pl.when((z < nz - 1) & (z - d >= 0))
            def _():
                upward(z, d, j).wait_send()

            @pl.when((z > 0) & (z + d < nz))
            def _():
                downward(z, d, j).wait_send()


def run_scores(normed, query, key, value, task, attn, request_of, collective):
    nz, nx, nc = (lax.axis_size(a) for a in ALL)
    share, depth = normed.shape
    quarters = nx * nc
    rows = share * quarters
    width = query.shape[1]
    heads = width // HD
    tasks = task.shape[1]
    dma = pltpu.SemaphoreType.DMA
    f32, bf = jnp.float32, jnp.bfloat16
    vmem = pl.BlockSpec(memory_space=pltpu.VMEM)
    return pl.pallas_call(
        score_kernel,
        in_specs=[vmem] * 7,
        out_specs=vmem,
        out_shape=jax.ShapeDtypeStruct((tasks, rows), f32),
        scratch_shapes=[
            pltpu.VMEM((quarters, share, depth), bf),
            pltpu.VMEM((nz, 2, rows, width // 2), bf),
            pltpu.VMEM((nz, heads * 16, rows), bf),
            pltpu.VMEM((nz, 1, rows), jnp.int32),
            pltpu.VMEM((rows, width), bf),
            pltpu.VMEM((heads, rows, rows), bf),
            pltpu.VMEM((heads, rows, 1), f32),
            pltpu.VMEM((heads, rows, 16), f32),
            pltpu.VMEM((nx * nc, 8, rows), f32),
            dma((3,)),
            dma((3,)),
            dma((nz,)),
            dma((nz,)),
            dma((nz, 3)),
            dma((nz, 3)),
            dma((nz, 3)),
            dma((3,)),
            dma((3,)),
        ],
        compiler_params=pltpu.CompilerParams(
            collective_id=collective, has_side_effects=True, vmem_limit_bytes=VMEM_LIMIT
        ),
    )(normed, query, key, value, task.T, attn.T, request_of[None, :]).T


def fused(sizes, rows, heads, held):
    return sizes == (4, 2, 2) and rows % 512 == 0 and heads == 4 and held % (2 * TOGETHER) == 0


def local(
    candidates,
    gate_weight,
    expert_in,
    expert_out,
    norm_gain,
    query_weight,
    key_weight,
    value_weight,
    task_weight,
    attn_weight,
    request_of,
):
    rows = candidates.shape[0]
    tasks = task_weight.shape[1]
    nz, nx, nc = (lax.axis_size(a) for a in ALL)
    if fused((nz, nx, nc), rows, query_weight.shape[1] // HD, expert_in.shape[0]):
        normed = run_mix(
            candidates, gate_weight, expert_in, expert_out, norm_gain[None, :], tasks, 3
        )
        return run_scores(
            normed, query_weight, key_weight, value_weight, task_weight, attn_weight, request_of, 4
        )
    share = rows // (nx * nc)
    spot = lax.axis_index("inner") * nx + lax.axis_index("expert")
    wide = lax.axis_index("wide")
    quarter = lax.dynamic_slice_in_dim(candidates, spot * share, share, 0)
    everyone, requests = run_gather(quarter, request_of[None, :], 0)
    partial_mix = run_experts(everyone, gate_weight, expert_in, expert_out, tasks)
    normed = run_reduce(partial_mix, norm_gain[None, :], share, 1)
    normed_all = run_gather(normed, None, 2)
    own = lax.dynamic_slice_in_dim(normed_all, wide * rows, rows, 0)
    queries = jnp.dot(own, query_weight, preferred_element_type=jnp.float32).astype(jnp.bfloat16)
    keys = jnp.dot(normed_all, key_weight, preferred_element_type=jnp.float32).astype(jnp.bfloat16)
    values = jnp.dot(normed_all, value_weight, preferred_element_type=jnp.float32).astype(
        jnp.bfloat16
    )
    term = run_attention(
        queries, keys, values, request_of[:, None], requests, attn_weight
    )
    attention = lax.psum(term.T, ("expert", "inner")).T
    return jnp.dot(own, task_weight, preferred_element_type=jnp.float32) + attention


def solution(mesh):
    return jax.shard_map(
        local,
        mesh=mesh,
        in_specs=(
            P(("groups", "wide"), None),
            P(),
            P("expert", None, ("wide", "inner")),
            P("expert", None, ("wide", "inner")),
            P(),
            P(None, ("expert", "inner")),
            P(None, ("expert", "inner")),
            P(None, ("expert", "inner")),
            P(),
            P(("expert", "inner"), None),
            P(("groups", "wide")),
        ),
        out_specs=P(("groups", "wide"), None),
        check_vma=False,
    )
```

```python
import functools
import math

import jax
import jax.numpy as jnp
from jax import lax
from jax.experimental import pallas as pl
from jax.experimental.pallas import tpu as pltpu
from jax.sharding import PartitionSpec as P

HD = 64
ALL = ("wide", "expert", "inner")
VMEM_LIMIT = 60 * 1024 * 1024


MESH = pl.DeviceIdType.MESH


def place():
    return tuple(lax.axis_index(a) for a in ALL), tuple(lax.axis_size(a) for a in ALL)


def turn(start, step, size):
    return lax.rem(start + step, size)


def greet():
    mine, sizes = place()
    barrier = pltpu.get_barrier_semaphore()
    for axis, here, size in zip(ALL, mine, sizes):
        for step in range(1, size):
            pl.semaphore_signal(
                barrier, inc=1, device_id={axis: turn(here, step, size)}, device_id_type=MESH
            )
    pl.semaphore_wait(barrier, sum(sizes) - len(sizes))


def gather_kernel(with_ids, *refs):
    if with_ids:
        own_ref, id_ref, out_ref, ids_ref, recv, send_z, send_x, send_c, local_sem, id_r, id_s = refs
    else:
        own_ref, out_ref, recv, send_z, send_x, send_c, local_sem = refs
    (z, x, c), (nz, nx, nc) = place()
    greet()

    def copy(src, zs, xs, cs, sem, axis, target):
        return pltpu.make_async_remote_copy(
            src_ref=src,
            dst_ref=out_ref.at[zs, cs, xs],
            send_sem=sem,
            recv_sem=recv.at[zs, cs, xs],
            device_id={axis: target},
            device_id_type=MESH,
        )

    def arrived(zs, xs, cs):
        copy(out_ref.at[zs, cs, xs], zs, xs, cs, send_z.at[0], "inner", turn(c, 1, nc)).wait_recv()

    sent = []

    def push(*what):
        item = copy(*what)
        item.start()
        sent.append(item)

    def spread_x(src, k, zs):
        for step in range(1, nx):
            push(src, zs, x, c, send_x.at[k, step - 1], "expert", turn(x, step, nx))

    def spread_c(src, k, j, zs, xs):
        for step in range(1, nc):
            push(src, zs, xs, c, send_c.at[k, j, step - 1], "inner", turn(c, step, nc))

    for step in range(1, nz):
        push(own_ref, z, x, c, send_z.at[step - 1], "wide", turn(z, step, nz))
    spread_x(own_ref, 0, z)
    spread_c(own_ref, 0, 0, z, x)
    keep = pltpu.make_async_copy(own_ref, out_ref.at[z, c, x], local_sem.at[0])
    keep.start()
    if with_ids:
        id_copies = []
        for step in range(1, nz):
            item = pltpu.make_async_remote_copy(
                src_ref=id_ref,
                dst_ref=ids_ref.at[z],
                send_sem=id_s.at[step - 1],
                recv_sem=id_r.at[z],
                device_id={"wide": turn(z, step, nz)},
                device_id_type=MESH,
            )
            item.start()
            id_copies.append(item)
        ids_ref[z] = id_ref[...]

    def pass_x(k):
        zs = turn(z, k, nz)
        for step in range(1, nx):
            xs = turn(x, step, nx)
            arrived(zs, xs, c)
            spread_c(out_ref.at[zs, c, xs], k, step, zs, xs)

    for k in range(1, nz):
        zs = turn(z, k, nz)
        arrived(zs, x, c)
        spread_x(out_ref.at[zs, c, x], k, zs)
        spread_c(out_ref.at[zs, c, x], k, 0, zs, x)
        pass_x(k - 1)
    pass_x(nz - 1)
    for k in range(nz):
        for j in range(nx):
            for step in range(1, nc):
                arrived(turn(z, k, nz), turn(x, j, nx), turn(c, step, nc))
    for item in sent:
        item.wait_send()
    keep.wait()
    if with_ids:
        for step in range(1, nz):
            zs = turn(z, step, nz)
            pltpu.make_async_remote_copy(
                src_ref=id_ref,
                dst_ref=ids_ref.at[zs],
                send_sem=id_s.at[step - 1],
                recv_sem=id_r.at[zs],
                device_id={"wide": zs},
                device_id_type=MESH,
            ).wait_recv()
        for item in id_copies:
            item.wait_send()


def run_gather(own, ids, collective):
    nz, nx, nc = (lax.axis_size(a) for a in ALL)
    dma = pltpu.SemaphoreType.DMA
    with_ids = ids is not None
    shape = jax.ShapeDtypeStruct((nz, nc, nx) + own.shape, own.dtype)
    vmem = pl.BlockSpec(memory_space=pltpu.VMEM)
    anywhere = pl.BlockSpec(memory_space=pl.ANY)
    scratch = [
        dma((nz, nc, nx)),
        dma((max(nz - 1, 1),)),
        dma((nz, max(nx - 1, 1))),
        dma((nz, nx, max(nc - 1, 1))),
        dma((1,)),
    ]
    if with_ids:
        scratch += [dma((nz,)), dma((max(nz - 1, 1),))]
    out = pl.pallas_call(
        functools.partial(gather_kernel, with_ids),
        in_specs=[vmem, vmem] if with_ids else [vmem],
        out_specs=[anywhere, vmem] if with_ids else anywhere,
        out_shape=[shape, jax.ShapeDtypeStruct((nz,) + ids.shape, ids.dtype)] if with_ids else shape,
        scratch_shapes=scratch,
        compiler_params=pltpu.CompilerParams(collective_id=collective, has_side_effects=True),
    )(*([own, ids] if with_ids else [own]))
    depth = own.shape[1]
    if with_ids:
        return out[0].reshape(-1, depth), out[1].reshape(1, -1)
    return out.reshape(-1, depth)


def reduce_kernel(
    part_ref, gain_ref, out_ref, mine, core_in, x_out, x_in, z_out, z_in,
    local_sem, core_s, core_r, x_s, x_r, z_s, z_r,
):
    (z, x, c), (nz, nx, nc) = place()
    f32 = jnp.float32
    greet()
    other = turn(c, 1, nc)
    core, kept = [], []
    for k in range(nz):
        s = turn(z, k + 1, nz)
        item = pltpu.make_async_remote_copy(
            src_ref=part_ref.at[s, other],
            dst_ref=core_in.at[k],
            send_sem=core_s.at[k],
            recv_sem=core_r.at[k],
            device_id={"inner": other},
            device_id_type=MESH,
        )
        item.start()
        core.append(item)
        stay = pltpu.make_async_copy(part_ref.at[s, c], mine.at[k], local_sem.at[k])
        stay.start()
        kept.append(stay)

    def pair(k, xs):
        return mine[k, xs].astype(f32) + core_in[k, xs].astype(f32)

    across, along = [], []

    def finish(k):
        total = pair(k, x)
        for step in range(1, nx):
            across[k][step - 1].wait_recv()
            total = total + x_in[k, step - 1].astype(f32)
        if k == nz - 1:
            return total
        z_out[k] = total.astype(z_out.dtype)
        item = pltpu.make_async_remote_copy(
            src_ref=z_out.at[k],
            dst_ref=z_in.at[k],
            send_sem=z_s.at[k],
            recv_sem=z_r.at[k],
            device_id={"wide": turn(z, k + 1, nz)},
            device_id_type=MESH,
        )
        item.start()
        along.append(item)

    for k in range(nz):
        kept[k].wait()
        core[k].wait_recv()
        items = []
        for step in range(1, nx):
            xs = turn(x, step, nx)
            x_out[k, step - 1] = pair(k, xs).astype(x_out.dtype)
            item = pltpu.make_async_remote_copy(
                src_ref=x_out.at[k, step - 1],
                dst_ref=x_in.at[k, step - 1],
                send_sem=x_s.at[k, step - 1],
                recv_sem=x_r.at[k, step - 1],
                device_id={"expert": xs},
                device_id_type=MESH,
            )
            item.start()
            items.append(item)
        across.append(items)
        if k > 0:
            finish(k - 1)
    total = finish(nz - 1)
    for k in range(nz - 1):
        along[k].wait_recv()
        total = total + z_in[k].astype(f32)
    center = jnp.mean(total, axis=1, keepdims=True)
    spread = jnp.mean(jnp.square(total - center), axis=1, keepdims=True)
    normed = (total - center) * lax.rsqrt(spread + 1e-05) * gain_ref[...].astype(f32)
    out_ref[...] = normed.astype(out_ref.dtype)
    for item in core + along + [i for items in across for i in items]:
        item.wait_send()


def run_reduce(part, gain, share, collective):
    nz, nx, nc = (lax.axis_size(a) for a in ALL)
    width = part.shape[1]
    dma = pltpu.SemaphoreType.DMA
    kind = part.dtype
    part = part.reshape(nz, nc, nx, share, width)
    few = max(nx - 1, 1)
    vmem = pl.BlockSpec(memory_space=pltpu.VMEM)
    return pl.pallas_call(
        reduce_kernel,
        in_specs=[pl.BlockSpec(memory_space=pl.ANY), vmem],
        out_specs=vmem,
        out_shape=jax.ShapeDtypeStruct((share, width), kind),
        scratch_shapes=[
            pltpu.VMEM((nz, nx, share, width), kind),
            pltpu.VMEM((nz, nx, share, width), kind),
            pltpu.VMEM((nz, few, share, width), kind),
            pltpu.VMEM((nz, few, share, width), kind),
            pltpu.VMEM((nz, share, width), kind),
            pltpu.VMEM((nz, share, width), kind),
            dma((nz,)),
            dma((nz,)),
            dma((nz,)),
            dma((nz, few)),
            dma((nz, few)),
            dma((nz,)),
            dma((nz,)),
        ],
        compiler_params=pltpu.CompilerParams(
            collective_id=collective, has_side_effects=True, vmem_limit_bytes=VMEM_LIMIT
        ),
    )(part, gain)


def expert_kernel(tasks, x_ref, gate_ref, win_ref, wout_ref, out_ref, acc_ref):
    rows = x_ref.shape[0]
    columns = gate_ref.shape[1]
    experts_all = columns // tasks
    held, _, _ = win_ref.shape
    width = wout_ref.shape[1]
    x = x_ref[...]
    logits = jnp.dot(x, gate_ref[...], preferred_element_type=jnp.float32)
    task = lax.broadcasted_iota(jnp.int32, (rows, columns), 1) // experts_all
    top = jnp.zeros_like(logits)
    for t in range(tasks):
        high = jnp.max(jnp.where(task == t, logits, -jnp.inf), axis=1, keepdims=True)
        top = jnp.where(task == t, high, top)
    powers = jnp.exp(logits - top)
    total = jnp.ones_like(logits)
    for t in range(tasks):
        part = jnp.sum(jnp.where(task == t, powers, 0.0), axis=1, keepdims=True)
        total = jnp.where(task == t, part, total)
    gates = powers / total
    shift = lax.rem(columns - lax.axis_index("expert") * held, columns)
    gates = pltpu.roll(gates, shift, 1)
    together = min(4, held)
    for first in range(0, held, together):
        made = []
        for e in range(first, first + together):
            hidden = jnp.maximum(
                jnp.dot(x, win_ref[e], preferred_element_type=jnp.float32), 0.0
            ).astype(jnp.bfloat16)
            made.append(
                lax.dot_general(
                    hidden,
                    wout_ref[e],
                    (((1,), (1,)), ((), ())),
                    preferred_element_type=jnp.float32,
                )
            )
        for t in range(tasks):
            piece = None
            for j, output in enumerate(made):
                lane = t * experts_all + first + j
                term = gates[:, lane : lane + 1] * output
                piece = term if piece is None else piece + term
            span = slice(t * width, (t + 1) * width)
            if first > 0:
                piece = piece + acc_ref[:, span]
            if first + together < held:
                acc_ref[:, span] = piece
            else:
                out_ref[:, span] = piece.astype(out_ref.dtype)


def run_experts(x, gate_weight, expert_in, expert_out, tasks):
    rows, depth = x.shape
    held, _, units = expert_in.shape
    width = expert_out.shape[1]
    block = min(512, rows)
    return pl.pallas_call(
        functools.partial(expert_kernel, tasks),
        grid=(rows // block,),
        in_specs=[
            pl.BlockSpec((block, depth), lambda i: (i, 0)),
            pl.BlockSpec(gate_weight.shape, lambda i: (0, 0)),
            pl.BlockSpec(expert_in.shape, lambda i: (0, 0, 0), pipeline_mode=pl.Buffered(1)),
            pl.BlockSpec(expert_out.shape, lambda i: (0, 0, 0), pipeline_mode=pl.Buffered(1)),
        ],
        out_specs=pl.BlockSpec((block, tasks * width), lambda i: (i, 0)),
        out_shape=jax.ShapeDtypeStruct((rows, tasks * width), jnp.bfloat16),
        scratch_shapes=[pltpu.VMEM((block, tasks * width), jnp.float32)],
        compiler_params=pltpu.CompilerParams(vmem_limit_bytes=VMEM_LIMIT),
    )(x, gate_weight, expert_in, expert_out)


def attention_kernel(q_ref, k_ref, v_ref, own_ref, all_ref, weight_ref, out_ref):
    same = own_ref[...] == all_ref[...]
    factor = 1.0 / math.sqrt(HD)
    result = None
    for first in range(0, q_ref.shape[1], HD):
        span = slice(first, first + HD)
        affinity = (
            lax.dot_general(
                q_ref[:, span],
                k_ref[:, span],
                (((1,), (1,)), ((), ())),
                preferred_element_type=jnp.float32,
            )
            * factor
        )
        affinity = jnp.where(same, affinity, -1e30)
        highest = jnp.max(affinity, axis=1, keepdims=True)
        powers = jnp.exp(affinity - highest)
        total = jnp.sum(powers, axis=1, keepdims=True)
        context = jnp.dot(
            powers.astype(jnp.bfloat16), v_ref[:, span], preferred_element_type=jnp.float32
        )
        context = (context / total).astype(jnp.bfloat16)
        term = jnp.dot(context, weight_ref[span, :], preferred_element_type=jnp.float32)
        result = term if result is None else result + term
    out_ref[...] = result


def run_attention(q, k, v, own, every, weight):
    rows, width = q.shape
    keys = k.shape[0]
    tasks = weight.shape[1]
    block = min(128, rows)
    return pl.pallas_call(
        attention_kernel,
        grid=(rows // block,),
        in_specs=[
            pl.BlockSpec((block, width), lambda i: (i, 0)),
            pl.BlockSpec((keys, width), lambda i: (0, 0)),
            pl.BlockSpec((keys, width), lambda i: (0, 0)),
            pl.BlockSpec((block, 1), lambda i: (i, 0)),
            pl.BlockSpec((1, keys), lambda i: (0, 0)),
            pl.BlockSpec((width, tasks), lambda i: (0, 0)),
        ],
        out_specs=pl.BlockSpec((block, tasks), lambda i: (i, 0)),
        out_shape=jax.ShapeDtypeStruct((rows, tasks), jnp.float32),
        compiler_params=pltpu.CompilerParams(vmem_limit_bytes=VMEM_LIMIT),
    )(q, k, v, own, every, weight)


def flip(position, step):
    low = lax.rem(position, 2)
    high = position // 2
    return (high + (step // 2) * (1 - 2 * high)) * 2 + low + lax.rem(step, 2) * (1 - 2 * low)


def remote(src, dst, send, recv, **where):
    return pltpu.make_async_remote_copy(
        src_ref=src, dst_ref=dst, send_sem=send, recv_sem=recv, device_id=where,
        device_id_type=MESH,
    )


TOGETHER = 4


def mix_part(
    tasks, cand_ref, gate_ref, win_hbm, wout_hbm, gain_ref, nb,
    xbuf, win, wout, gates_all, gates, hidden, made, acc, part, core_in, x_out, x_in, z_out, z_in,
    load_sem, up_s, down_s, z_r, x_s, x_r, c_s, c_r, core_s, core_r, rx_s, rx_r, rz_s, rz_r,
):
    (z, x, c), (nz, nx, nc) = place()
    f32, bf = jnp.float32, jnp.bfloat16
    other_x, other_c = 1 - x, 1 - c
    held = win.shape[0]
    quarters, share, depth = xbuf.shape[1:]
    rows = quarters * share
    width = wout.shape[1]
    spot = c * nx + x
    loads = [
        pltpu.make_async_copy(cand_ref, xbuf.at[z], load_sem.at[0]),
        pltpu.make_async_copy(win_hbm, win, load_sem.at[1]),
        pltpu.make_async_copy(wout_hbm, wout, load_sem.at[2]),
    ]
    for item in loads:
        item.start()
    greet_all()

    def upward(src, slab, d):
        return remote(src, xbuf.at[slab, spot], up_s.at[d], z_r.at[slab], wide=z + 1)

    def downward(src, slab, d):
        return remote(src, xbuf.at[slab, spot], down_s.at[d], z_r.at[slab], wide=z - 1)

    def sideways(slab):
        piece = xbuf.at[slab, spot]
        return remote(piece, piece, x_s.at[slab], x_r.at[slab], expert=other_x)

    def corewise(slab, j, q):
        piece = xbuf.at[slab, q]
        return remote(piece, piece, c_s.at[slab, j], c_r.at[slab, j], inner=other_c)

    @pl.when(z < nz - 1)
    def _():
        upward(cand_ref.at[spot], z, 0).start()

    @pl.when(z > 0)
    def _():
        downward(cand_ref.at[spot], z, 0).start()

    for item in loads:
        item.wait()

    def arrive_z(d):
        below, above = z - d, z + d

        @pl.when(below >= 0)
        def _():
            remote(
                xbuf.at[below, spot], xbuf.at[below, spot], up_s.at[0], z_r.at[below], wide=z - 1
            ).wait_recv()

            @pl.when(z < nz - 1)
            def _():
                upward(xbuf.at[below, spot], below, d).start()

        @pl.when(above < nz)
        def _():
            remote(
                xbuf.at[above, spot], xbuf.at[above, spot], down_s.at[0], z_r.at[above], wide=z + 1
            ).wait_recv()

            @pl.when(z > 0)
            def _():
                downward(xbuf.at[above, spot], above, d).start()

    def spread(slab):
        sideways(slab).start()
        corewise(slab, 0, spot).start()

    def arrive_x(slab):
        piece = xbuf.at[slab, c * nx + other_x]
        remote(piece, piece, x_s.at[slab], x_r.at[slab], expert=other_x).wait_recv()
        corewise(slab, 1, c * nx + other_x).start()

    def arrive_c(slab):
        for j, q in ((0, other_c * nx + x), (1, other_c * nx + other_x)):
            piece = xbuf.at[slab, q]
            remote(piece, piece, c_s.at[slab, j], c_r.at[slab, j], inner=other_c).wait_recv()

    def to_core(k):
        return remote(
            part.at[k, pl.ds(other_c * nx, nx)], core_in.at[k], core_s.at[k], core_r.at[k],
            inner=other_c,
        )

    def to_x(k):
        return remote(x_out.at[k], x_in.at[k], rx_s.at[k], rx_r.at[k], expert=other_x)

    def to_z(k):
        return remote(z_out.at[k], z_in.at[k], rz_s.at[k], rz_r.at[k], wide=flip(z, k))

    def reduce_core(k):
        to_core(k).wait_recv()
        x_out[k] = (
            part[k, c * nx + other_x].astype(f32) + core_in[k, other_x].astype(f32)
        ).astype(bf)
        to_x(k).start()

    def total_of(k):
        return (
            part[k, c * nx + x].astype(f32)
            + core_in[k, x].astype(f32)
            + x_in[k].astype(f32)
        )

    def reduce_x(k):
        to_x(k).wait_recv()

        @pl.when(k > 0)
        def _():
            z_out[k] = total_of(k).astype(bf)
            to_z(k).start()

    groups = held // TOGETHER

    def gating(i, k):
        side = (i % 2) * TOGETHER
        for q in range(quarters):
            lanes = slice(q * share, (q + 1) * share)
            weights = [
                [
                    gates[t * held + i * TOGETHER + j : t * held + i * TOGETHER + j + 1, lanes]
                    for j in range(TOGETHER)
                ]
                for t in range(tasks)
            ]
            for f in range(0, width, 16):
                outs = [made[side + j, f : f + 16, lanes] for j in range(TOGETHER)]
                for t in range(tasks):
                    span = slice(t * width + f, t * width + f + 16)
                    piece = weights[t][0] * outs[0]
                    for j in range(1, TOGETHER):
                        piece = piece + weights[t][j] * outs[j]
                    if i > 0:
                        piece = piece + acc[q, span, :]
                    if i < groups - 1:
                        acc[q, span, :] = piece
                    else:
                        part[k, q, span, :] = piece.astype(bf)

    def stage(i, data, k):
        if i < groups:
            for j in range(TOGETHER):
                e = i * TOGETHER + j
                hidden[(i % 2) * TOGETHER + j] = jnp.maximum(
                    jnp.dot(data, win[e], preferred_element_type=f32), 0.0
                ).astype(bf)
        if 0 < i <= groups:
            side = ((i - 1) % 2) * TOGETHER
            for j in range(TOGETHER):
                e = (i - 1) * TOGETHER + j
                made[side + j] = lax.dot_general(
                    wout[e], hidden[side + j], (((1,), (1,)), ((), ())),
                    preferred_element_type=f32,
                )
        if i > 1:
            gating(i - 2, k)

    def step(k, carry):
        slab = flip(z, k)
        data = xbuf[slab].reshape(rows, depth)
        logits = lax.dot_general(
            gate_ref[...], data, (((0,), (1,)), ((), ())), preferred_element_type=f32
        )
        logits = logits.reshape(tasks, logits.shape[0] // tasks, rows)
        powers = jnp.exp(logits - jnp.max(logits, axis=1, keepdims=True))
        gates_all[...] = powers / jnp.sum(powers, axis=1, keepdims=True)
        for t in range(tasks):
            gates[t * held : (t + 1) * held, :] = gates_all[
                t, pl.ds(pl.multiple_of(x * held, held), held), :
            ]
        after = flip(z, k + 1)

        @pl.when((k > 0) & (k < nz - 1))
        def _():
            arrive_z(k + 1)
            spread(after)

        for i in range(2):
            stage(i, data, k)

        @pl.when(k == 0)
        def _():
            arrive_z(1)
            spread(after)

        @pl.when(k > 1)
        def _():
            reduce_x(k - 2)

        @pl.when(k > 0)
        def _():
            reduce_core(k - 1)

        data = xbuf[slab].reshape(rows, depth)
        for i in range(2, groups + 2):
            stage(i, data, k)
        to_core(k).start()

        @pl.when(k < nz - 1)
        def _():
            arrive_x(after)
            arrive_c(after)

        return carry

    lax.fori_loop(0, nz, step, 0)
    reduce_core(nz - 1)
    reduce_x(nz - 2)
    reduce_x(nz - 1)
    total = total_of(0)
    for k in range(1, nz):
        to_z(k).wait_recv()
        total = total + z_in[k].astype(f32)
    total = total.T
    center = jnp.mean(total, axis=1, keepdims=True)
    spread = jnp.mean(jnp.square(total - center), axis=1, keepdims=True)
    gain = gain_ref[...].astype(f32)
    gain = jnp.concatenate([gain[i : i + 1, :] for i in range(gain.shape[0])], axis=1)
    normed = (total - center) * lax.rsqrt(spread + 1e-05) * gain
    nb[spot] = normed.astype(bf)
    yield
    for d in range(nz - 1):

        @pl.when((z < nz - 1) & (z - d >= 0))
        def _():
            upward(xbuf.at[z, spot], z, d).wait_send()

        @pl.when((z > 0) & (z + d < nz))
        def _():
            downward(xbuf.at[z, spot], z, d).wait_send()

    for k in range(1, nz):
        slab = flip(z, k)
        sideways(slab).wait_send()
        corewise(slab, 0, spot).wait_send()
        corewise(slab, 1, spot).wait_send()
        to_z(k).wait_send()
    for k in range(nz):
        to_core(k).wait_send()
        to_x(k).wait_send()


def greet_all():
    (z, x, c), (nz, nx, nc) = place()
    barrier = pltpu.get_barrier_semaphore()
    pl.semaphore_signal(
        barrier, inc=1, device_id={"expert": 1 - x, "inner": 1 - c}, device_id_type=MESH
    )
    for axis, here, size in zip(ALL, (z, x, c), (nz, nx, nc)):
        for turned in range(1, size):
            pl.semaphore_signal(
                barrier, inc=1, device_id={axis: turn(here, turned, size)}, device_id_type=MESH
            )
    pl.semaphore_wait(barrier, nz + nx + nc - 2)


def whole_kernel(
    tasks, mix_count, cand_ref, gate_ref, win_hbm, wout_hbm, gain_ref,
    q_hbm, k_hbm, v_hbm, task_ref, attn_ref, id_ref, out_ref, *scratch
):
    nb = scratch[mix_count]
    mix = mix_part(
        tasks, cand_ref, gate_ref, win_hbm, wout_hbm, gain_ref, nb, *scratch[:mix_count]
    )
    score = score_part(
        q_hbm, k_hbm, v_hbm, task_ref, attn_ref, id_ref, out_ref, *scratch[mix_count:]
    )
    next(score)
    next(mix)
    next(score, None)
    next(mix, None)


def score_part(
    q_hbm, k_hbm, v_hbm, task_ref, attn_ref, id_ref, out_ref,
    nb, q_ref, k_ref, v_ref, keys, extra, ids, queries, powers, high, sums, partial,
    load_sem, n_s, n_r, id_s, id_r, up_s, down_s, key_r, p_s, p_r,
):
    (z, x, c), (nz, nx, nc) = place()
    f32, bf = jnp.float32, jnp.bfloat16
    other_x, other_c = 1 - x, 1 - c
    spot = c * nx + x
    quarters, share, depth = nb.shape
    rows = quarters * share
    heads = queries.shape[1] // HD
    tasks = task_ref.shape[0]
    loads = [
        pltpu.make_async_copy(k_hbm, k_ref, load_sem.at[0]),
        pltpu.make_async_copy(v_hbm, v_ref, load_sem.at[1]),
        pltpu.make_async_copy(q_hbm, q_ref, load_sem.at[2]),
    ]
    for item in loads:
        item.start()
    yield

    def give(q, j, **where):
        return remote(nb.at[q], nb.at[q], n_s.at[j], n_r.at[j], **where)

    first = give(spot, 0, expert=other_x)
    second = give(spot, 1, inner=other_c)
    first.start()
    second.start()
    id_copies = []
    for turned in range(1, nz):
        target = turn(z, turned, nz)
        item = remote(id_ref, ids.at[z], id_s.at[turned], id_r.at[z], wide=target)
        item.start()
        id_copies.append(item)
    ids[z] = id_ref[...]
    for item in loads:
        item.wait()
    own = jnp.broadcast_to(id_ref[...].astype(f32), (8, rows)).T[:, :1]
    extra[:, 2 * heads * tasks :, :] = jnp.ones((nz, 16, rows), bf)
    across = c * nx + other_x
    give(across, 0, expert=other_x).wait_recv()
    third = give(across, 2, inner=other_c)
    third.start()
    give(other_c * nx + x, 1, inner=other_c).wait_recv()
    give(other_c * nx + other_x, 2, inner=other_c).wait_recv()
    data = nb[...].reshape(rows, depth)
    half = heads // 2 * HD
    keys_own = jnp.dot(data, k_ref[...], preferred_element_type=f32).astype(bf)
    values = jnp.dot(data, v_ref[...], preferred_element_type=f32).astype(bf)
    for j in range(2):
        keys[z, j] = keys_own[:, j * half : (j + 1) * half]
    shape = (heads * tasks, heads * HD)
    row = lax.broadcasted_iota(jnp.int32, shape, 0) // tasks
    column = lax.broadcasted_iota(jnp.int32, shape, 1) // HD
    stacked = jnp.concatenate([attn_ref[...].astype(f32)] * heads, axis=0)
    lift = lax.dot_general(
        jnp.where(row == column, stacked, 0.0).astype(bf), values, (((1,), (1,)), ((), ())),
        preferred_element_type=f32,
    )
    coarse = lift.astype(bf)
    extra[z, : heads * tasks, :] = coarse
    extra[z, heads * tasks : 2 * heads * tasks, :] = (lift - coarse.astype(f32)).astype(bf)

    def parts(slab):
        return [keys.at[slab, 0], keys.at[slab, 1], extra.at[slab, pl.ds(0, 2 * heads * tasks)]]

    def upward(slab, d, j):
        piece = parts(slab)[j]
        return remote(piece, piece, up_s.at[d, j], key_r.at[slab, j], wide=z + 1)

    def downward(slab, d, j):
        piece = parts(slab)[j]
        return remote(piece, piece, down_s.at[d, j], key_r.at[slab, j], wide=z - 1)

    order = (2, 0, 1)

    @pl.when(z < nz - 1)
    def _():
        for j in order:
            upward(z, 0, j).start()

    @pl.when(z > 0)
    def _():
        for j in order:
            downward(z, 0, j).start()

    queries[...] = (
        jnp.dot(data, q_ref[...], preferred_element_type=f32) * (1.0 / math.sqrt(HD))
    ).astype(bf)
    for item in id_copies:
        item.wait_send()
    for turned in range(1, nz):
        source = turn(z, turned, nz)
        remote(id_ref, ids.at[source], id_s.at[turned], id_r.at[source], wide=source).wait_recv()

    def attend(slab, fresh):
        same = own == ids[slab].astype(f32)
        tops = []
        for h in range(heads):
            span = slice(h * HD, (h + 1) * HD)
            inside = (h * HD) % half
            affinity = lax.dot_general(
                queries[:, span],
                keys[slab, h * HD // half][:, inside : inside + HD],
                (((1,), (1,)), ((), ())),
                preferred_element_type=f32,
            )
            affinity = jnp.where(same, affinity, -1e30)
            top = jnp.max(affinity, axis=1, keepdims=True)
            powers[h] = jnp.exp(affinity - top).astype(bf)
            tops.append(top)
        for h in range(heads):
            got = lax.dot_general(
                powers[h], extra[slab], (((1,), (1,)), ((), ())),
                preferred_element_type=f32,
            )
            if fresh:
                high[h] = tops[h]
                sums[h] = got
            else:
                peak = jnp.maximum(high[h], tops[h])
                sums[h] = sums[h] * jnp.exp(high[h] - peak) + got * jnp.exp(tops[h] - peak)
                high[h] = peak

    attend(z, True)

    def step(d, carry):
        below, above = z - d, z + d

        @pl.when(below >= 0)
        def _():
            for j in order:
                piece = parts(below)[j]
                remote(piece, piece, up_s.at[0, j], key_r.at[below, j], wide=z - 1).wait_recv()

                @pl.when(z < nz - 1)
                def _():
                    upward(below, d, j).start()

        @pl.when(above < nz)
        def _():
            for j in order:
                piece = parts(above)[j]
                remote(piece, piece, down_s.at[0, j], key_r.at[above, j], wide=z + 1).wait_recv()

                @pl.when(z > 0)
                def _():
                    downward(above, d, j).start()

        attend(flip(z, d), False)
        return carry

    lax.fori_loop(1, nz, step, 0)
    columns = sums.shape[2]
    lane = lax.broadcasted_iota(jnp.int32, (rows, columns), 1)
    result = jnp.zeros((rows, columns), f32)
    for h in range(heads):
        got = sums[h]
        share_h = got / got[:, 2 * heads * tasks : 2 * heads * tasks + 1]
        mine = (lane < 2 * heads * tasks) & ((lane % (heads * tasks)) // tasks == h)
        result = jnp.where(mine, share_h, result)
    shape = (8, columns)
    pick = (
        lax.broadcasted_iota(jnp.int32, shape, 1) % tasks
        == lax.broadcasted_iota(jnp.int32, shape, 0)
    ) & (lax.broadcasted_iota(jnp.int32, shape, 1) < 2 * heads * tasks)
    partial[0] = lax.dot_general(
        pick.astype(f32), result, (((1,), (1,)), ((), ())),
        preferred_element_type=f32, precision=lax.Precision.HIGHEST,
    )
    sends = []
    for j, where in enumerate(
        ({"inner": other_c}, {"expert": other_x}, {"expert": other_x, "inner": other_c})
    ):
        item = remote(partial.at[0], partial.at[j + 1], p_s.at[j], p_r.at[j], **where)
        item.start()
        sends.append(item)
    base = lax.dot_general(
        task_ref[...], data, (((1,), (1,)), ((), ())), preferred_element_type=f32
    )
    for item in sends:
        item.wait()
    everything = (partial[0] + partial[1]) + (partial[2] + partial[3])
    out_ref[...] = everything[:tasks, :] + base
    first.wait_send()
    second.wait_send()
    third.wait_send()
    for d in range(nz - 1):
        for j in order:

            @pl.when((z < nz - 1) & (z - d >= 0))
            def _():
                upward(z, d, j).wait_send()

            @pl.when((z > 0) & (z + d < nz))
            def _():
                downward(z, d, j).wait_send()


def run_whole(
    cand, gate_weight, expert_in, expert_out, gain, query, key, value, task, attn, request_of,
    collective,
):
    nz, nx, nc = (lax.axis_size(a) for a in ALL)
    rows, depth = cand.shape
    quarters = nx * nc
    share = rows // quarters
    held, _, units = expert_in.shape
    width = expert_out.shape[1]
    tasks = task.shape[1]
    dma = pltpu.SemaphoreType.DMA
    f32, bf = jnp.float32, jnp.bfloat16
    vmem = pl.BlockSpec(memory_space=pltpu.VMEM)
    anywhere = pl.BlockSpec(memory_space=pl.ANY)
    model = tasks * width
    experts_all = gate_weight.shape[1] // tasks
    lanes = query.shape[1]
    heads = lanes // HD
    mix_scratch = [
        pltpu.VMEM((nz, quarters, share, depth), bf),
        pltpu.VMEM(expert_in.shape, bf),
        pltpu.VMEM(expert_out.shape, bf),
        pltpu.VMEM((tasks, experts_all, rows), f32),
        pltpu.VMEM((tasks * held, rows), f32),
        pltpu.VMEM((2 * TOGETHER, rows, units), bf),
        pltpu.VMEM((2 * TOGETHER, width, rows), f32),
        pltpu.VMEM((quarters, model, share), f32),
        pltpu.VMEM((nz, quarters, model, share), bf),
        pltpu.VMEM((nz, nx, model, share), bf),
        pltpu.VMEM((nz, model, share), bf),
        pltpu.VMEM((nz, model, share), bf),
        pltpu.VMEM((nz, model, share), bf),
        pltpu.VMEM((nz, model, share), bf),
        dma((3,)),
        dma((nz,)),
        dma((nz,)),
        dma((nz,)),
        dma((nz,)),
        dma((nz,)),
        dma((nz, 2)),
        dma((nz, 2)),
        dma((nz,)),
        dma((nz,)),
        dma((nz,)),
        dma((nz,)),
        dma((nz,)),
        dma((nz,)),
    ]
    columns = 2 * heads * tasks + 16
    score_scratch = [
        pltpu.VMEM((quarters, share, model), bf),
        pltpu.VMEM(query.shape, bf),
        pltpu.VMEM(key.shape, bf),
        pltpu.VMEM(value.shape, bf),
        pltpu.VMEM((nz, 2, rows, lanes // 2), bf),
        pltpu.VMEM((nz, columns, rows), bf),
        pltpu.VMEM((nz, 1, rows), jnp.int32),
        pltpu.VMEM((rows, lanes), bf),
        pltpu.VMEM((heads, rows, rows), bf),
        pltpu.VMEM((heads, rows, 1), f32),
        pltpu.VMEM((heads, rows, columns), f32),
        pltpu.VMEM((nx * nc, 8, rows), f32),
        dma((3,)),
        dma((3,)),
        dma((3,)),
        dma((nz,)),
        dma((nz,)),
        dma((nz, 3)),
        dma((nz, 3)),
        dma((nz, 3)),
        dma((3,)),
        dma((3,)),
    ]
    return pl.pallas_call(
        functools.partial(whole_kernel, tasks, len(mix_scratch)),
        in_specs=[anywhere, vmem, anywhere, anywhere, vmem, anywhere, anywhere, anywhere]
        + [vmem] * 3,
        out_specs=vmem,
        out_shape=jax.ShapeDtypeStruct((tasks, rows), f32),
        scratch_shapes=mix_scratch + score_scratch,
        compiler_params=pltpu.CompilerParams(
            collective_id=collective, has_side_effects=True, vmem_limit_bytes=VMEM_LIMIT
        ),
    )(
        cand.reshape(quarters, share, depth), gate_weight, expert_in, expert_out,
        gain.reshape(-1, 128), query, key, value, task.T, attn.T, request_of[None, :],
    ).T


def fused(sizes, rows, heads, held):
    return sizes == (4, 2, 2) and rows % 512 == 0 and heads == 4 and held % (2 * TOGETHER) == 0


def local(
    candidates,
    gate_weight,
    expert_in,
    expert_out,
    norm_gain,
    query_weight,
    key_weight,
    value_weight,
    task_weight,
    attn_weight,
    request_of,
):
    rows = candidates.shape[0]
    tasks = task_weight.shape[1]
    nz, nx, nc = (lax.axis_size(a) for a in ALL)
    if fused((nz, nx, nc), rows, query_weight.shape[1] // HD, expert_in.shape[0]):
        return run_whole(
            candidates, gate_weight, expert_in, expert_out, norm_gain, query_weight, key_weight,
            value_weight, task_weight, attn_weight, request_of, 3,
        )
    share = rows // (nx * nc)
    spot = lax.axis_index("inner") * nx + lax.axis_index("expert")
    wide = lax.axis_index("wide")
    quarter = lax.dynamic_slice_in_dim(candidates, spot * share, share, 0)
    everyone, requests = run_gather(quarter, request_of[None, :], 0)
    partial_mix = run_experts(everyone, gate_weight, expert_in, expert_out, tasks)
    normed = run_reduce(partial_mix, norm_gain[None, :], share, 1)
    normed_all = run_gather(normed, None, 2)
    own = lax.dynamic_slice_in_dim(normed_all, wide * rows, rows, 0)
    queries = jnp.dot(own, query_weight, preferred_element_type=jnp.float32).astype(jnp.bfloat16)
    keys = jnp.dot(normed_all, key_weight, preferred_element_type=jnp.float32).astype(jnp.bfloat16)
    values = jnp.dot(normed_all, value_weight, preferred_element_type=jnp.float32).astype(
        jnp.bfloat16
    )
    term = run_attention(
        queries, keys, values, request_of[:, None], requests, attn_weight
    )
    attention = lax.psum(term.T, ("expert", "inner")).T
    return jnp.dot(own, task_weight, preferred_element_type=jnp.float32) + attention


def solution(mesh):
    return jax.shard_map(
        local,
        mesh=mesh,
        in_specs=(
            P(("groups", "wide"), None),
            P(),
            P("expert", None, ("wide", "inner")),
            P("expert", None, ("wide", "inner")),
            P(),
            P(None, ("expert", "inner")),
            P(None, ("expert", "inner")),
            P(None, ("expert", "inner")),
            P(),
            P(("expert", "inner"), None),
            P(("groups", "wide")),
        ),
        out_specs=P(("groups", "wide"), None),
        check_vma=False,
    )
```

```python
import functools
import math

import jax
import jax.numpy as jnp
from jax import lax
from jax.experimental import pallas as pl
from jax.experimental.pallas import tpu as pltpu
from jax.sharding import PartitionSpec as P

HD = 64
ALL = ("wide", "expert", "inner")
VMEM_LIMIT = 60 * 1024 * 1024


MESH = pl.DeviceIdType.MESH


def place():
    return tuple(lax.axis_index(a) for a in ALL), tuple(lax.axis_size(a) for a in ALL)


def turn(start, step, size):
    return lax.rem(start + step, size)


def greet():
    mine, sizes = place()
    barrier = pltpu.get_barrier_semaphore()
    for axis, here, size in zip(ALL, mine, sizes):
        for step in range(1, size):
            pl.semaphore_signal(
                barrier, inc=1, device_id={axis: turn(here, step, size)}, device_id_type=MESH
            )
    pl.semaphore_wait(barrier, sum(sizes) - len(sizes))


def gather_kernel(with_ids, *refs):
    if with_ids:
        own_ref, id_ref, out_ref, ids_ref, recv, send_z, send_x, send_c, local_sem, id_r, id_s = refs
    else:
        own_ref, out_ref, recv, send_z, send_x, send_c, local_sem = refs
    (z, x, c), (nz, nx, nc) = place()
    greet()

    def copy(src, zs, xs, cs, sem, axis, target):
        return pltpu.make_async_remote_copy(
            src_ref=src,
            dst_ref=out_ref.at[zs, cs, xs],
            send_sem=sem,
            recv_sem=recv.at[zs, cs, xs],
            device_id={axis: target},
            device_id_type=MESH,
        )

    def arrived(zs, xs, cs):
        copy(out_ref.at[zs, cs, xs], zs, xs, cs, send_z.at[0], "inner", turn(c, 1, nc)).wait_recv()

    sent = []

    def push(*what):
        item = copy(*what)
        item.start()
        sent.append(item)

    def spread_x(src, k, zs):
        for step in range(1, nx):
            push(src, zs, x, c, send_x.at[k, step - 1], "expert", turn(x, step, nx))

    def spread_c(src, k, j, zs, xs):
        for step in range(1, nc):
            push(src, zs, xs, c, send_c.at[k, j, step - 1], "inner", turn(c, step, nc))

    for step in range(1, nz):
        push(own_ref, z, x, c, send_z.at[step - 1], "wide", turn(z, step, nz))
    spread_x(own_ref, 0, z)
    spread_c(own_ref, 0, 0, z, x)
    keep = pltpu.make_async_copy(own_ref, out_ref.at[z, c, x], local_sem.at[0])
    keep.start()
    if with_ids:
        id_copies = []
        for step in range(1, nz):
            item = pltpu.make_async_remote_copy(
                src_ref=id_ref,
                dst_ref=ids_ref.at[z],
                send_sem=id_s.at[step - 1],
                recv_sem=id_r.at[z],
                device_id={"wide": turn(z, step, nz)},
                device_id_type=MESH,
            )
            item.start()
            id_copies.append(item)
        ids_ref[z] = id_ref[...]

    def pass_x(k):
        zs = turn(z, k, nz)
        for step in range(1, nx):
            xs = turn(x, step, nx)
            arrived(zs, xs, c)
            spread_c(out_ref.at[zs, c, xs], k, step, zs, xs)

    for k in range(1, nz):
        zs = turn(z, k, nz)
        arrived(zs, x, c)
        spread_x(out_ref.at[zs, c, x], k, zs)
        spread_c(out_ref.at[zs, c, x], k, 0, zs, x)
        pass_x(k - 1)
    pass_x(nz - 1)
    for k in range(nz):
        for j in range(nx):
            for step in range(1, nc):
                arrived(turn(z, k, nz), turn(x, j, nx), turn(c, step, nc))
    for item in sent:
        item.wait_send()
    keep.wait()
    if with_ids:
        for step in range(1, nz):
            zs = turn(z, step, nz)
            pltpu.make_async_remote_copy(
                src_ref=id_ref,
                dst_ref=ids_ref.at[zs],
                send_sem=id_s.at[step - 1],
                recv_sem=id_r.at[zs],
                device_id={"wide": zs},
                device_id_type=MESH,
            ).wait_recv()
        for item in id_copies:
            item.wait_send()


def run_gather(own, ids, collective):
    nz, nx, nc = (lax.axis_size(a) for a in ALL)
    dma = pltpu.SemaphoreType.DMA
    with_ids = ids is not None
    shape = jax.ShapeDtypeStruct((nz, nc, nx) + own.shape, own.dtype)
    vmem = pl.BlockSpec(memory_space=pltpu.VMEM)
    anywhere = pl.BlockSpec(memory_space=pl.ANY)
    scratch = [
        dma((nz, nc, nx)),
        dma((max(nz - 1, 1),)),
        dma((nz, max(nx - 1, 1))),
        dma((nz, nx, max(nc - 1, 1))),
        dma((1,)),
    ]
    if with_ids:
        scratch += [dma((nz,)), dma((max(nz - 1, 1),))]
    out = pl.pallas_call(
        functools.partial(gather_kernel, with_ids),
        in_specs=[vmem, vmem] if with_ids else [vmem],
        out_specs=[anywhere, vmem] if with_ids else anywhere,
        out_shape=[shape, jax.ShapeDtypeStruct((nz,) + ids.shape, ids.dtype)] if with_ids else shape,
        scratch_shapes=scratch,
        compiler_params=pltpu.CompilerParams(collective_id=collective, has_side_effects=True),
    )(*([own, ids] if with_ids else [own]))
    depth = own.shape[1]
    if with_ids:
        return out[0].reshape(-1, depth), out[1].reshape(1, -1)
    return out.reshape(-1, depth)


def reduce_kernel(
    part_ref, gain_ref, out_ref, mine, core_in, x_out, x_in, z_out, z_in,
    local_sem, core_s, core_r, x_s, x_r, z_s, z_r,
):
    (z, x, c), (nz, nx, nc) = place()
    f32 = jnp.float32
    greet()
    other = turn(c, 1, nc)
    core, kept = [], []
    for k in range(nz):
        s = turn(z, k + 1, nz)
        item = pltpu.make_async_remote_copy(
            src_ref=part_ref.at[s, other],
            dst_ref=core_in.at[k],
            send_sem=core_s.at[k],
            recv_sem=core_r.at[k],
            device_id={"inner": other},
            device_id_type=MESH,
        )
        item.start()
        core.append(item)
        stay = pltpu.make_async_copy(part_ref.at[s, c], mine.at[k], local_sem.at[k])
        stay.start()
        kept.append(stay)

    def pair(k, xs):
        return mine[k, xs].astype(f32) + core_in[k, xs].astype(f32)

    across, along = [], []

    def finish(k):
        total = pair(k, x)
        for step in range(1, nx):
            across[k][step - 1].wait_recv()
            total = total + x_in[k, step - 1].astype(f32)
        if k == nz - 1:
            return total
        z_out[k] = total.astype(z_out.dtype)
        item = pltpu.make_async_remote_copy(
            src_ref=z_out.at[k],
            dst_ref=z_in.at[k],
            send_sem=z_s.at[k],
            recv_sem=z_r.at[k],
            device_id={"wide": turn(z, k + 1, nz)},
            device_id_type=MESH,
        )
        item.start()
        along.append(item)

    for k in range(nz):
        kept[k].wait()
        core[k].wait_recv()
        items = []
        for step in range(1, nx):
            xs = turn(x, step, nx)
            x_out[k, step - 1] = pair(k, xs).astype(x_out.dtype)
            item = pltpu.make_async_remote_copy(
                src_ref=x_out.at[k, step - 1],
                dst_ref=x_in.at[k, step - 1],
                send_sem=x_s.at[k, step - 1],
                recv_sem=x_r.at[k, step - 1],
                device_id={"expert": xs},
                device_id_type=MESH,
            )
            item.start()
            items.append(item)
        across.append(items)
        if k > 0:
            finish(k - 1)
    total = finish(nz - 1)
    for k in range(nz - 1):
        along[k].wait_recv()
        total = total + z_in[k].astype(f32)
    center = jnp.mean(total, axis=1, keepdims=True)
    spread = jnp.mean(jnp.square(total - center), axis=1, keepdims=True)
    normed = (total - center) * lax.rsqrt(spread + 1e-05) * gain_ref[...].astype(f32)
    out_ref[...] = normed.astype(out_ref.dtype)
    for item in core + along + [i for items in across for i in items]:
        item.wait_send()


def run_reduce(part, gain, share, collective):
    nz, nx, nc = (lax.axis_size(a) for a in ALL)
    width = part.shape[1]
    dma = pltpu.SemaphoreType.DMA
    kind = part.dtype
    part = part.reshape(nz, nc, nx, share, width)
    few = max(nx - 1, 1)
    vmem = pl.BlockSpec(memory_space=pltpu.VMEM)
    return pl.pallas_call(
        reduce_kernel,
        in_specs=[pl.BlockSpec(memory_space=pl.ANY), vmem],
        out_specs=vmem,
        out_shape=jax.ShapeDtypeStruct((share, width), kind),
        scratch_shapes=[
            pltpu.VMEM((nz, nx, share, width), kind),
            pltpu.VMEM((nz, nx, share, width), kind),
            pltpu.VMEM((nz, few, share, width), kind),
            pltpu.VMEM((nz, few, share, width), kind),
            pltpu.VMEM((nz, share, width), kind),
            pltpu.VMEM((nz, share, width), kind),
            dma((nz,)),
            dma((nz,)),
            dma((nz,)),
            dma((nz, few)),
            dma((nz, few)),
            dma((nz,)),
            dma((nz,)),
        ],
        compiler_params=pltpu.CompilerParams(
            collective_id=collective, has_side_effects=True, vmem_limit_bytes=VMEM_LIMIT
        ),
    )(part, gain)


def expert_kernel(tasks, x_ref, gate_ref, win_ref, wout_ref, out_ref, acc_ref):
    rows = x_ref.shape[0]
    columns = gate_ref.shape[1]
    experts_all = columns // tasks
    held, _, _ = win_ref.shape
    width = wout_ref.shape[1]
    x = x_ref[...]
    logits = jnp.dot(x, gate_ref[...], preferred_element_type=jnp.float32)
    task = lax.broadcasted_iota(jnp.int32, (rows, columns), 1) // experts_all
    top = jnp.zeros_like(logits)
    for t in range(tasks):
        high = jnp.max(jnp.where(task == t, logits, -jnp.inf), axis=1, keepdims=True)
        top = jnp.where(task == t, high, top)
    powers = jnp.exp(logits - top)
    total = jnp.ones_like(logits)
    for t in range(tasks):
        part = jnp.sum(jnp.where(task == t, powers, 0.0), axis=1, keepdims=True)
        total = jnp.where(task == t, part, total)
    gates = powers / total
    shift = lax.rem(columns - lax.axis_index("expert") * held, columns)
    gates = pltpu.roll(gates, shift, 1)
    together = min(4, held)
    for first in range(0, held, together):
        made = []
        for e in range(first, first + together):
            hidden = jnp.maximum(
                jnp.dot(x, win_ref[e], preferred_element_type=jnp.float32), 0.0
            ).astype(jnp.bfloat16)
            made.append(
                lax.dot_general(
                    hidden,
                    wout_ref[e],
                    (((1,), (1,)), ((), ())),
                    preferred_element_type=jnp.float32,
                )
            )
        for t in range(tasks):
            piece = None
            for j, output in enumerate(made):
                lane = t * experts_all + first + j
                term = gates[:, lane : lane + 1] * output
                piece = term if piece is None else piece + term
            span = slice(t * width, (t + 1) * width)
            if first > 0:
                piece = piece + acc_ref[:, span]
            if first + together < held:
                acc_ref[:, span] = piece
            else:
                out_ref[:, span] = piece.astype(out_ref.dtype)


def run_experts(x, gate_weight, expert_in, expert_out, tasks):
    rows, depth = x.shape
    held, _, units = expert_in.shape
    width = expert_out.shape[1]
    block = min(512, rows)
    return pl.pallas_call(
        functools.partial(expert_kernel, tasks),
        grid=(rows // block,),
        in_specs=[
            pl.BlockSpec((block, depth), lambda i: (i, 0)),
            pl.BlockSpec(gate_weight.shape, lambda i: (0, 0)),
            pl.BlockSpec(expert_in.shape, lambda i: (0, 0, 0), pipeline_mode=pl.Buffered(1)),
            pl.BlockSpec(expert_out.shape, lambda i: (0, 0, 0), pipeline_mode=pl.Buffered(1)),
        ],
        out_specs=pl.BlockSpec((block, tasks * width), lambda i: (i, 0)),
        out_shape=jax.ShapeDtypeStruct((rows, tasks * width), jnp.bfloat16),
        scratch_shapes=[pltpu.VMEM((block, tasks * width), jnp.float32)],
        compiler_params=pltpu.CompilerParams(vmem_limit_bytes=VMEM_LIMIT),
    )(x, gate_weight, expert_in, expert_out)


def attention_kernel(q_ref, k_ref, v_ref, own_ref, all_ref, weight_ref, out_ref):
    same = own_ref[...] == all_ref[...]
    factor = 1.0 / math.sqrt(HD)
    result = None
    for first in range(0, q_ref.shape[1], HD):
        span = slice(first, first + HD)
        affinity = (
            lax.dot_general(
                q_ref[:, span],
                k_ref[:, span],
                (((1,), (1,)), ((), ())),
                preferred_element_type=jnp.float32,
            )
            * factor
        )
        affinity = jnp.where(same, affinity, -1e30)
        highest = jnp.max(affinity, axis=1, keepdims=True)
        powers = jnp.exp(affinity - highest)
        total = jnp.sum(powers, axis=1, keepdims=True)
        context = jnp.dot(
            powers.astype(jnp.bfloat16), v_ref[:, span], preferred_element_type=jnp.float32
        )
        context = (context / total).astype(jnp.bfloat16)
        term = jnp.dot(context, weight_ref[span, :], preferred_element_type=jnp.float32)
        result = term if result is None else result + term
    out_ref[...] = result


def run_attention(q, k, v, own, every, weight):
    rows, width = q.shape
    keys = k.shape[0]
    tasks = weight.shape[1]
    block = min(128, rows)
    return pl.pallas_call(
        attention_kernel,
        grid=(rows // block,),
        in_specs=[
            pl.BlockSpec((block, width), lambda i: (i, 0)),
            pl.BlockSpec((keys, width), lambda i: (0, 0)),
            pl.BlockSpec((keys, width), lambda i: (0, 0)),
            pl.BlockSpec((block, 1), lambda i: (i, 0)),
            pl.BlockSpec((1, keys), lambda i: (0, 0)),
            pl.BlockSpec((width, tasks), lambda i: (0, 0)),
        ],
        out_specs=pl.BlockSpec((block, tasks), lambda i: (i, 0)),
        out_shape=jax.ShapeDtypeStruct((rows, tasks), jnp.float32),
        compiler_params=pltpu.CompilerParams(vmem_limit_bytes=VMEM_LIMIT),
    )(q, k, v, own, every, weight)


def flip(position, step):
    low = lax.rem(position, 2)
    high = position // 2
    return (high + (step // 2) * (1 - 2 * high)) * 2 + low + lax.rem(step, 2) * (1 - 2 * low)


def remote(src, dst, send, recv, **where):
    return pltpu.make_async_remote_copy(
        src_ref=src, dst_ref=dst, send_sem=send, recv_sem=recv, device_id=where,
        device_id_type=MESH,
    )


TOGETHER = 4


def mix_part(
    tasks, cand_ref, gate_ref, win_hbm, wout_hbm, gain_ref, nb,
    xbuf, win, wout, gates_all, gates, hidden, made, acc, part, core_in, x_out, x_in, z_out, z_in,
    load_sem, up_s, down_s, z_r, x_s, x_r, c_s, c_r, core_s, core_r, rx_s, rx_r, rz_s, rz_r,
):
    (z, x, c), (nz, nx, nc) = place()
    f32, bf = jnp.float32, jnp.bfloat16
    other_x, other_c = 1 - x, 1 - c
    held = win.shape[0]
    quarters, share, depth = xbuf.shape[1:]
    rows = quarters * share
    width = wout.shape[1]
    spot = c * nx + x
    loads = [
        pltpu.make_async_copy(cand_ref, xbuf.at[z], load_sem.at[0]),
        pltpu.make_async_copy(win_hbm, win, load_sem.at[1]),
        pltpu.make_async_copy(wout_hbm, wout, load_sem.at[2]),
    ]
    for item in loads:
        item.start()
    greet_all()

    piece_rows = share // 2
    half_model = part.shape[2] // 2

    def rows_of(h):
        return pl.ds(h * piece_rows, piece_rows)

    def features(f):
        return pl.ds(f * half_model, half_model)

    def upward(src, slab, d, h):
        return remote(
            src.at[rows_of(h)], xbuf.at[slab, spot, rows_of(h)], up_s.at[d, h], z_r.at[slab, h],
            wide=z + 1,
        )

    def downward(src, slab, d, h):
        return remote(
            src.at[rows_of(h)], xbuf.at[slab, spot, rows_of(h)], down_s.at[d, h],
            z_r.at[slab, h], wide=z - 1,
        )

    def sideways(slab, q, h):
        piece = xbuf.at[slab, q, rows_of(h)]
        return remote(piece, piece, x_s.at[slab, h], x_r.at[slab, h], expert=other_x)

    def corewise(slab, j, q):
        piece = xbuf.at[slab, q]
        return remote(piece, piece, c_s.at[slab, j], c_r.at[slab, j], inner=other_c)

    for h in range(2):

        @pl.when(z < nz - 1)
        def _():
            upward(cand_ref.at[spot], z, 0, h).start()

        @pl.when(z > 0)
        def _():
            downward(cand_ref.at[spot], z, 0, h).start()

    for item in loads:
        item.wait()

    def arrive_z(d, h):
        below, above = z - d, z + d

        @pl.when(below >= 0)
        def _():
            upward(xbuf.at[below, spot], below, 0, h).wait_recv()

            @pl.when(z < nz - 1)
            def _():
                upward(xbuf.at[below, spot], below, d, h).start()

        @pl.when(above < nz)
        def _():
            downward(xbuf.at[above, spot], above, 0, h).wait_recv()

            @pl.when(z > 0)
            def _():
                downward(xbuf.at[above, spot], above, d, h).start()

        slab = flip(z, d)
        sideways(slab, spot, h).start()
        if h == 1:
            corewise(slab, 0, spot).start()

    def arrive_x(slab):
        q = c * nx + other_x
        for h in range(2):
            sideways(slab, q, h).wait_recv()
        corewise(slab, 1, q).start()

    def arrive_c(slab):
        for j, q in ((0, other_c * nx + x), (1, other_c * nx + other_x)):
            corewise(slab, j, q).wait_recv()

    def to_core(k):
        return remote(
            part.at[k, pl.ds(other_c * nx, nx)], core_in.at[k], core_s.at[k], core_r.at[k],
            inner=other_c,
        )

    def to_x(k, f):
        return remote(
            x_out.at[k, features(f)], x_in.at[k, features(f)], rx_s.at[k, f], rx_r.at[k, f],
            expert=other_x,
        )

    def to_z(k, f):
        return remote(
            z_out.at[k, features(f)], z_in.at[k, features(f)], rz_s.at[k, f], rz_r.at[k, f],
            wide=flip(z, k),
        )

    def reduce_core(k):
        to_core(k).wait_recv()
        for f in range(2):
            x_out[k, features(f)] = (
                part[k, c * nx + other_x, features(f)].astype(f32)
                + core_in[k, other_x, features(f)].astype(f32)
            ).astype(bf)
            to_x(k, f).start()

    def total_of(k, f):
        return (
            part[k, c * nx + x, features(f)].astype(f32)
            + core_in[k, x, features(f)].astype(f32)
            + x_in[k, features(f)].astype(f32)
        )

    def reduce_x(k, f):
        to_x(k, f).wait_recv()
        z_out[k, features(f)] = total_of(k, f).astype(bf)
        to_z(k, f).start()

    groups = held // TOGETHER

    def gating(i, k):
        side = (i % 2) * TOGETHER
        for q in range(quarters):
            lanes = slice(q * share, (q + 1) * share)
            weights = [
                [
                    gates[t * held + i * TOGETHER + j : t * held + i * TOGETHER + j + 1, lanes]
                    for j in range(TOGETHER)
                ]
                for t in range(tasks)
            ]
            for f in range(0, width, 16):
                outs = [made[side + j, f : f + 16, lanes] for j in range(TOGETHER)]
                for t in range(tasks):
                    span = slice(t * width + f, t * width + f + 16)
                    piece = weights[t][0] * outs[0]
                    for j in range(1, TOGETHER):
                        piece = piece + weights[t][j] * outs[j]
                    if i > 0:
                        piece = piece + acc[q, span, :]
                    if i < groups - 1:
                        acc[q, span, :] = piece
                    else:
                        part[k, q, span, :] = piece.astype(bf)

    def stage(i, data, k):
        if i < groups:
            for j in range(TOGETHER):
                e = i * TOGETHER + j
                hidden[(i % 2) * TOGETHER + j] = jnp.maximum(
                    jnp.dot(data, win[e], preferred_element_type=f32), 0.0
                ).astype(bf)
        if 0 < i <= groups:
            side = ((i - 1) % 2) * TOGETHER
            for j in range(TOGETHER):
                e = (i - 1) * TOGETHER + j
                made[side + j] = lax.dot_general(
                    wout[e], hidden[side + j], (((1,), (1,)), ((), ())),
                    preferred_element_type=f32,
                )
        if i > 1:
            gating(i - 2, k)

    agenda = (
        (0, 0, lambda: arrive_z(1, 0)),
        (0, 2, lambda: arrive_z(1, 1)),
        (0, 4, lambda: arrive_z(2, 0)),
        (1, 2, lambda: arrive_z(3, 0)),
        (1, 4, lambda: arrive_z(3, 1)),
        (1, 5, lambda: reduce_core(0)),
        (2, 1, lambda: reduce_core(1)),
        (3, 1, lambda: reduce_core(2)),
        (3, 2, lambda: reduce_x(1, 0)),
        (3, 3, lambda: reduce_x(1, 1)),
        (3, 5, lambda: reduce_x(2, 0)),
    )

    def step(k, carry):
        slab = flip(z, k)
        data = xbuf[slab].reshape(rows, depth)
        logits = lax.dot_general(
            gate_ref[...], data, (((0,), (1,)), ((), ())), preferred_element_type=f32
        )
        logits = logits.reshape(tasks, logits.shape[0] // tasks, rows)
        powers = jnp.exp(logits - jnp.max(logits, axis=1, keepdims=True))
        gates_all[...] = powers / jnp.sum(powers, axis=1, keepdims=True)
        for t in range(tasks):
            gates[t * held : (t + 1) * held, :] = gates_all[
                t, pl.ds(pl.multiple_of(x * held, held), held), :
            ]
        after = flip(z, k + 1)
        for i in range(groups + 2):
            for moment, boundary, action in agenda:
                if boundary == i:
                    pl.when(k == moment)(action)
            if i > 0:
                data = xbuf[slab].reshape(rows, depth)
            stage(i, data, k)
        to_core(k).start()

        @pl.when(k == 0)
        def _():
            arrive_z(2, 1)

        @pl.when(k < nz - 1)
        def _():
            arrive_x(after)
            arrive_c(after)

        return carry

    lax.fori_loop(0, nz, step, 0)
    reduce_x(2, 1)
    reduce_core(3)
    for f in range(2):
        reduce_x(3, f)
    totals = []
    for f in range(2):
        to_x(0, f).wait_recv()
        total = total_of(0, f)
        for k in range(1, nz):
            to_z(k, f).wait_recv()
            total = total + z_in[k, features(f)].astype(f32)
        totals.append(total)
    total = jnp.concatenate(totals, axis=0)
    total = total.T
    center = jnp.mean(total, axis=1, keepdims=True)
    spread = jnp.mean(jnp.square(total - center), axis=1, keepdims=True)
    gain = gain_ref[...].astype(f32)
    gain = jnp.concatenate([gain[i : i + 1, :] for i in range(gain.shape[0])], axis=1)
    normed = (total - center) * lax.rsqrt(spread + 1e-05) * gain
    nb[spot] = normed.astype(bf)
    yield
    for d in range(nz - 1):
        for h in range(2):

            @pl.when((z < nz - 1) & (z - d >= 0))
            def _():
                upward(xbuf.at[z, spot], z, d, h).wait_send()

            @pl.when((z > 0) & (z + d < nz))
            def _():
                downward(xbuf.at[z, spot], z, d, h).wait_send()

    for k in range(1, nz):
        slab = flip(z, k)
        corewise(slab, 0, spot).wait_send()
        corewise(slab, 1, spot).wait_send()
        for h in range(2):
            sideways(slab, spot, h).wait_send()
            to_z(k, h).wait_send()
    for k in range(nz):
        to_core(k).wait_send()
        for f in range(2):
            to_x(k, f).wait_send()


def greet_all():
    (z, x, c), (nz, nx, nc) = place()
    barrier = pltpu.get_barrier_semaphore()
    pl.semaphore_signal(
        barrier, inc=1, device_id={"expert": 1 - x, "inner": 1 - c}, device_id_type=MESH
    )
    for axis, here, size in zip(ALL, (z, x, c), (nz, nx, nc)):
        for turned in range(1, size):
            pl.semaphore_signal(
                barrier, inc=1, device_id={axis: turn(here, turned, size)}, device_id_type=MESH
            )
    pl.semaphore_wait(barrier, nz + nx + nc - 2)


def whole_kernel(
    tasks, mix_count, cand_ref, gate_ref, win_hbm, wout_hbm, gain_ref,
    q_hbm, k_hbm, v_hbm, task_ref, attn_ref, id_ref, out_ref, *scratch
):
    nb = scratch[mix_count]
    mix = mix_part(
        tasks, cand_ref, gate_ref, win_hbm, wout_hbm, gain_ref, nb, *scratch[:mix_count]
    )
    score = score_part(
        q_hbm, k_hbm, v_hbm, task_ref, attn_ref, id_ref, out_ref, *scratch[mix_count:]
    )
    next(score)
    next(mix)
    next(score, None)
    next(mix, None)


def score_part(
    q_hbm, k_hbm, v_hbm, task_ref, attn_ref, id_ref, out_ref,
    nb, q_ref, k_ref, v_ref, keys, extra, ids, queries, powers, high, sums, partial,
    load_sem, n_s, n_r, id_s, id_r, up_s, down_s, key_r, p_s, p_r,
):
    (z, x, c), (nz, nx, nc) = place()
    f32, bf = jnp.float32, jnp.bfloat16
    other_x, other_c = 1 - x, 1 - c
    spot = c * nx + x
    quarters, share, depth = nb.shape
    rows = quarters * share
    heads = queries.shape[1] // HD
    tasks = task_ref.shape[0]
    loads = [
        pltpu.make_async_copy(k_hbm, k_ref, load_sem.at[0]),
        pltpu.make_async_copy(v_hbm, v_ref, load_sem.at[1]),
        pltpu.make_async_copy(q_hbm, q_ref, load_sem.at[2]),
    ]
    for item in loads:
        item.start()
    yield

    def give(q, j, **where):
        return remote(nb.at[q], nb.at[q], n_s.at[j], n_r.at[j], **where)

    first = give(spot, 0, expert=other_x)
    second = give(spot, 1, inner=other_c)
    first.start()
    second.start()
    id_copies = []
    for turned in range(1, nz):
        target = turn(z, turned, nz)
        item = remote(id_ref, ids.at[z], id_s.at[turned], id_r.at[z], wide=target)
        item.start()
        id_copies.append(item)
    ids[z] = id_ref[...]
    for item in loads:
        item.wait()
    own = jnp.broadcast_to(id_ref[...].astype(f32), (8, rows)).T[:, :1]
    extra[:, 2 * heads * tasks :, :] = jnp.ones((nz, 16, rows), bf)
    across = c * nx + other_x
    give(across, 0, expert=other_x).wait_recv()
    third = give(across, 2, inner=other_c)
    third.start()
    give(other_c * nx + x, 1, inner=other_c).wait_recv()
    give(other_c * nx + other_x, 2, inner=other_c).wait_recv()
    data = nb[...].reshape(rows, depth)
    half = heads // 2 * HD

    def parts(slab):
        return [keys.at[slab, 0], keys.at[slab, 1], extra.at[slab, pl.ds(0, 2 * heads * tasks)]]

    def upward(slab, d, j):
        piece = parts(slab)[j]
        return remote(piece, piece, up_s.at[d, j], key_r.at[slab, j], wide=z + 1)

    def downward(slab, d, j):
        piece = parts(slab)[j]
        return remote(piece, piece, down_s.at[d, j], key_r.at[slab, j], wide=z - 1)

    order = (0, 1, 2)

    def announce(j):
        @pl.when(z < nz - 1)
        def _():
            upward(z, 0, j).start()

        @pl.when(z > 0)
        def _():
            downward(z, 0, j).start()

    for j in range(2):
        keys[z, j] = jnp.dot(
            data, k_ref[:, j * half : (j + 1) * half], preferred_element_type=f32
        ).astype(bf)
        announce(j)
    values = jnp.dot(data, v_ref[...], preferred_element_type=f32).astype(bf)
    shape = (heads * tasks, heads * HD)
    row = lax.broadcasted_iota(jnp.int32, shape, 0) // tasks
    column = lax.broadcasted_iota(jnp.int32, shape, 1) // HD
    stacked = jnp.concatenate([attn_ref[...].astype(f32)] * heads, axis=0)
    lift = lax.dot_general(
        jnp.where(row == column, stacked, 0.0).astype(bf), values, (((1,), (1,)), ((), ())),
        preferred_element_type=f32,
    )
    coarse = lift.astype(bf)
    extra[z, : heads * tasks, :] = coarse
    extra[z, heads * tasks : 2 * heads * tasks, :] = (lift - coarse.astype(f32)).astype(bf)

    announce(2)
    queries[...] = (
        jnp.dot(data, q_ref[...], preferred_element_type=f32) * (1.0 / math.sqrt(HD))
    ).astype(bf)
    for item in id_copies:
        item.wait_send()
    for turned in range(1, nz):
        source = turn(z, turned, nz)
        remote(id_ref, ids.at[source], id_s.at[turned], id_r.at[source], wide=source).wait_recv()

    per = heads // 2

    def compare(slab, j):
        same = own == ids[slab].astype(f32)
        tops = []
        for i in range(per):
            h = j * per + i
            affinity = lax.dot_general(
                queries[:, h * HD : (h + 1) * HD],
                keys[slab, j][:, i * HD : (i + 1) * HD],
                (((1,), (1,)), ((), ())),
                preferred_element_type=f32,
            )
            affinity = jnp.where(same, affinity, -1e30)
            top = jnp.max(affinity, axis=1, keepdims=True)
            powers[h] = jnp.exp(affinity - top).astype(bf)
            tops.append(top)
        return tops

    def combine(slab, tops, fresh):
        for h in range(heads):
            got = lax.dot_general(
                powers[h], extra[slab], (((1,), (1,)), ((), ())), preferred_element_type=f32
            )
            if fresh:
                high[h] = tops[h]
                sums[h] = got
            else:
                peak = jnp.maximum(high[h], tops[h])
                sums[h] = sums[h] * jnp.exp(high[h] - peak) + got * jnp.exp(tops[h] - peak)
                high[h] = peak

    def pass_on(d, j):
        below, above = z - d, z + d

        @pl.when(below >= 0)
        def _():
            upward(below, 0, j).wait_recv()

            @pl.when(z < nz - 1)
            def _():
                upward(below, d, j).start()

        @pl.when(above < nz)
        def _():
            downward(above, 0, j).wait_recv()

            @pl.when(z > 0)
            def _():
                downward(above, d, j).start()

    combine(z, compare(z, 0) + compare(z, 1), True)

    def step(d, carry):
        slab = flip(z, d)
        pass_on(d, 0)
        tops = compare(slab, 0)
        pass_on(d, 1)
        tops = tops + compare(slab, 1)
        pass_on(d, 2)
        combine(slab, tops, False)
        return carry

    lax.fori_loop(1, nz, step, 0)
    columns = sums.shape[2]
    lane = lax.broadcasted_iota(jnp.int32, (rows, columns), 1)
    result = jnp.zeros((rows, columns), f32)
    for h in range(heads):
        got = sums[h]
        share_h = got / got[:, 2 * heads * tasks : 2 * heads * tasks + 1]
        mine = (lane < 2 * heads * tasks) & ((lane % (heads * tasks)) // tasks == h)
        result = jnp.where(mine, share_h, result)
    shape = (8, columns)
    pick = (
        lax.broadcasted_iota(jnp.int32, shape, 1) % tasks
        == lax.broadcasted_iota(jnp.int32, shape, 0)
    ) & (lax.broadcasted_iota(jnp.int32, shape, 1) < 2 * heads * tasks)
    partial[0] = lax.dot_general(
        pick.astype(f32), result, (((1,), (1,)), ((), ())),
        preferred_element_type=f32, precision=lax.Precision.HIGHEST,
    )
    sends = []
    for j, where in enumerate(
        ({"inner": other_c}, {"expert": other_x}, {"expert": other_x, "inner": other_c})
    ):
        item = remote(partial.at[0], partial.at[j + 1], p_s.at[j], p_r.at[j], **where)
        item.start()
        sends.append(item)
    base = lax.dot_general(
        task_ref[...], data, (((1,), (1,)), ((), ())), preferred_element_type=f32
    )
    for item in sends:
        item.wait()
    everything = (partial[0] + partial[1]) + (partial[2] + partial[3])
    out_ref[...] = everything[:tasks, :] + base
    first.wait_send()
    second.wait_send()
    third.wait_send()
    for d in range(nz - 1):
        for j in order:

            @pl.when((z < nz - 1) & (z - d >= 0))
            def _():
                upward(z, d, j).wait_send()

            @pl.when((z > 0) & (z + d < nz))
            def _():
                downward(z, d, j).wait_send()


def run_whole(
    cand, gate_weight, expert_in, expert_out, gain, query, key, value, task, attn, request_of,
    collective,
):
    nz, nx, nc = (lax.axis_size(a) for a in ALL)
    rows, depth = cand.shape
    quarters = nx * nc
    share = rows // quarters
    held, _, units = expert_in.shape
    width = expert_out.shape[1]
    tasks = task.shape[1]
    dma = pltpu.SemaphoreType.DMA
    f32, bf = jnp.float32, jnp.bfloat16
    vmem = pl.BlockSpec(memory_space=pltpu.VMEM)
    anywhere = pl.BlockSpec(memory_space=pl.ANY)
    model = tasks * width
    experts_all = gate_weight.shape[1] // tasks
    lanes = query.shape[1]
    heads = lanes // HD
    mix_scratch = [
        pltpu.VMEM((nz, quarters, share, depth), bf),
        pltpu.VMEM(expert_in.shape, bf),
        pltpu.VMEM(expert_out.shape, bf),
        pltpu.VMEM((tasks, experts_all, rows), f32),
        pltpu.VMEM((tasks * held, rows), f32),
        pltpu.VMEM((2 * TOGETHER, rows, units), bf),
        pltpu.VMEM((2 * TOGETHER, width, rows), f32),
        pltpu.VMEM((quarters, model, share), f32),
        pltpu.VMEM((nz, quarters, model, share), bf),
        pltpu.VMEM((nz, nx, model, share), bf),
        pltpu.VMEM((nz, model, share), bf),
        pltpu.VMEM((nz, model, share), bf),
        pltpu.VMEM((nz, model, share), bf),
        pltpu.VMEM((nz, model, share), bf),
        dma((3,)),
        dma((nz, 2)),
        dma((nz, 2)),
        dma((nz, 2)),
        dma((nz, 2)),
        dma((nz, 2)),
        dma((nz, 2)),
        dma((nz, 2)),
        dma((nz,)),
        dma((nz,)),
        dma((nz, 2)),
        dma((nz, 2)),
        dma((nz, 2)),
        dma((nz, 2)),
    ]
    columns = 2 * heads * tasks + 16
    score_scratch = [
        pltpu.VMEM((quarters, share, model), bf),
        pltpu.VMEM(query.shape, bf),
        pltpu.VMEM(key.shape, bf),
        pltpu.VMEM(value.shape, bf),
        pltpu.VMEM((nz, 2, rows, lanes // 2), bf),
        pltpu.VMEM((nz, columns, rows), bf),
        pltpu.VMEM((nz, 1, rows), jnp.int32),
        pltpu.VMEM((rows, lanes), bf),
        pltpu.VMEM((heads, rows, rows), bf),
        pltpu.VMEM((heads, rows, 1), f32),
        pltpu.VMEM((heads, rows, columns), f32),
        pltpu.VMEM((nx * nc, 8, rows), f32),
        dma((3,)),
        dma((3,)),
        dma((3,)),
        dma((nz,)),
        dma((nz,)),
        dma((nz, 3)),
        dma((nz, 3)),
        dma((nz, 3)),
        dma((3,)),
        dma((3,)),
    ]
    return pl.pallas_call(
        functools.partial(whole_kernel, tasks, len(mix_scratch)),
        in_specs=[anywhere, vmem, anywhere, anywhere, vmem, anywhere, anywhere, anywhere]
        + [vmem] * 3,
        out_specs=vmem,
        out_shape=jax.ShapeDtypeStruct((tasks, rows), f32),
        scratch_shapes=mix_scratch + score_scratch,
        compiler_params=pltpu.CompilerParams(
            collective_id=collective, has_side_effects=True, vmem_limit_bytes=VMEM_LIMIT
        ),
    )(
        cand.reshape(quarters, share, depth), gate_weight, expert_in, expert_out,
        gain.reshape(-1, 128), query, key, value, task.T, attn.T, request_of[None, :],
    ).T


def fused(sizes, rows, heads, held):
    return sizes == (4, 2, 2) and rows % 512 == 0 and heads == 4 and held % (2 * TOGETHER) == 0


def local(
    candidates,
    gate_weight,
    expert_in,
    expert_out,
    norm_gain,
    query_weight,
    key_weight,
    value_weight,
    task_weight,
    attn_weight,
    request_of,
):
    rows = candidates.shape[0]
    tasks = task_weight.shape[1]
    nz, nx, nc = (lax.axis_size(a) for a in ALL)
    if fused((nz, nx, nc), rows, query_weight.shape[1] // HD, expert_in.shape[0]):
        return run_whole(
            candidates, gate_weight, expert_in, expert_out, norm_gain, query_weight, key_weight,
            value_weight, task_weight, attn_weight, request_of, 3,
        )
    share = rows // (nx * nc)
    spot = lax.axis_index("inner") * nx + lax.axis_index("expert")
    wide = lax.axis_index("wide")
    quarter = lax.dynamic_slice_in_dim(candidates, spot * share, share, 0)
    everyone, requests = run_gather(quarter, request_of[None, :], 0)
    partial_mix = run_experts(everyone, gate_weight, expert_in, expert_out, tasks)
    normed = run_reduce(partial_mix, norm_gain[None, :], share, 1)
    normed_all = run_gather(normed, None, 2)
    own = lax.dynamic_slice_in_dim(normed_all, wide * rows, rows, 0)
    queries = jnp.dot(own, query_weight, preferred_element_type=jnp.float32).astype(jnp.bfloat16)
    keys = jnp.dot(normed_all, key_weight, preferred_element_type=jnp.float32).astype(jnp.bfloat16)
    values = jnp.dot(normed_all, value_weight, preferred_element_type=jnp.float32).astype(
        jnp.bfloat16
    )
    term = run_attention(
        queries, keys, values, request_of[:, None], requests, attn_weight
    )
    attention = lax.psum(term.T, ("expert", "inner")).T
    return jnp.dot(own, task_weight, preferred_element_type=jnp.float32) + attention


def solution(mesh):
    return jax.shard_map(
        local,
        mesh=mesh,
        in_specs=(
            P(("groups", "wide"), None),
            P(),
            P("expert", None, ("wide", "inner")),
            P("expert", None, ("wide", "inner")),
            P(),
            P(None, ("expert", "inner")),
            P(None, ("expert", "inner")),
            P(None, ("expert", "inner")),
            P(),
            P(("expert", "inner"), None),
            P(("groups", "wide")),
        ),
        out_specs=P(("groups", "wide"), None),
        check_vma=False,
    )
```

```python
import functools
import math

import jax
import jax.numpy as jnp
from jax import lax
from jax.experimental import pallas as pl
from jax.experimental.pallas import tpu as pltpu
from jax.sharding import PartitionSpec as P

HD = 64
ALL = ("wide", "expert", "inner")
VMEM_LIMIT = 60 * 1024 * 1024


MESH = pl.DeviceIdType.MESH


def place():
    return tuple(lax.axis_index(a) for a in ALL), tuple(lax.axis_size(a) for a in ALL)


def turn(start, step, size):
    return lax.rem(start + step, size)


def greet():
    mine, sizes = place()
    barrier = pltpu.get_barrier_semaphore()
    for axis, here, size in zip(ALL, mine, sizes):
        for step in range(1, size):
            pl.semaphore_signal(
                barrier, inc=1, device_id={axis: turn(here, step, size)}, device_id_type=MESH
            )
    pl.semaphore_wait(barrier, sum(sizes) - len(sizes))


def gather_kernel(with_ids, *refs):
    if with_ids:
        own_ref, id_ref, out_ref, ids_ref, recv, send_z, send_x, send_c, local_sem, id_r, id_s = refs
    else:
        own_ref, out_ref, recv, send_z, send_x, send_c, local_sem = refs
    (z, x, c), (nz, nx, nc) = place()
    greet()

    def copy(src, zs, xs, cs, sem, axis, target):
        return pltpu.make_async_remote_copy(
            src_ref=src,
            dst_ref=out_ref.at[zs, cs, xs],
            send_sem=sem,
            recv_sem=recv.at[zs, cs, xs],
            device_id={axis: target},
            device_id_type=MESH,
        )

    def arrived(zs, xs, cs):
        copy(out_ref.at[zs, cs, xs], zs, xs, cs, send_z.at[0], "inner", turn(c, 1, nc)).wait_recv()

    sent = []

    def push(*what):
        item = copy(*what)
        item.start()
        sent.append(item)

    def spread_x(src, k, zs):
        for step in range(1, nx):
            push(src, zs, x, c, send_x.at[k, step - 1], "expert", turn(x, step, nx))

    def spread_c(src, k, j, zs, xs):
        for step in range(1, nc):
            push(src, zs, xs, c, send_c.at[k, j, step - 1], "inner", turn(c, step, nc))

    for step in range(1, nz):
        push(own_ref, z, x, c, send_z.at[step - 1], "wide", turn(z, step, nz))
    spread_x(own_ref, 0, z)
    spread_c(own_ref, 0, 0, z, x)
    keep = pltpu.make_async_copy(own_ref, out_ref.at[z, c, x], local_sem.at[0])
    keep.start()
    if with_ids:
        id_copies = []
        for step in range(1, nz):
            item = pltpu.make_async_remote_copy(
                src_ref=id_ref,
                dst_ref=ids_ref.at[z],
                send_sem=id_s.at[step - 1],
                recv_sem=id_r.at[z],
                device_id={"wide": turn(z, step, nz)},
                device_id_type=MESH,
            )
            item.start()
            id_copies.append(item)
        ids_ref[z] = id_ref[...]

    def pass_x(k):
        zs = turn(z, k, nz)
        for step in range(1, nx):
            xs = turn(x, step, nx)
            arrived(zs, xs, c)
            spread_c(out_ref.at[zs, c, xs], k, step, zs, xs)

    for k in range(1, nz):
        zs = turn(z, k, nz)
        arrived(zs, x, c)
        spread_x(out_ref.at[zs, c, x], k, zs)
        spread_c(out_ref.at[zs, c, x], k, 0, zs, x)
        pass_x(k - 1)
    pass_x(nz - 1)
    for k in range(nz):
        for j in range(nx):
            for step in range(1, nc):
                arrived(turn(z, k, nz), turn(x, j, nx), turn(c, step, nc))
    for item in sent:
        item.wait_send()
    keep.wait()
    if with_ids:
        for step in range(1, nz):
            zs = turn(z, step, nz)
            pltpu.make_async_remote_copy(
                src_ref=id_ref,
                dst_ref=ids_ref.at[zs],
                send_sem=id_s.at[step - 1],
                recv_sem=id_r.at[zs],
                device_id={"wide": zs},
                device_id_type=MESH,
            ).wait_recv()
        for item in id_copies:
            item.wait_send()


def run_gather(own, ids, collective):
    nz, nx, nc = (lax.axis_size(a) for a in ALL)
    dma = pltpu.SemaphoreType.DMA
    with_ids = ids is not None
    shape = jax.ShapeDtypeStruct((nz, nc, nx) + own.shape, own.dtype)
    vmem = pl.BlockSpec(memory_space=pltpu.VMEM)
    anywhere = pl.BlockSpec(memory_space=pl.ANY)
    scratch = [
        dma((nz, nc, nx)),
        dma((max(nz - 1, 1),)),
        dma((nz, max(nx - 1, 1))),
        dma((nz, nx, max(nc - 1, 1))),
        dma((1,)),
    ]
    if with_ids:
        scratch += [dma((nz,)), dma((max(nz - 1, 1),))]
    out = pl.pallas_call(
        functools.partial(gather_kernel, with_ids),
        in_specs=[vmem, vmem] if with_ids else [vmem],
        out_specs=[anywhere, vmem] if with_ids else anywhere,
        out_shape=[shape, jax.ShapeDtypeStruct((nz,) + ids.shape, ids.dtype)] if with_ids else shape,
        scratch_shapes=scratch,
        compiler_params=pltpu.CompilerParams(collective_id=collective, has_side_effects=True),
    )(*([own, ids] if with_ids else [own]))
    depth = own.shape[1]
    if with_ids:
        return out[0].reshape(-1, depth), out[1].reshape(1, -1)
    return out.reshape(-1, depth)


def reduce_kernel(
    part_ref, gain_ref, out_ref, mine, core_in, x_out, x_in, z_out, z_in,
    local_sem, core_s, core_r, x_s, x_r, z_s, z_r,
):
    (z, x, c), (nz, nx, nc) = place()
    f32 = jnp.float32
    greet()
    other = turn(c, 1, nc)
    core, kept = [], []
    for k in range(nz):
        s = turn(z, k + 1, nz)
        item = pltpu.make_async_remote_copy(
            src_ref=part_ref.at[s, other],
            dst_ref=core_in.at[k],
            send_sem=core_s.at[k],
            recv_sem=core_r.at[k],
            device_id={"inner": other},
            device_id_type=MESH,
        )
        item.start()
        core.append(item)
        stay = pltpu.make_async_copy(part_ref.at[s, c], mine.at[k], local_sem.at[k])
        stay.start()
        kept.append(stay)

    def pair(k, xs):
        return mine[k, xs].astype(f32) + core_in[k, xs].astype(f32)

    across, along = [], []

    def finish(k):
        total = pair(k, x)
        for step in range(1, nx):
            across[k][step - 1].wait_recv()
            total = total + x_in[k, step - 1].astype(f32)
        if k == nz - 1:
            return total
        z_out[k] = total.astype(z_out.dtype)
        item = pltpu.make_async_remote_copy(
            src_ref=z_out.at[k],
            dst_ref=z_in.at[k],
            send_sem=z_s.at[k],
            recv_sem=z_r.at[k],
            device_id={"wide": turn(z, k + 1, nz)},
            device_id_type=MESH,
        )
        item.start()
        along.append(item)

    for k in range(nz):
        kept[k].wait()
        core[k].wait_recv()
        items = []
        for step in range(1, nx):
            xs = turn(x, step, nx)
            x_out[k, step - 1] = pair(k, xs).astype(x_out.dtype)
            item = pltpu.make_async_remote_copy(
                src_ref=x_out.at[k, step - 1],
                dst_ref=x_in.at[k, step - 1],
                send_sem=x_s.at[k, step - 1],
                recv_sem=x_r.at[k, step - 1],
                device_id={"expert": xs},
                device_id_type=MESH,
            )
            item.start()
            items.append(item)
        across.append(items)
        if k > 0:
            finish(k - 1)
    total = finish(nz - 1)
    for k in range(nz - 1):
        along[k].wait_recv()
        total = total + z_in[k].astype(f32)
    center = jnp.mean(total, axis=1, keepdims=True)
    spread = jnp.mean(jnp.square(total - center), axis=1, keepdims=True)
    normed = (total - center) * lax.rsqrt(spread + 1e-05) * gain_ref[...].astype(f32)
    out_ref[...] = normed.astype(out_ref.dtype)
    for item in core + along + [i for items in across for i in items]:
        item.wait_send()


def run_reduce(part, gain, share, collective):
    nz, nx, nc = (lax.axis_size(a) for a in ALL)
    width = part.shape[1]
    dma = pltpu.SemaphoreType.DMA
    kind = part.dtype
    part = part.reshape(nz, nc, nx, share, width)
    few = max(nx - 1, 1)
    vmem = pl.BlockSpec(memory_space=pltpu.VMEM)
    return pl.pallas_call(
        reduce_kernel,
        in_specs=[pl.BlockSpec(memory_space=pl.ANY), vmem],
        out_specs=vmem,
        out_shape=jax.ShapeDtypeStruct((share, width), kind),
        scratch_shapes=[
            pltpu.VMEM((nz, nx, share, width), kind),
            pltpu.VMEM((nz, nx, share, width), kind),
            pltpu.VMEM((nz, few, share, width), kind),
            pltpu.VMEM((nz, few, share, width), kind),
            pltpu.VMEM((nz, share, width), kind),
            pltpu.VMEM((nz, share, width), kind),
            dma((nz,)),
            dma((nz,)),
            dma((nz,)),
            dma((nz, few)),
            dma((nz, few)),
            dma((nz,)),
            dma((nz,)),
        ],
        compiler_params=pltpu.CompilerParams(
            collective_id=collective, has_side_effects=True, vmem_limit_bytes=VMEM_LIMIT
        ),
    )(part, gain)


def expert_kernel(tasks, x_ref, gate_ref, win_ref, wout_ref, out_ref, acc_ref):
    rows = x_ref.shape[0]
    columns = gate_ref.shape[1]
    experts_all = columns // tasks
    held, _, _ = win_ref.shape
    width = wout_ref.shape[1]
    x = x_ref[...]
    logits = jnp.dot(x, gate_ref[...], preferred_element_type=jnp.float32)
    task = lax.broadcasted_iota(jnp.int32, (rows, columns), 1) // experts_all
    top = jnp.zeros_like(logits)
    for t in range(tasks):
        high = jnp.max(jnp.where(task == t, logits, -jnp.inf), axis=1, keepdims=True)
        top = jnp.where(task == t, high, top)
    powers = jnp.exp(logits - top)
    total = jnp.ones_like(logits)
    for t in range(tasks):
        part = jnp.sum(jnp.where(task == t, powers, 0.0), axis=1, keepdims=True)
        total = jnp.where(task == t, part, total)
    gates = powers / total
    shift = lax.rem(columns - lax.axis_index("expert") * held, columns)
    gates = pltpu.roll(gates, shift, 1)
    together = min(4, held)
    for first in range(0, held, together):
        made = []
        for e in range(first, first + together):
            hidden = jnp.maximum(
                jnp.dot(x, win_ref[e], preferred_element_type=jnp.float32), 0.0
            ).astype(jnp.bfloat16)
            made.append(
                lax.dot_general(
                    hidden,
                    wout_ref[e],
                    (((1,), (1,)), ((), ())),
                    preferred_element_type=jnp.float32,
                )
            )
        for t in range(tasks):
            piece = None
            for j, output in enumerate(made):
                lane = t * experts_all + first + j
                term = gates[:, lane : lane + 1] * output
                piece = term if piece is None else piece + term
            span = slice(t * width, (t + 1) * width)
            if first > 0:
                piece = piece + acc_ref[:, span]
            if first + together < held:
                acc_ref[:, span] = piece
            else:
                out_ref[:, span] = piece.astype(out_ref.dtype)


def run_experts(x, gate_weight, expert_in, expert_out, tasks):
    rows, depth = x.shape
    held, _, units = expert_in.shape
    width = expert_out.shape[1]
    block = min(512, rows)
    return pl.pallas_call(
        functools.partial(expert_kernel, tasks),
        grid=(rows // block,),
        in_specs=[
            pl.BlockSpec((block, depth), lambda i: (i, 0)),
            pl.BlockSpec(gate_weight.shape, lambda i: (0, 0)),
            pl.BlockSpec(expert_in.shape, lambda i: (0, 0, 0), pipeline_mode=pl.Buffered(1)),
            pl.BlockSpec(expert_out.shape, lambda i: (0, 0, 0), pipeline_mode=pl.Buffered(1)),
        ],
        out_specs=pl.BlockSpec((block, tasks * width), lambda i: (i, 0)),
        out_shape=jax.ShapeDtypeStruct((rows, tasks * width), jnp.bfloat16),
        scratch_shapes=[pltpu.VMEM((block, tasks * width), jnp.float32)],
        compiler_params=pltpu.CompilerParams(vmem_limit_bytes=VMEM_LIMIT),
    )(x, gate_weight, expert_in, expert_out)


def attention_kernel(q_ref, k_ref, v_ref, own_ref, all_ref, weight_ref, out_ref):
    same = own_ref[...] == all_ref[...]
    factor = 1.0 / math.sqrt(HD)
    result = None
    for first in range(0, q_ref.shape[1], HD):
        span = slice(first, first + HD)
        affinity = (
            lax.dot_general(
                q_ref[:, span],
                k_ref[:, span],
                (((1,), (1,)), ((), ())),
                preferred_element_type=jnp.float32,
            )
            * factor
        )
        affinity = jnp.where(same, affinity, -1e30)
        highest = jnp.max(affinity, axis=1, keepdims=True)
        powers = jnp.exp(affinity - highest)
        total = jnp.sum(powers, axis=1, keepdims=True)
        context = jnp.dot(
            powers.astype(jnp.bfloat16), v_ref[:, span], preferred_element_type=jnp.float32
        )
        context = (context / total).astype(jnp.bfloat16)
        term = jnp.dot(context, weight_ref[span, :], preferred_element_type=jnp.float32)
        result = term if result is None else result + term
    out_ref[...] = result


def run_attention(q, k, v, own, every, weight):
    rows, width = q.shape
    keys = k.shape[0]
    tasks = weight.shape[1]
    block = min(128, rows)
    return pl.pallas_call(
        attention_kernel,
        grid=(rows // block,),
        in_specs=[
            pl.BlockSpec((block, width), lambda i: (i, 0)),
            pl.BlockSpec((keys, width), lambda i: (0, 0)),
            pl.BlockSpec((keys, width), lambda i: (0, 0)),
            pl.BlockSpec((block, 1), lambda i: (i, 0)),
            pl.BlockSpec((1, keys), lambda i: (0, 0)),
            pl.BlockSpec((width, tasks), lambda i: (0, 0)),
        ],
        out_specs=pl.BlockSpec((block, tasks), lambda i: (i, 0)),
        out_shape=jax.ShapeDtypeStruct((rows, tasks), jnp.float32),
        compiler_params=pltpu.CompilerParams(vmem_limit_bytes=VMEM_LIMIT),
    )(q, k, v, own, every, weight)


def flip(position, step):
    low = lax.rem(position, 2)
    high = position // 2
    return (high + (step // 2) * (1 - 2 * high)) * 2 + low + lax.rem(step, 2) * (1 - 2 * low)


def remote(src, dst, send, recv, **where):
    return pltpu.make_async_remote_copy(
        src_ref=src, dst_ref=dst, send_sem=send, recv_sem=recv, device_id=where,
        device_id_type=MESH,
    )


TOGETHER = 4


def mix_part(
    tasks, cand_ref, gate_ref, win_hbm, wout_hbm, gain_ref, nb,
    xbuf, win, wout, gates_all, gates, hidden, made, acc, part, core_in, x_out, x_in, z_out, z_in,
    load_sem, up_s, down_s, z_r, x_s, x_r, c_s, c_r, core_s, core_r, rx_s, rx_r, rz_s, rz_r,
):
    (z, x, c), (nz, nx, nc) = place()
    f32, bf = jnp.float32, jnp.bfloat16
    other_x, other_c = 1 - x, 1 - c
    held = win.shape[0]
    quarters, share, depth = xbuf.shape[1:]
    rows = quarters * share
    width = wout.shape[1]
    spot = c * nx + x
    loads = [
        pltpu.make_async_copy(cand_ref, xbuf.at[z], load_sem.at[0]),
        pltpu.make_async_copy(win_hbm, win, load_sem.at[1]),
        pltpu.make_async_copy(wout_hbm, wout, load_sem.at[2]),
    ]
    for item in loads:
        item.start()
    greet_all()

    middle = lax.rem(z, 2) + z // 2 - 2 * lax.rem(z, 2) * (z // 2)

    def partner_of(k):
        return k + middle * (lax.rem(nz - k, nz) - k)

    def slab_of(k):
        return flip(z, partner_of(k))

    piece_rows = share // 2
    half_model = part.shape[2] // 2

    def rows_of(h):
        return pl.ds(h * piece_rows, piece_rows)

    def features(f):
        return pl.ds(f * half_model, half_model)

    def upward(src, slab, d, h):
        return remote(
            src.at[rows_of(h)], xbuf.at[slab, spot, rows_of(h)], up_s.at[d, h], z_r.at[slab, h],
            wide=z + 1,
        )

    def downward(src, slab, d, h):
        return remote(
            src.at[rows_of(h)], xbuf.at[slab, spot, rows_of(h)], down_s.at[d, h],
            z_r.at[slab, h], wide=z - 1,
        )

    def sideways(slab, q, h):
        piece = xbuf.at[slab, q, rows_of(h)]
        return remote(piece, piece, x_s.at[slab, h], x_r.at[slab, h], expert=other_x)

    def corewise(slab, j, q):
        piece = xbuf.at[slab, q]
        return remote(piece, piece, c_s.at[slab, j], c_r.at[slab, j], inner=other_c)

    for h in range(2):

        @pl.when(z < nz - 1)
        def _():
            upward(cand_ref.at[spot], z, 0, h).start()

        @pl.when(z > 0)
        def _():
            downward(cand_ref.at[spot], z, 0, h).start()

    for item in loads:
        item.wait()

    def arrive_z(d, h):
        below, above = z - d, z + d

        @pl.when(below >= 0)
        def _():
            upward(xbuf.at[below, spot], below, 0, h).wait_recv()

            @pl.when(z < nz - 1)
            def _():
                upward(xbuf.at[below, spot], below, d, h).start()

        @pl.when(above < nz)
        def _():
            downward(xbuf.at[above, spot], above, 0, h).wait_recv()

            @pl.when(z > 0)
            def _():
                downward(xbuf.at[above, spot], above, d, h).start()

        slab = slab_of(d)
        sideways(slab, spot, h).start()
        if h == 1:
            corewise(slab, 0, spot).start()

    def arrive_x(slab):
        q = c * nx + other_x
        for h in range(2):
            sideways(slab, q, h).wait_recv()
        corewise(slab, 1, q).start()

    def arrive_c(slab):
        for j, q in ((0, other_c * nx + x), (1, other_c * nx + other_x)):
            corewise(slab, j, q).wait_recv()

    def to_core(k):
        return remote(
            part.at[k, pl.ds(other_c * nx, nx)], core_in.at[k], core_s.at[k], core_r.at[k],
            inner=other_c,
        )

    def to_x(k, f):
        return remote(
            x_out.at[k, features(f)], x_in.at[k, features(f)], rx_s.at[k, f], rx_r.at[k, f],
            expert=other_x,
        )

    def to_z(k, f):
        e = partner_of(k)
        return remote(
            z_out.at[k, features(f)], z_in.at[e, features(f)], rz_s.at[k, f], rz_r.at[e, f],
            wide=slab_of(k),
        )

    def reduce_core(k):
        to_core(k).wait_recv()
        for f in range(2):
            x_out[k, features(f)] = (
                part[k, c * nx + other_x, features(f)].astype(f32)
                + core_in[k, other_x, features(f)].astype(f32)
            ).astype(bf)
            to_x(k, f).start()

    def total_of(k, f):
        return (
            part[k, c * nx + x, features(f)].astype(f32)
            + core_in[k, x, features(f)].astype(f32)
            + x_in[k, features(f)].astype(f32)
        )

    def reduce_x(k, f):
        to_x(k, f).wait_recv()
        z_out[k, features(f)] = total_of(k, f).astype(bf)
        to_z(k, f).start()

    groups = held // TOGETHER

    def gating(i, k):
        side = (i % 2) * TOGETHER
        for q in range(quarters):
            lanes = slice(q * share, (q + 1) * share)
            weights = [
                [
                    gates[t * held + i * TOGETHER + j : t * held + i * TOGETHER + j + 1, lanes]
                    for j in range(TOGETHER)
                ]
                for t in range(tasks)
            ]
            for f in range(0, width, 16):
                outs = [made[side + j, f : f + 16, lanes] for j in range(TOGETHER)]
                for t in range(tasks):
                    span = slice(t * width + f, t * width + f + 16)
                    piece = weights[t][0] * outs[0]
                    for j in range(1, TOGETHER):
                        piece = piece + weights[t][j] * outs[j]
                    if i > 0:
                        piece = piece + acc[q, span, :]
                    if i < groups - 1:
                        acc[q, span, :] = piece
                    else:
                        part[k, q, span, :] = piece.astype(bf)

    def stage(i, data, k):
        if i < groups:
            for j in range(TOGETHER):
                e = i * TOGETHER + j
                hidden[(i % 2) * TOGETHER + j] = jnp.maximum(
                    jnp.dot(data, win[e], preferred_element_type=f32), 0.0
                ).astype(bf)
        if 0 < i <= groups:
            side = ((i - 1) % 2) * TOGETHER
            for j in range(TOGETHER):
                e = (i - 1) * TOGETHER + j
                made[side + j] = lax.dot_general(
                    wout[e], hidden[side + j], (((1,), (1,)), ((), ())),
                    preferred_element_type=f32,
                )
        if i > 1:
            gating(i - 2, k)

    agenda = (
        (0, 0, lambda: arrive_z(1, 0)),
        (0, 2, lambda: arrive_z(1, 1)),
        (0, 4, lambda: arrive_z(2, 0)),
        (1, 2, lambda: arrive_z(3, 0)),
        (1, 4, lambda: arrive_z(3, 1)),
        (1, 5, lambda: reduce_core(0)),
        (2, 1, lambda: reduce_core(1)),
        (3, 1, lambda: reduce_core(2)),
        (3, 2, lambda: reduce_x(1, 0)),
        (3, 3, lambda: reduce_x(1, 1)),
        (3, 5, lambda: reduce_x(2, 0)),
    )

    def step(k, carry):
        slab = slab_of(k)
        data = xbuf[slab].reshape(rows, depth)
        logits = lax.dot_general(
            gate_ref[...], data, (((0,), (1,)), ((), ())), preferred_element_type=f32
        )
        logits = logits.reshape(tasks, logits.shape[0] // tasks, rows)
        powers = jnp.exp(logits - jnp.max(logits, axis=1, keepdims=True))
        gates_all[...] = powers / jnp.sum(powers, axis=1, keepdims=True)
        for t in range(tasks):
            gates[t * held : (t + 1) * held, :] = gates_all[
                t, pl.ds(pl.multiple_of(x * held, held), held), :
            ]
        after = slab_of(k + 1)
        for i in range(groups + 2):
            for moment, boundary, action in agenda:
                if boundary == i:
                    pl.when(k == moment)(action)
            if i > 0:
                data = xbuf[slab].reshape(rows, depth)
            stage(i, data, k)
        to_core(k).start()

        @pl.when(k == 0)
        def _():
            arrive_z(2, 1)

        @pl.when(k < nz - 1)
        def _():
            arrive_x(after)
            arrive_c(after)

        return carry

    lax.fori_loop(0, nz, step, 0)
    reduce_x(2, 1)
    reduce_core(3)
    for f in range(2):
        reduce_x(3, f)
    totals = []
    for f in range(2):
        to_x(0, f).wait_recv()
        total = total_of(0, f)
        for k in range(1, nz):
            place_in = z_in.at[k, features(f)]
            remote(
                place_in, place_in, rz_s.at[k, f], rz_r.at[k, f], wide=flip(z, k)
            ).wait_recv()
            total = total + place_in[...].astype(f32)
        totals.append(total)
    total = jnp.concatenate(totals, axis=0)
    total = total.T
    center = jnp.mean(total, axis=1, keepdims=True)
    spread = jnp.mean(jnp.square(total - center), axis=1, keepdims=True)
    gain = gain_ref[...].astype(f32)
    gain = jnp.concatenate([gain[i : i + 1, :] for i in range(gain.shape[0])], axis=1)
    normed = (total - center) * lax.rsqrt(spread + 1e-05) * gain
    nb[x, c] = normed.astype(bf)
    yield
    for d in range(nz - 1):
        for h in range(2):

            @pl.when((z < nz - 1) & (z - d >= 0))
            def _():
                upward(xbuf.at[z, spot], z, d, h).wait_send()

            @pl.when((z > 0) & (z + d < nz))
            def _():
                downward(xbuf.at[z, spot], z, d, h).wait_send()

    for k in range(1, nz):
        slab = flip(z, k)
        corewise(slab, 0, spot).wait_send()
        corewise(slab, 1, spot).wait_send()
        for h in range(2):
            sideways(slab, spot, h).wait_send()
            to_z(k, h).wait_send()
    for k in range(nz):
        to_core(k).wait_send()
        for f in range(2):
            to_x(k, f).wait_send()


def greet_all():
    (z, x, c), (nz, nx, nc) = place()
    barrier = pltpu.get_barrier_semaphore()
    pl.semaphore_signal(
        barrier, inc=1, device_id={"expert": 1 - x, "inner": 1 - c}, device_id_type=MESH
    )
    for axis, here, size in zip(ALL, (z, x, c), (nz, nx, nc)):
        for turned in range(1, size):
            pl.semaphore_signal(
                barrier, inc=1, device_id={axis: turn(here, turned, size)}, device_id_type=MESH
            )
    pl.semaphore_wait(barrier, nz + nx + nc - 2)


def whole_kernel(
    tasks, mix_count, cand_ref, gate_ref, win_hbm, wout_hbm, gain_ref,
    q_hbm, k_hbm, v_hbm, task_ref, attn_ref, id_ref, out_ref, *scratch
):
    nb = scratch[mix_count]
    mix = mix_part(
        tasks, cand_ref, gate_ref, win_hbm, wout_hbm, gain_ref, nb, *scratch[:mix_count]
    )
    score = score_part(
        q_hbm, k_hbm, v_hbm, task_ref, attn_ref, id_ref, out_ref, *scratch[mix_count:]
    )
    next(score)
    next(mix)
    next(score, None)
    next(mix, None)


def score_part(
    q_hbm, k_hbm, v_hbm, task_ref, attn_ref, id_ref, out_ref,
    nb, q_ref, k_ref, v_ref, keys, extra, ids, queries, powers, high, sums, partial,
    load_sem, n_s, n_r, id_s, id_r, up_s, down_s, key_r, p_s, p_r,
):
    (z, x, c), (nz, nx, nc) = place()
    f32, bf = jnp.float32, jnp.bfloat16
    other_x, other_c = 1 - x, 1 - c
    _, _, share, depth = nb.shape
    rows = nx * nc * share
    both = nc * share
    heads = queries.shape[1] // HD
    tasks = task_ref.shape[0]
    loads = [
        pltpu.make_async_copy(k_hbm, k_ref, load_sem.at[0]),
        pltpu.make_async_copy(v_hbm, v_ref, load_sem.at[1]),
        pltpu.make_async_copy(q_hbm, q_ref, load_sem.at[2]),
    ]
    for item in loads:
        item.start()
    yield

    def give(side, core, j, **where):
        return remote(nb.at[side, core], nb.at[side, core], n_s.at[j], n_r.at[j], **where)

    first = give(x, c, 0, expert=other_x)
    second = give(x, c, 1, inner=other_c)
    third = give(other_x, c, 2, inner=other_c)
    first.start()
    second.start()
    id_copies = []
    for turned in range(1, nz):
        target = turn(z, turned, nz)
        item = remote(id_ref, ids.at[z], id_s.at[turned], id_r.at[z], wide=target)
        item.start()
        id_copies.append(item)
    ids[z] = id_ref[...]
    for item in loads:
        item.wait()
    own = jnp.concatenate([id_ref[q] for q in range(nx * nc)], axis=1).astype(f32)
    own = jnp.broadcast_to(own, (8, rows)).T[:, :1]
    lifted = heads * tasks
    extra[:, :, lifted:, :] = jnp.ones((nz, nx, 16, both), bf)
    shape = (lifted, heads * HD)
    row = lax.broadcasted_iota(jnp.int32, shape, 0) // tasks
    column = lax.broadcasted_iota(jnp.int32, shape, 1) // HD
    stacked = jnp.concatenate([attn_ref[...].astype(f32)] * heads, axis=0)
    blocks = jnp.where(row == column, stacked, 0.0).astype(bf)
    sides = (x, other_x)

    def parts(slab, m):
        return [keys.at[slab, sides[m]], extra.at[slab, sides[m], pl.ds(0, lifted)]]

    def upward(slab, d, m, j):
        piece = parts(slab, m)[j]
        return remote(piece, piece, up_s.at[d, m, j], key_r.at[slab, m, j], wide=z + 1)

    def downward(slab, d, m, j):
        piece = parts(slab, m)[j]
        return remote(piece, piece, down_s.at[d, m, j], key_r.at[slab, m, j], wide=z - 1)

    def announce(m, j):
        @pl.when(z < nz - 1)
        def _():
            upward(z, 0, m, j).start()

        @pl.when(z > 0)
        def _():
            downward(z, 0, m, j).start()

    def pass_on(d, m):
        for slab, here, further, way in (
            (z - d, z - d >= 0, z < nz - 1, upward),
            (z + d, z + d < nz, z > 0, downward),
        ):

            @pl.when(here)
            def _():
                for j in range(2):
                    way(slab, 0, m, j).wait_recv()

                    @pl.when(further)
                    def _():
                        way(slab, d, m, j).start()

    def make(m):
        data = nb[sides[m]].reshape(both, depth)
        keys[z, sides[m]] = jnp.dot(data, k_ref[...], preferred_element_type=f32).astype(bf)
        announce(m, 0)
        values = jnp.dot(data, v_ref[...], preferred_element_type=f32).astype(bf)
        extra[z, sides[m], :lifted, :] = lax.dot_general(
            blocks, values, (((1,), (1,)), ((), ())), preferred_element_type=f32
        ).astype(bf)
        announce(m, 1)

    give(x, other_c, 1, inner=other_c).wait_recv()
    make(0)
    give(other_x, c, 0, expert=other_x).wait_recv()
    third.start()
    pass_on(1, 0)
    give(other_x, other_c, 2, inner=other_c).wait_recv()
    make(1)
    data = jnp.concatenate([nb[q % nx, q // nx] for q in range(nx * nc)], axis=0)
    queries[...] = (
        jnp.dot(data, q_ref[...], preferred_element_type=f32) * (1.0 / math.sqrt(HD))
    ).astype(bf)
    for item in id_copies:
        item.wait_send()
    for turned in range(1, nz):
        source = turn(z, turned, nz)
        remote(id_ref, ids.at[source], id_s.at[turned], id_r.at[source], wide=source).wait_recv()

    def attend(slab, m, fresh=False):
        side = sides[m]
        theirs = jnp.concatenate([ids[slab, side], ids[slab, nx + side]], axis=1)
        same = own == theirs.astype(f32)
        tops = []
        for h in range(heads):
            span = slice(h * HD, (h + 1) * HD)
            affinity = lax.dot_general(
                queries[:, span],
                keys[slab, side][:, span],
                (((1,), (1,)), ((), ())),
                preferred_element_type=f32,
            )
            affinity = jnp.where(same, affinity, -1e30)
            top = jnp.max(affinity, axis=1, keepdims=True)
            powers[h] = jnp.exp(affinity - top).astype(bf)
            tops.append(top)
        for h in range(heads):
            got = lax.dot_general(
                powers[h], extra[slab, side], (((1,), (1,)), ((), ())),
                preferred_element_type=f32,
            )
            if fresh:
                high[h] = tops[h]
                sums[h] = got
            else:
                peak = jnp.maximum(high[h], tops[h])
                sums[h] = sums[h] * jnp.exp(high[h] - peak) + got * jnp.exp(tops[h] - peak)
                high[h] = peak

    attend(z, 0, True)
    attend(z, 1)
    pass_on(1, 1)
    attend(flip(z, 1), 0)
    pass_on(2, 0)
    attend(flip(z, 1), 1)
    pass_on(2, 1)
    attend(flip(z, 2), 0)
    attend(flip(z, 2), 1)
    pass_on(3, 0)
    attend(flip(z, 3), 0)
    pass_on(3, 1)
    attend(flip(z, 3), 1)
    columns = sums.shape[2]
    lane = lax.broadcasted_iota(jnp.int32, (rows, columns), 1)
    result = jnp.zeros((rows, columns), f32)
    for h in range(heads):
        got = sums[h]
        mean = got / got[:, lifted : lifted + 1]
        result = jnp.where((lane < lifted) & (lane // tasks == h), mean, result)
    shape = (8, columns)
    spot = lax.broadcasted_iota(jnp.int32, shape, 1)
    pick = (spot % tasks == lax.broadcasted_iota(jnp.int32, shape, 0)) & (spot < lifted)
    partial[0] = lax.dot_general(
        pick.astype(f32), result, (((1,), (1,)), ((), ())),
        preferred_element_type=f32, precision=lax.Precision.HIGHEST,
    )
    sends = []
    for j, where in enumerate(
        ({"inner": other_c}, {"expert": other_x}, {"expert": other_x, "inner": other_c})
    ):
        item = remote(partial.at[0], partial.at[j + 1], p_s.at[j], p_r.at[j], **where)
        item.start()
        sends.append(item)
    base = lax.dot_general(
        task_ref[...], data, (((1,), (1,)), ((), ())), preferred_element_type=f32
    )
    for item in sends:
        item.wait()
    everything = (partial[0] + partial[1]) + (partial[2] + partial[3])
    out_ref[...] = everything[:tasks, :] + base
    first.wait_send()
    second.wait_send()
    third.wait_send()
    for d in range(nz - 1):
        for m in range(2):
            for j in range(2):

                @pl.when((z < nz - 1) & (z - d >= 0))
                def _():
                    upward(z, d, m, j).wait_send()

                @pl.when((z > 0) & (z + d < nz))
                def _():
                    downward(z, d, m, j).wait_send()


def run_whole(
    cand, gate_weight, expert_in, expert_out, gain, query, key, value, task, attn, request_of,
    collective,
):
    nz, nx, nc = (lax.axis_size(a) for a in ALL)
    rows, depth = cand.shape
    quarters = nx * nc
    share = rows // quarters
    held, _, units = expert_in.shape
    width = expert_out.shape[1]
    tasks = task.shape[1]
    dma = pltpu.SemaphoreType.DMA
    f32, bf = jnp.float32, jnp.bfloat16
    vmem = pl.BlockSpec(memory_space=pltpu.VMEM)
    anywhere = pl.BlockSpec(memory_space=pl.ANY)
    model = tasks * width
    experts_all = gate_weight.shape[1] // tasks
    lanes = query.shape[1]
    heads = lanes // HD
    mix_scratch = [
        pltpu.VMEM((nz, quarters, share, depth), bf),
        pltpu.VMEM(expert_in.shape, bf),
        pltpu.VMEM(expert_out.shape, bf),
        pltpu.VMEM((tasks, experts_all, rows), f32),
        pltpu.VMEM((tasks * held, rows), f32),
        pltpu.VMEM((2 * TOGETHER, rows, units), bf),
        pltpu.VMEM((2 * TOGETHER, width, rows), f32),
        pltpu.VMEM((quarters, model, share), f32),
        pltpu.VMEM((nz, quarters, model, share), bf),
        pltpu.VMEM((nz, nx, model, share), bf),
        pltpu.VMEM((nz, model, share), bf),
        pltpu.VMEM((nz, model, share), bf),
        pltpu.VMEM((nz, model, share), bf),
        pltpu.VMEM((nz, model, share), bf),
        dma((3,)),
        dma((nz, 2)),
        dma((nz, 2)),
        dma((nz, 2)),
        dma((nz, 2)),
        dma((nz, 2)),
        dma((nz, 2)),
        dma((nz, 2)),
        dma((nz,)),
        dma((nz,)),
        dma((nz, 2)),
        dma((nz, 2)),
        dma((nz, 2)),
        dma((nz, 2)),
    ]
    columns = heads * tasks + 16
    score_scratch = [
        pltpu.VMEM((nx, nc, share, model), bf),
        pltpu.VMEM(query.shape, bf),
        pltpu.VMEM(key.shape, bf),
        pltpu.VMEM(value.shape, bf),
        pltpu.VMEM((nz, nx, nc * share, lanes), bf),
        pltpu.VMEM((nz, nx, columns, nc * share), bf),
        pltpu.VMEM((nz, quarters, 1, share), jnp.int32),
        pltpu.VMEM((rows, lanes), bf),
        pltpu.VMEM((heads, rows, nc * share), bf),
        pltpu.VMEM((heads, rows, 1), f32),
        pltpu.VMEM((heads, rows, columns), f32),
        pltpu.VMEM((nx * nc, 8, rows), f32),
        dma((3,)),
        dma((3,)),
        dma((3,)),
        dma((nz,)),
        dma((nz,)),
        dma((nz, 2, 2)),
        dma((nz, 2, 2)),
        dma((nz, 2, 2)),
        dma((3,)),
        dma((3,)),
    ]
    return pl.pallas_call(
        functools.partial(whole_kernel, tasks, len(mix_scratch)),
        in_specs=[anywhere, vmem, anywhere, anywhere, vmem, anywhere, anywhere, anywhere]
        + [vmem] * 3,
        out_specs=vmem,
        out_shape=jax.ShapeDtypeStruct((tasks, rows), f32),
        scratch_shapes=mix_scratch + score_scratch,
        compiler_params=pltpu.CompilerParams(
            collective_id=collective, has_side_effects=True, vmem_limit_bytes=VMEM_LIMIT
        ),
    )(
        cand.reshape(quarters, share, depth), gate_weight, expert_in, expert_out,
        gain.reshape(-1, 128), query, key, value, task.T, attn.T,
        request_of.reshape(quarters, 1, share),
    ).T


def fused(sizes, rows, heads, held):
    return sizes == (4, 2, 2) and rows % 512 == 0 and heads == 4 and held % (2 * TOGETHER) == 0


def local(
    candidates,
    gate_weight,
    expert_in,
    expert_out,
    norm_gain,
    query_weight,
    key_weight,
    value_weight,
    task_weight,
    attn_weight,
    request_of,
):
    rows = candidates.shape[0]
    tasks = task_weight.shape[1]
    nz, nx, nc = (lax.axis_size(a) for a in ALL)
    if fused((nz, nx, nc), rows, query_weight.shape[1] // HD, expert_in.shape[0]):
        return run_whole(
            candidates, gate_weight, expert_in, expert_out, norm_gain, query_weight, key_weight,
            value_weight, task_weight, attn_weight, request_of, 3,
        )
    share = rows // (nx * nc)
    spot = lax.axis_index("inner") * nx + lax.axis_index("expert")
    wide = lax.axis_index("wide")
    quarter = lax.dynamic_slice_in_dim(candidates, spot * share, share, 0)
    everyone, requests = run_gather(quarter, request_of[None, :], 0)
    partial_mix = run_experts(everyone, gate_weight, expert_in, expert_out, tasks)
    normed = run_reduce(partial_mix, norm_gain[None, :], share, 1)
    normed_all = run_gather(normed, None, 2)
    own = lax.dynamic_slice_in_dim(normed_all, wide * rows, rows, 0)
    queries = jnp.dot(own, query_weight, preferred_element_type=jnp.float32).astype(jnp.bfloat16)
    keys = jnp.dot(normed_all, key_weight, preferred_element_type=jnp.float32).astype(jnp.bfloat16)
    values = jnp.dot(normed_all, value_weight, preferred_element_type=jnp.float32).astype(
        jnp.bfloat16
    )
    term = run_attention(
        queries, keys, values, request_of[:, None], requests, attn_weight
    )
    attention = lax.psum(term.T, ("expert", "inner")).T
    return jnp.dot(own, task_weight, preferred_element_type=jnp.float32) + attention


def solution(mesh):
    return jax.shard_map(
        local,
        mesh=mesh,
        in_specs=(
            P(("groups", "wide"), None),
            P(),
            P("expert", None, ("wide", "inner")),
            P("expert", None, ("wide", "inner")),
            P(),
            P(None, ("expert", "inner")),
            P(None, ("expert", "inner")),
            P(None, ("expert", "inner")),
            P(),
            P(("expert", "inner"), None),
            P(("groups", "wide")),
        ),
        out_specs=P(("groups", "wide"), None),
        check_vma=False,
    )
```

```python
import functools
import math

import jax
import jax.numpy as jnp
from jax import lax
from jax.experimental import pallas as pl
from jax.experimental.pallas import tpu as pltpu
from jax.sharding import PartitionSpec as P

HD = 64
ALL = ("wide", "expert", "inner")
VMEM_LIMIT = 60 * 1024 * 1024


MESH = pl.DeviceIdType.MESH


def place():
    return tuple(lax.axis_index(a) for a in ALL), tuple(lax.axis_size(a) for a in ALL)


def turn(start, step, size):
    return lax.rem(start + step, size)


def greet():
    mine, sizes = place()
    barrier = pltpu.get_barrier_semaphore()
    for axis, here, size in zip(ALL, mine, sizes):
        for step in range(1, size):
            pl.semaphore_signal(
                barrier, inc=1, device_id={axis: turn(here, step, size)}, device_id_type=MESH
            )
    pl.semaphore_wait(barrier, sum(sizes) - len(sizes))


def gather_kernel(with_ids, *refs):
    if with_ids:
        own_ref, id_ref, out_ref, ids_ref, recv, send_z, send_x, send_c, local_sem, id_r, id_s = refs
    else:
        own_ref, out_ref, recv, send_z, send_x, send_c, local_sem = refs
    (z, x, c), (nz, nx, nc) = place()
    greet()

    def copy(src, zs, xs, cs, sem, axis, target):
        return pltpu.make_async_remote_copy(
            src_ref=src,
            dst_ref=out_ref.at[zs, cs, xs],
            send_sem=sem,
            recv_sem=recv.at[zs, cs, xs],
            device_id={axis: target},
            device_id_type=MESH,
        )

    def arrived(zs, xs, cs):
        copy(out_ref.at[zs, cs, xs], zs, xs, cs, send_z.at[0], "inner", turn(c, 1, nc)).wait_recv()

    sent = []

    def push(*what):
        item = copy(*what)
        item.start()
        sent.append(item)

    def spread_x(src, k, zs):
        for step in range(1, nx):
            push(src, zs, x, c, send_x.at[k, step - 1], "expert", turn(x, step, nx))

    def spread_c(src, k, j, zs, xs):
        for step in range(1, nc):
            push(src, zs, xs, c, send_c.at[k, j, step - 1], "inner", turn(c, step, nc))

    for step in range(1, nz):
        push(own_ref, z, x, c, send_z.at[step - 1], "wide", turn(z, step, nz))
    spread_x(own_ref, 0, z)
    spread_c(own_ref, 0, 0, z, x)
    keep = pltpu.make_async_copy(own_ref, out_ref.at[z, c, x], local_sem.at[0])
    keep.start()
    if with_ids:
        id_copies = []
        for step in range(1, nz):
            item = pltpu.make_async_remote_copy(
                src_ref=id_ref,
                dst_ref=ids_ref.at[z],
                send_sem=id_s.at[step - 1],
                recv_sem=id_r.at[z],
                device_id={"wide": turn(z, step, nz)},
                device_id_type=MESH,
            )
            item.start()
            id_copies.append(item)
        ids_ref[z] = id_ref[...]

    def pass_x(k):
        zs = turn(z, k, nz)
        for step in range(1, nx):
            xs = turn(x, step, nx)
            arrived(zs, xs, c)
            spread_c(out_ref.at[zs, c, xs], k, step, zs, xs)

    for k in range(1, nz):
        zs = turn(z, k, nz)
        arrived(zs, x, c)
        spread_x(out_ref.at[zs, c, x], k, zs)
        spread_c(out_ref.at[zs, c, x], k, 0, zs, x)
        pass_x(k - 1)
    pass_x(nz - 1)
    for k in range(nz):
        for j in range(nx):
            for step in range(1, nc):
                arrived(turn(z, k, nz), turn(x, j, nx), turn(c, step, nc))
    for item in sent:
        item.wait_send()
    keep.wait()
    if with_ids:
        for step in range(1, nz):
            zs = turn(z, step, nz)
            pltpu.make_async_remote_copy(
                src_ref=id_ref,
                dst_ref=ids_ref.at[zs],
                send_sem=id_s.at[step - 1],
                recv_sem=id_r.at[zs],
                device_id={"wide": zs},
                device_id_type=MESH,
            ).wait_recv()
        for item in id_copies:
            item.wait_send()


def run_gather(own, ids, collective):
    nz, nx, nc = (lax.axis_size(a) for a in ALL)
    dma = pltpu.SemaphoreType.DMA
    with_ids = ids is not None
    shape = jax.ShapeDtypeStruct((nz, nc, nx) + own.shape, own.dtype)
    vmem = pl.BlockSpec(memory_space=pltpu.VMEM)
    anywhere = pl.BlockSpec(memory_space=pl.ANY)
    scratch = [
        dma((nz, nc, nx)),
        dma((max(nz - 1, 1),)),
        dma((nz, max(nx - 1, 1))),
        dma((nz, nx, max(nc - 1, 1))),
        dma((1,)),
    ]
    if with_ids:
        scratch += [dma((nz,)), dma((max(nz - 1, 1),))]
    out = pl.pallas_call(
        functools.partial(gather_kernel, with_ids),
        in_specs=[vmem, vmem] if with_ids else [vmem],
        out_specs=[anywhere, vmem] if with_ids else anywhere,
        out_shape=[shape, jax.ShapeDtypeStruct((nz,) + ids.shape, ids.dtype)] if with_ids else shape,
        scratch_shapes=scratch,
        compiler_params=pltpu.CompilerParams(collective_id=collective, has_side_effects=True),
    )(*([own, ids] if with_ids else [own]))
    depth = own.shape[1]
    if with_ids:
        return out[0].reshape(-1, depth), out[1].reshape(1, -1)
    return out.reshape(-1, depth)


def reduce_kernel(
    part_ref, gain_ref, out_ref, mine, core_in, x_out, x_in, z_out, z_in,
    local_sem, core_s, core_r, x_s, x_r, z_s, z_r,
):
    (z, x, c), (nz, nx, nc) = place()
    f32 = jnp.float32
    greet()
    other = turn(c, 1, nc)
    core, kept = [], []
    for k in range(nz):
        s = turn(z, k + 1, nz)
        item = pltpu.make_async_remote_copy(
            src_ref=part_ref.at[s, other],
            dst_ref=core_in.at[k],
            send_sem=core_s.at[k],
            recv_sem=core_r.at[k],
            device_id={"inner": other},
            device_id_type=MESH,
        )
        item.start()
        core.append(item)
        stay = pltpu.make_async_copy(part_ref.at[s, c], mine.at[k], local_sem.at[k])
        stay.start()
        kept.append(stay)

    def pair(k, xs):
        return mine[k, xs].astype(f32) + core_in[k, xs].astype(f32)

    across, along = [], []

    def finish(k):
        total = pair(k, x)
        for step in range(1, nx):
            across[k][step - 1].wait_recv()
            total = total + x_in[k, step - 1].astype(f32)
        if k == nz - 1:
            return total
        z_out[k] = total.astype(z_out.dtype)
        item = pltpu.make_async_remote_copy(
            src_ref=z_out.at[k],
            dst_ref=z_in.at[k],
            send_sem=z_s.at[k],
            recv_sem=z_r.at[k],
            device_id={"wide": turn(z, k + 1, nz)},
            device_id_type=MESH,
        )
        item.start()
        along.append(item)

    for k in range(nz):
        kept[k].wait()
        core[k].wait_recv()
        items = []
        for step in range(1, nx):
            xs = turn(x, step, nx)
            x_out[k, step - 1] = pair(k, xs).astype(x_out.dtype)
            item = pltpu.make_async_remote_copy(
                src_ref=x_out.at[k, step - 1],
                dst_ref=x_in.at[k, step - 1],
                send_sem=x_s.at[k, step - 1],
                recv_sem=x_r.at[k, step - 1],
                device_id={"expert": xs},
                device_id_type=MESH,
            )
            item.start()
            items.append(item)
        across.append(items)
        if k > 0:
            finish(k - 1)
    total = finish(nz - 1)
    for k in range(nz - 1):
        along[k].wait_recv()
        total = total + z_in[k].astype(f32)
    center = jnp.mean(total, axis=1, keepdims=True)
    spread = jnp.mean(jnp.square(total - center), axis=1, keepdims=True)
    normed = (total - center) * lax.rsqrt(spread + 1e-05) * gain_ref[...].astype(f32)
    out_ref[...] = normed.astype(out_ref.dtype)
    for item in core + along + [i for items in across for i in items]:
        item.wait_send()


def run_reduce(part, gain, share, collective):
    nz, nx, nc = (lax.axis_size(a) for a in ALL)
    width = part.shape[1]
    dma = pltpu.SemaphoreType.DMA
    kind = part.dtype
    part = part.reshape(nz, nc, nx, share, width)
    few = max(nx - 1, 1)
    vmem = pl.BlockSpec(memory_space=pltpu.VMEM)
    return pl.pallas_call(
        reduce_kernel,
        in_specs=[pl.BlockSpec(memory_space=pl.ANY), vmem],
        out_specs=vmem,
        out_shape=jax.ShapeDtypeStruct((share, width), kind),
        scratch_shapes=[
            pltpu.VMEM((nz, nx, share, width), kind),
            pltpu.VMEM((nz, nx, share, width), kind),
            pltpu.VMEM((nz, few, share, width), kind),
            pltpu.VMEM((nz, few, share, width), kind),
            pltpu.VMEM((nz, share, width), kind),
            pltpu.VMEM((nz, share, width), kind),
            dma((nz,)),
            dma((nz,)),
            dma((nz,)),
            dma((nz, few)),
            dma((nz, few)),
            dma((nz,)),
            dma((nz,)),
        ],
        compiler_params=pltpu.CompilerParams(
            collective_id=collective, has_side_effects=True, vmem_limit_bytes=VMEM_LIMIT
        ),
    )(part, gain)


def expert_kernel(tasks, x_ref, gate_ref, win_ref, wout_ref, out_ref, acc_ref):
    rows = x_ref.shape[0]
    columns = gate_ref.shape[1]
    experts_all = columns // tasks
    held, _, _ = win_ref.shape
    width = wout_ref.shape[1]
    x = x_ref[...]
    logits = jnp.dot(x, gate_ref[...], preferred_element_type=jnp.float32)
    task = lax.broadcasted_iota(jnp.int32, (rows, columns), 1) // experts_all
    top = jnp.zeros_like(logits)
    for t in range(tasks):
        high = jnp.max(jnp.where(task == t, logits, -jnp.inf), axis=1, keepdims=True)
        top = jnp.where(task == t, high, top)
    powers = jnp.exp(logits - top)
    total = jnp.ones_like(logits)
    for t in range(tasks):
        part = jnp.sum(jnp.where(task == t, powers, 0.0), axis=1, keepdims=True)
        total = jnp.where(task == t, part, total)
    gates = powers / total
    shift = lax.rem(columns - lax.axis_index("expert") * held, columns)
    gates = pltpu.roll(gates, shift, 1)
    together = min(4, held)
    for first in range(0, held, together):
        made = []
        for e in range(first, first + together):
            hidden = jnp.maximum(
                jnp.dot(x, win_ref[e], preferred_element_type=jnp.float32), 0.0
            ).astype(jnp.bfloat16)
            made.append(
                lax.dot_general(
                    hidden,
                    wout_ref[e],
                    (((1,), (1,)), ((), ())),
                    preferred_element_type=jnp.float32,
                )
            )
        for t in range(tasks):
            piece = None
            for j, output in enumerate(made):
                lane = t * experts_all + first + j
                term = gates[:, lane : lane + 1] * output
                piece = term if piece is None else piece + term
            span = slice(t * width, (t + 1) * width)
            if first > 0:
                piece = piece + acc_ref[:, span]
            if first + together < held:
                acc_ref[:, span] = piece
            else:
                out_ref[:, span] = piece.astype(out_ref.dtype)


def run_experts(x, gate_weight, expert_in, expert_out, tasks):
    rows, depth = x.shape
    held, _, units = expert_in.shape
    width = expert_out.shape[1]
    block = min(512, rows)
    return pl.pallas_call(
        functools.partial(expert_kernel, tasks),
        grid=(rows // block,),
        in_specs=[
            pl.BlockSpec((block, depth), lambda i: (i, 0)),
            pl.BlockSpec(gate_weight.shape, lambda i: (0, 0)),
            pl.BlockSpec(expert_in.shape, lambda i: (0, 0, 0), pipeline_mode=pl.Buffered(1)),
            pl.BlockSpec(expert_out.shape, lambda i: (0, 0, 0), pipeline_mode=pl.Buffered(1)),
        ],
        out_specs=pl.BlockSpec((block, tasks * width), lambda i: (i, 0)),
        out_shape=jax.ShapeDtypeStruct((rows, tasks * width), jnp.bfloat16),
        scratch_shapes=[pltpu.VMEM((block, tasks * width), jnp.float32)],
        compiler_params=pltpu.CompilerParams(vmem_limit_bytes=VMEM_LIMIT),
    )(x, gate_weight, expert_in, expert_out)


def attention_kernel(q_ref, k_ref, v_ref, own_ref, all_ref, weight_ref, out_ref):
    same = own_ref[...] == all_ref[...]
    factor = 1.0 / math.sqrt(HD)
    result = None
    for first in range(0, q_ref.shape[1], HD):
        span = slice(first, first + HD)
        affinity = (
            lax.dot_general(
                q_ref[:, span],
                k_ref[:, span],
                (((1,), (1,)), ((), ())),
                preferred_element_type=jnp.float32,
            )
            * factor
        )
        affinity = jnp.where(same, affinity, -1e30)
        highest = jnp.max(affinity, axis=1, keepdims=True)
        powers = jnp.exp(affinity - highest)
        total = jnp.sum(powers, axis=1, keepdims=True)
        context = jnp.dot(
            powers.astype(jnp.bfloat16), v_ref[:, span], preferred_element_type=jnp.float32
        )
        context = (context / total).astype(jnp.bfloat16)
        term = jnp.dot(context, weight_ref[span, :], preferred_element_type=jnp.float32)
        result = term if result is None else result + term
    out_ref[...] = result


def run_attention(q, k, v, own, every, weight):
    rows, width = q.shape
    keys = k.shape[0]
    tasks = weight.shape[1]
    block = min(128, rows)
    return pl.pallas_call(
        attention_kernel,
        grid=(rows // block,),
        in_specs=[
            pl.BlockSpec((block, width), lambda i: (i, 0)),
            pl.BlockSpec((keys, width), lambda i: (0, 0)),
            pl.BlockSpec((keys, width), lambda i: (0, 0)),
            pl.BlockSpec((block, 1), lambda i: (i, 0)),
            pl.BlockSpec((1, keys), lambda i: (0, 0)),
            pl.BlockSpec((width, tasks), lambda i: (0, 0)),
        ],
        out_specs=pl.BlockSpec((block, tasks), lambda i: (i, 0)),
        out_shape=jax.ShapeDtypeStruct((rows, tasks), jnp.float32),
        compiler_params=pltpu.CompilerParams(vmem_limit_bytes=VMEM_LIMIT),
    )(q, k, v, own, every, weight)


def flip(position, step):
    low = lax.rem(position, 2)
    high = position // 2
    return (high + (step // 2) * (1 - 2 * high)) * 2 + low + lax.rem(step, 2) * (1 - 2 * low)


def remote(src, dst, send, recv, **where):
    return pltpu.make_async_remote_copy(
        src_ref=src, dst_ref=dst, send_sem=send, recv_sem=recv, device_id=where,
        device_id_type=MESH,
    )


TOGETHER = 4


def mix_part(
    tasks, cand_ref, gate_ref, win_hbm, wout_hbm, gain_ref, nb,
    xbuf, win, wout, gates_all, gates, hidden, made, acc, part, core_in, x_out, x_in, z_out, z_in,
    load_sem, up_s, down_s, z_r, x_s, x_r, c_s, c_r, core_s, core_r, rx_s, rx_r, rz_s, rz_r,
):
    (z, x, c), (nz, nx, nc) = place()
    f32, bf = jnp.float32, jnp.bfloat16
    other_x, other_c = 1 - x, 1 - c
    held = win.shape[0]
    quarters, share, depth = xbuf.shape[1:]
    rows = quarters * share
    width = wout.shape[1]
    spot = c * nx + x
    loads = [
        pltpu.make_async_copy(cand_ref, xbuf.at[z], load_sem.at[0]),
        pltpu.make_async_copy(win_hbm, win, load_sem.at[1]),
        pltpu.make_async_copy(wout_hbm, wout, load_sem.at[2]),
    ]
    for item in loads:
        item.start()
    greet_all()

    piece_rows = share // 2
    half_model = part.shape[2] // 2

    def rows_of(h):
        return pl.ds(h * piece_rows, piece_rows)

    def features(f):
        return pl.ds(f * half_model, half_model)

    def upward(src, slab, d, h):
        return remote(
            src.at[rows_of(h)], xbuf.at[slab, spot, rows_of(h)], up_s.at[d, h], z_r.at[slab, h],
            wide=z + 1,
        )

    def downward(src, slab, d, h):
        return remote(
            src.at[rows_of(h)], xbuf.at[slab, spot, rows_of(h)], down_s.at[d, h],
            z_r.at[slab, h], wide=z - 1,
        )

    def sideways(slab, q, h):
        piece = xbuf.at[slab, q, rows_of(h)]
        return remote(piece, piece, x_s.at[slab, h], x_r.at[slab, h], expert=other_x)

    def corewise(slab, j, q):
        piece = xbuf.at[slab, q]
        return remote(piece, piece, c_s.at[slab, j], c_r.at[slab, j], inner=other_c)

    for h in range(2):

        @pl.when(z < nz - 1)
        def _():
            upward(cand_ref.at[spot], z, 0, h).start()

        @pl.when(z > 0)
        def _():
            downward(cand_ref.at[spot], z, 0, h).start()

    for item in loads:
        item.wait()

    def arrive_z(d, h):
        below, above = z - d, z + d

        @pl.when(below >= 0)
        def _():
            upward(xbuf.at[below, spot], below, 0, h).wait_recv()

            @pl.when(z < nz - 1)
            def _():
                upward(xbuf.at[below, spot], below, d, h).start()

        @pl.when(above < nz)
        def _():
            downward(xbuf.at[above, spot], above, 0, h).wait_recv()

            @pl.when(z > 0)
            def _():
                downward(xbuf.at[above, spot], above, d, h).start()

        slab = flip(z, d)
        sideways(slab, spot, h).start()
        if h == 1:
            corewise(slab, 0, spot).start()

    def arrive_x(slab):
        q = c * nx + other_x
        for h in range(2):
            sideways(slab, q, h).wait_recv()
        corewise(slab, 1, q).start()

    def arrive_c(slab):
        for j, q in ((0, other_c * nx + x), (1, other_c * nx + other_x)):
            corewise(slab, j, q).wait_recv()

    def to_core(k):
        return remote(
            part.at[k, pl.ds(other_c * nx, nx)], core_in.at[k], core_s.at[k], core_r.at[k],
            inner=other_c,
        )

    def to_x(k, f):
        return remote(
            x_out.at[k, features(f)], x_in.at[k, features(f)], rx_s.at[k, f], rx_r.at[k, f],
            expert=other_x,
        )

    def to_z(k, f):
        return remote(
            z_out.at[k, features(f)], z_in.at[k, features(f)], rz_s.at[k, f], rz_r.at[k, f],
            wide=flip(z, k),
        )

    def reduce_core(k):
        to_core(k).wait_recv()
        for f in range(2):
            x_out[k, features(f)] = (
                part[k, c * nx + other_x, features(f)].astype(f32)
                + core_in[k, other_x, features(f)].astype(f32)
            ).astype(bf)
            to_x(k, f).start()

    def total_of(k, f):
        return (
            part[k, c * nx + x, features(f)].astype(f32)
            + core_in[k, x, features(f)].astype(f32)
            + x_in[k, features(f)].astype(f32)
        )

    def reduce_x(k, f):
        to_x(k, f).wait_recv()
        z_out[k, features(f)] = total_of(k, f).astype(bf)
        to_z(k, f).start()

    groups = held // TOGETHER

    def gating(i, k):
        side = (i % 2) * TOGETHER
        for q in range(quarters):
            lanes = slice(q * share, (q + 1) * share)
            weights = [
                [
                    gates[t * held + i * TOGETHER + j : t * held + i * TOGETHER + j + 1, lanes]
                    for j in range(TOGETHER)
                ]
                for t in range(tasks)
            ]
            for f in range(0, width, 16):
                outs = [made[side + j, f : f + 16, lanes] for j in range(TOGETHER)]
                for t in range(tasks):
                    span = slice(t * width + f, t * width + f + 16)
                    piece = weights[t][0] * outs[0]
                    for j in range(1, TOGETHER):
                        piece = piece + weights[t][j] * outs[j]
                    if i > 0:
                        piece = piece + acc[q, span, :]
                    if i < groups - 1:
                        acc[q, span, :] = piece
                    else:
                        part[k, q, span, :] = piece.astype(bf)

    def stage(i, data, k):
        if i < groups:
            for j in range(TOGETHER):
                e = i * TOGETHER + j
                hidden[(i % 2) * TOGETHER + j] = jnp.maximum(
                    jnp.dot(data, win[e], preferred_element_type=f32), 0.0
                ).astype(bf)
        if 0 < i <= groups:
            side = ((i - 1) % 2) * TOGETHER
            for j in range(TOGETHER):
                e = (i - 1) * TOGETHER + j
                made[side + j] = lax.dot_general(
                    wout[e], hidden[side + j], (((1,), (1,)), ((), ())),
                    preferred_element_type=f32,
                )
        if i > 1:
            gating(i - 2, k)

    agenda = (
        (0, 0, lambda: arrive_z(1, 0)),
        (0, 2, lambda: arrive_z(1, 1)),
        (0, 4, lambda: arrive_z(2, 0)),
        (1, 2, lambda: arrive_z(3, 0)),
        (1, 4, lambda: arrive_z(3, 1)),
        (1, 5, lambda: reduce_core(0)),
        (2, 1, lambda: reduce_core(1)),
        (3, 1, lambda: reduce_core(2)),
        (3, 2, lambda: reduce_x(1, 0)),
        (3, 3, lambda: reduce_x(1, 1)),
        (3, 5, lambda: reduce_x(2, 0)),
    )

    def step(k, carry):
        slab = flip(z, k)
        data = xbuf[slab].reshape(rows, depth)
        logits = lax.dot_general(
            gate_ref[...], data, (((0,), (1,)), ((), ())), preferred_element_type=f32
        )
        logits = logits.reshape(tasks, logits.shape[0] // tasks, rows)
        powers = jnp.exp(logits - jnp.max(logits, axis=1, keepdims=True))
        gates_all[...] = powers / jnp.sum(powers, axis=1, keepdims=True)
        for t in range(tasks):
            gates[t * held : (t + 1) * held, :] = gates_all[
                t, pl.ds(pl.multiple_of(x * held, held), held), :
            ]
        after = flip(z, k + 1)
        for i in range(groups + 2):
            for moment, boundary, action in agenda:
                if boundary == i:
                    pl.when(k == moment)(action)
            if i > 0:
                data = xbuf[slab].reshape(rows, depth)
            stage(i, data, k)
        to_core(k).start()

        @pl.when(k == 0)
        def _():
            arrive_z(2, 1)

        @pl.when(k < nz - 1)
        def _():
            arrive_x(after)
            arrive_c(after)

        return carry

    lax.fori_loop(0, nz, step, 0)
    reduce_x(2, 1)
    reduce_core(3)
    for f in range(2):
        reduce_x(3, f)
    totals = []
    for f in range(2):
        to_x(0, f).wait_recv()
        total = total_of(0, f)
        for k in range(1, nz):
            to_z(k, f).wait_recv()
            total = total + z_in[k, features(f)].astype(f32)
        totals.append(total)
    total = jnp.concatenate(totals, axis=0)
    total = total.T
    center = jnp.mean(total, axis=1, keepdims=True)
    spread = jnp.mean(jnp.square(total - center), axis=1, keepdims=True)
    gain = gain_ref[...].astype(f32)
    gain = jnp.concatenate([gain[i : i + 1, :] for i in range(gain.shape[0])], axis=1)
    normed = (total - center) * lax.rsqrt(spread + 1e-05) * gain
    nb[x, c] = normed.astype(bf)
    yield
    for d in range(nz - 1):
        for h in range(2):

            @pl.when((z < nz - 1) & (z - d >= 0))
            def _():
                upward(xbuf.at[z, spot], z, d, h).wait_send()

            @pl.when((z > 0) & (z + d < nz))
            def _():
                downward(xbuf.at[z, spot], z, d, h).wait_send()

    for k in range(1, nz):
        slab = flip(z, k)
        corewise(slab, 0, spot).wait_send()
        corewise(slab, 1, spot).wait_send()
        for h in range(2):
            sideways(slab, spot, h).wait_send()
            to_z(k, h).wait_send()
    for k in range(nz):
        to_core(k).wait_send()
        for f in range(2):
            to_x(k, f).wait_send()


def greet_all():
    (z, x, c), (nz, nx, nc) = place()
    barrier = pltpu.get_barrier_semaphore()
    pl.semaphore_signal(
        barrier, inc=1, device_id={"expert": 1 - x, "inner": 1 - c}, device_id_type=MESH
    )
    for axis, here, size in zip(ALL, (z, x, c), (nz, nx, nc)):
        for turned in range(1, size):
            pl.semaphore_signal(
                barrier, inc=1, device_id={axis: turn(here, turned, size)}, device_id_type=MESH
            )
    pl.semaphore_wait(barrier, nz + nx + nc - 2)


def whole_kernel(
    tasks, mix_count, cand_ref, gate_ref, win_hbm, wout_hbm, gain_ref,
    q_hbm, k_hbm, v_hbm, task_ref, attn_ref, id_ref, out_ref, *scratch
):
    nb = scratch[mix_count]
    mix = mix_part(
        tasks, cand_ref, gate_ref, win_hbm, wout_hbm, gain_ref, nb, *scratch[:mix_count]
    )
    score = score_part(
        q_hbm, k_hbm, v_hbm, task_ref, attn_ref, id_ref, out_ref, *scratch[mix_count:]
    )
    next(score)
    next(mix)
    next(score, None)
    next(mix, None)


def score_part(
    q_hbm, k_hbm, v_hbm, task_ref, attn_ref, id_ref, out_ref,
    nb, q_ref, k_ref, v_ref, keys, extra, ids, queries, powers, high, sums, partial,
    load_sem, n_s, n_r, id_s, id_r, up_s, down_s, key_r, p_s, p_r,
):
    (z, x, c), (nz, nx, nc) = place()
    f32, bf = jnp.float32, jnp.bfloat16
    other_x, other_c = 1 - x, 1 - c
    _, _, share, depth = nb.shape
    rows = nx * nc * share
    both = nc * share
    heads = queries.shape[0]
    tasks = task_ref.shape[0]
    loads = [
        pltpu.make_async_copy(k_hbm, k_ref, load_sem.at[0]),
        pltpu.make_async_copy(v_hbm, v_ref, load_sem.at[1]),
        pltpu.make_async_copy(q_hbm, q_ref, load_sem.at[2]),
    ]
    for item in loads:
        item.start()
    yield

    def give(side, core, j, **where):
        return remote(nb.at[side, core], nb.at[side, core], n_s.at[j], n_r.at[j], **where)

    first = give(x, c, 0, expert=other_x)
    second = give(x, c, 1, inner=other_c)
    third = give(other_x, c, 2, inner=other_c)
    first.start()
    second.start()
    id_copies = []
    for turned in range(1, nz):
        target = turn(z, turned, nz)
        item = remote(id_ref, ids.at[z], id_s.at[turned], id_r.at[z], wide=target)
        item.start()
        id_copies.append(item)
    ids[z] = id_ref[...]
    for item in loads:
        item.wait()
    own = jnp.concatenate([id_ref[q] for q in range(nx * nc)], axis=1).astype(f32)
    lifted = heads * tasks
    extra[:, :, lifted:, :] = jnp.ones((nz, nx, 16, both), bf)
    shape = (lifted, heads * HD)
    row = lax.broadcasted_iota(jnp.int32, shape, 0) // tasks
    column = lax.broadcasted_iota(jnp.int32, shape, 1) // HD
    stacked = jnp.concatenate([attn_ref[...].astype(f32)] * heads, axis=0)
    blocks = jnp.where(row == column, stacked, 0.0).astype(bf)
    sides = (x, other_x)

    def parts(slab, m):
        return [keys.at[slab, sides[m]], extra.at[slab, sides[m], pl.ds(0, lifted)]]

    def upward(slab, d, m, j):
        piece = parts(slab, m)[j]
        return remote(piece, piece, up_s.at[d, m, j], key_r.at[slab, m, j], wide=z + 1)

    def downward(slab, d, m, j):
        piece = parts(slab, m)[j]
        return remote(piece, piece, down_s.at[d, m, j], key_r.at[slab, m, j], wide=z - 1)

    def announce(m, j):
        @pl.when(z < nz - 1)
        def _():
            upward(z, 0, m, j).start()

        @pl.when(z > 0)
        def _():
            downward(z, 0, m, j).start()

    def pass_on(d, m):
        for slab, here, further, way in (
            (z - d, z - d >= 0, z < nz - 1, upward),
            (z + d, z + d < nz, z > 0, downward),
        ):

            @pl.when(here)
            def _():
                for j in range(2):
                    way(slab, 0, m, j).wait_recv()

                    @pl.when(further)
                    def _():
                        way(slab, d, m, j).start()

    def make(m):
        data = nb[sides[m]].reshape(both, depth)
        keys[z, sides[m]] = jnp.dot(data, k_ref[...], preferred_element_type=f32).astype(bf)
        announce(m, 0)
        values = jnp.dot(data, v_ref[...], preferred_element_type=f32).astype(bf)
        extra[z, sides[m], :lifted, :] = lax.dot_general(
            blocks, values, (((1,), (1,)), ((), ())), preferred_element_type=f32
        ).astype(bf)
        announce(m, 1)

    give(x, other_c, 1, inner=other_c).wait_recv()
    make(0)
    give(other_x, c, 0, expert=other_x).wait_recv()
    third.start()
    pass_on(1, 0)
    give(other_x, other_c, 2, inner=other_c).wait_recv()
    make(1)
    data = jnp.concatenate([nb[q % nx, q // nx] for q in range(nx * nc)], axis=0)
    made = jnp.dot(data, q_ref[...], preferred_element_type=f32) * (1.0 / math.sqrt(HD))
    lane = lax.broadcasted_iota(jnp.int32, (rows, 2 * HD), 1)
    for h in range(heads):
        pair = made[:, h // 2 * 2 * HD : (h // 2 + 1) * 2 * HD]
        queries[h] = jnp.where(lane // HD == h % 2, pair, 0.0).astype(bf)
    for item in id_copies:
        item.wait_send()
    for turned in range(1, nz):
        source = turn(z, turned, nz)
        remote(id_ref, ids.at[source], id_s.at[turned], id_r.at[source], wide=source).wait_recv()

    def attend(slab, m, fresh=False):
        side = sides[m]
        theirs = jnp.concatenate([ids[slab, side], ids[slab, nx + side]], axis=1).astype(f32)
        same = jnp.broadcast_to(theirs, (8, both)).T[:, :1] == own
        tops = []
        for h in range(heads):
            pair = slice(h // 2 * 2 * HD, (h // 2 + 1) * 2 * HD)
            affinity = lax.dot_general(
                keys[slab, side][:, pair], queries[h], (((1,), (1,)), ((), ())),
                preferred_element_type=f32,
            )
            affinity = jnp.where(same, affinity, -1e30)
            top = jnp.max(affinity, axis=0, keepdims=True)
            powers[h] = jnp.exp(affinity - top).astype(bf)
            tops.append(top)
        for h in range(heads):
            got = jnp.dot(extra[slab, side], powers[h], preferred_element_type=f32)
            if fresh:
                high[h] = tops[h]
                sums[h] = got
            else:
                peak = jnp.maximum(high[h], tops[h])
                sums[h] = sums[h] * jnp.exp(high[h] - peak) + got * jnp.exp(tops[h] - peak)
                high[h] = peak

    attend(z, 0, True)
    attend(z, 1)
    pass_on(1, 1)
    attend(flip(z, 1), 0)
    pass_on(2, 0)
    attend(flip(z, 1), 1)
    pass_on(2, 1)
    attend(flip(z, 2), 0)
    attend(flip(z, 2), 1)
    pass_on(3, 0)
    attend(flip(z, 3), 0)
    pass_on(3, 1)
    attend(flip(z, 3), 1)
    result = None
    for h in range(heads):
        term = sums[h, h * tasks : (h + 1) * tasks] / sums[h, lifted : lifted + 1]
        result = term if result is None else result + term
    partial[0] = jnp.concatenate([result, jnp.zeros((8 - tasks, rows), f32)], axis=0)
    sends = []
    for j, where in enumerate(
        ({"inner": other_c}, {"expert": other_x}, {"expert": other_x, "inner": other_c})
    ):
        item = remote(partial.at[0], partial.at[j + 1], p_s.at[j], p_r.at[j], **where)
        item.start()
        sends.append(item)
    base = lax.dot_general(
        task_ref[...], data, (((1,), (1,)), ((), ())), preferred_element_type=f32
    )
    for item in sends:
        item.wait()
    everything = (partial[0] + partial[1]) + (partial[2] + partial[3])
    out_ref[...] = everything[:tasks, :] + base
    first.wait_send()
    second.wait_send()
    third.wait_send()
    for d in range(nz - 1):
        for m in range(2):
            for j in range(2):

                @pl.when((z < nz - 1) & (z - d >= 0))
                def _():
                    upward(z, d, m, j).wait_send()

                @pl.when((z > 0) & (z + d < nz))
                def _():
                    downward(z, d, m, j).wait_send()


def run_whole(
    cand, gate_weight, expert_in, expert_out, gain, query, key, value, task, attn, request_of,
    collective,
):
    nz, nx, nc = (lax.axis_size(a) for a in ALL)
    rows, depth = cand.shape
    quarters = nx * nc
    share = rows // quarters
    held, _, units = expert_in.shape
    width = expert_out.shape[1]
    tasks = task.shape[1]
    dma = pltpu.SemaphoreType.DMA
    f32, bf = jnp.float32, jnp.bfloat16
    vmem = pl.BlockSpec(memory_space=pltpu.VMEM)
    anywhere = pl.BlockSpec(memory_space=pl.ANY)
    model = tasks * width
    experts_all = gate_weight.shape[1] // tasks
    lanes = query.shape[1]
    heads = lanes // HD
    mix_scratch = [
        pltpu.VMEM((nz, quarters, share, depth), bf),
        pltpu.VMEM(expert_in.shape, bf),
        pltpu.VMEM(expert_out.shape, bf),
        pltpu.VMEM((tasks, experts_all, rows), f32),
        pltpu.VMEM((tasks * held, rows), f32),
        pltpu.VMEM((2 * TOGETHER, rows, units), bf),
        pltpu.VMEM((2 * TOGETHER, width, rows), f32),
        pltpu.VMEM((quarters, model, share), f32),
        pltpu.VMEM((nz, quarters, model, share), bf),
        pltpu.VMEM((nz, nx, model, share), bf),
        pltpu.VMEM((nz, model, share), bf),
        pltpu.VMEM((nz, model, share), bf),
        pltpu.VMEM((nz, model, share), bf),
        pltpu.VMEM((nz, model, share), bf),
        dma((3,)),
        dma((nz, 2)),
        dma((nz, 2)),
        dma((nz, 2)),
        dma((nz, 2)),
        dma((nz, 2)),
        dma((nz, 2)),
        dma((nz, 2)),
        dma((nz,)),
        dma((nz,)),
        dma((nz, 2)),
        dma((nz, 2)),
        dma((nz, 2)),
        dma((nz, 2)),
    ]
    columns = heads * tasks + 16
    score_scratch = [
        pltpu.VMEM((nx, nc, share, model), bf),
        pltpu.VMEM(query.shape, bf),
        pltpu.VMEM(key.shape, bf),
        pltpu.VMEM(value.shape, bf),
        pltpu.VMEM((nz, nx, nc * share, lanes), bf),
        pltpu.VMEM((nz, nx, columns, nc * share), bf),
        pltpu.VMEM((nz, quarters, 1, share), jnp.int32),
        pltpu.VMEM((heads, rows, 2 * HD), bf),
        pltpu.VMEM((heads, nc * share, rows), bf),
        pltpu.VMEM((heads, 1, rows), f32),
        pltpu.VMEM((heads, columns, rows), f32),
        pltpu.VMEM((nx * nc, 8, rows), f32),
        dma((3,)),
        dma((3,)),
        dma((3,)),
        dma((nz,)),
        dma((nz,)),
        dma((nz, 2, 2)),
        dma((nz, 2, 2)),
        dma((nz, 2, 2)),
        dma((3,)),
        dma((3,)),
    ]
    return pl.pallas_call(
        functools.partial(whole_kernel, tasks, len(mix_scratch)),
        in_specs=[anywhere, vmem, anywhere, anywhere, vmem, anywhere, anywhere, anywhere]
        + [vmem] * 3,
        out_specs=vmem,
        out_shape=jax.ShapeDtypeStruct((tasks, rows), f32),
        scratch_shapes=mix_scratch + score_scratch,
        compiler_params=pltpu.CompilerParams(
            collective_id=collective, has_side_effects=True, vmem_limit_bytes=VMEM_LIMIT
        ),
    )(
        cand.reshape(quarters, share, depth), gate_weight, expert_in, expert_out,
        gain.reshape(-1, 128), query, key, value, task.T, attn.T,
        request_of.reshape(quarters, 1, share),
    ).T


def fused(sizes, rows, heads, held):
    return sizes == (4, 2, 2) and rows % 512 == 0 and heads == 4 and held % (2 * TOGETHER) == 0


def local(
    candidates,
    gate_weight,
    expert_in,
    expert_out,
    norm_gain,
    query_weight,
    key_weight,
    value_weight,
    task_weight,
    attn_weight,
    request_of,
):
    rows = candidates.shape[0]
    tasks = task_weight.shape[1]
    nz, nx, nc = (lax.axis_size(a) for a in ALL)
    if fused((nz, nx, nc), rows, query_weight.shape[1] // HD, expert_in.shape[0]):
        return run_whole(
            candidates, gate_weight, expert_in, expert_out, norm_gain, query_weight, key_weight,
            value_weight, task_weight, attn_weight, request_of, 3,
        )
    share = rows // (nx * nc)
    spot = lax.axis_index("inner") * nx + lax.axis_index("expert")
    wide = lax.axis_index("wide")
    quarter = lax.dynamic_slice_in_dim(candidates, spot * share, share, 0)
    everyone, requests = run_gather(quarter, request_of[None, :], 0)
    partial_mix = run_experts(everyone, gate_weight, expert_in, expert_out, tasks)
    normed = run_reduce(partial_mix, norm_gain[None, :], share, 1)
    normed_all = run_gather(normed, None, 2)
    own = lax.dynamic_slice_in_dim(normed_all, wide * rows, rows, 0)
    queries = jnp.dot(own, query_weight, preferred_element_type=jnp.float32).astype(jnp.bfloat16)
    keys = jnp.dot(normed_all, key_weight, preferred_element_type=jnp.float32).astype(jnp.bfloat16)
    values = jnp.dot(normed_all, value_weight, preferred_element_type=jnp.float32).astype(
        jnp.bfloat16
    )
    term = run_attention(
        queries, keys, values, request_of[:, None], requests, attn_weight
    )
    attention = lax.psum(term.T, ("expert", "inner")).T
    return jnp.dot(own, task_weight, preferred_element_type=jnp.float32) + attention


def solution(mesh):
    return jax.shard_map(
        local,
        mesh=mesh,
        in_specs=(
            P(("groups", "wide"), None),
            P(),
            P("expert", None, ("wide", "inner")),
            P("expert", None, ("wide", "inner")),
            P(),
            P(None, ("expert", "inner")),
            P(None, ("expert", "inner")),
            P(None, ("expert", "inner")),
            P(),
            P(("expert", "inner"), None),
            P(("groups", "wide")),
        ),
        out_specs=P(("groups", "wide"), None),
        check_vma=False,
    )
```

```python
import functools
import math

import jax
import jax.numpy as jnp
from jax import lax
from jax.experimental import pallas as pl
from jax.experimental.pallas import tpu as pltpu
from jax.sharding import PartitionSpec as P

HD = 64
ALL = ("wide", "expert", "inner")
VMEM_LIMIT = 60 * 1024 * 1024


MESH = pl.DeviceIdType.MESH


def place():
    return tuple(lax.axis_index(a) for a in ALL), tuple(lax.axis_size(a) for a in ALL)


def turn(start, step, size):
    return lax.rem(start + step, size)


def greet():
    mine, sizes = place()
    barrier = pltpu.get_barrier_semaphore()
    for axis, here, size in zip(ALL, mine, sizes):
        for step in range(1, size):
            pl.semaphore_signal(
                barrier, inc=1, device_id={axis: turn(here, step, size)}, device_id_type=MESH
            )
    pl.semaphore_wait(barrier, sum(sizes) - len(sizes))


def gather_kernel(with_ids, *refs):
    if with_ids:
        own_ref, id_ref, out_ref, ids_ref, recv, send_z, send_x, send_c, local_sem, id_r, id_s = refs
    else:
        own_ref, out_ref, recv, send_z, send_x, send_c, local_sem = refs
    (z, x, c), (nz, nx, nc) = place()
    greet()

    def copy(src, zs, xs, cs, sem, axis, target):
        return pltpu.make_async_remote_copy(
            src_ref=src,
            dst_ref=out_ref.at[zs, cs, xs],
            send_sem=sem,
            recv_sem=recv.at[zs, cs, xs],
            device_id={axis: target},
            device_id_type=MESH,
        )

    def arrived(zs, xs, cs):
        copy(out_ref.at[zs, cs, xs], zs, xs, cs, send_z.at[0], "inner", turn(c, 1, nc)).wait_recv()

    sent = []

    def push(*what):
        item = copy(*what)
        item.start()
        sent.append(item)

    def spread_x(src, k, zs):
        for step in range(1, nx):
            push(src, zs, x, c, send_x.at[k, step - 1], "expert", turn(x, step, nx))

    def spread_c(src, k, j, zs, xs):
        for step in range(1, nc):
            push(src, zs, xs, c, send_c.at[k, j, step - 1], "inner", turn(c, step, nc))

    for step in range(1, nz):
        push(own_ref, z, x, c, send_z.at[step - 1], "wide", turn(z, step, nz))
    spread_x(own_ref, 0, z)
    spread_c(own_ref, 0, 0, z, x)
    keep = pltpu.make_async_copy(own_ref, out_ref.at[z, c, x], local_sem.at[0])
    keep.start()
    if with_ids:
        id_copies = []
        for step in range(1, nz):
            item = pltpu.make_async_remote_copy(
                src_ref=id_ref,
                dst_ref=ids_ref.at[z],
                send_sem=id_s.at[step - 1],
                recv_sem=id_r.at[z],
                device_id={"wide": turn(z, step, nz)},
                device_id_type=MESH,
            )
            item.start()
            id_copies.append(item)
        ids_ref[z] = id_ref[...]

    def pass_x(k):
        zs = turn(z, k, nz)
        for step in range(1, nx):
            xs = turn(x, step, nx)
            arrived(zs, xs, c)
            spread_c(out_ref.at[zs, c, xs], k, step, zs, xs)

    for k in range(1, nz):
        zs = turn(z, k, nz)
        arrived(zs, x, c)
        spread_x(out_ref.at[zs, c, x], k, zs)
        spread_c(out_ref.at[zs, c, x], k, 0, zs, x)
        pass_x(k - 1)
    pass_x(nz - 1)
    for k in range(nz):
        for j in range(nx):
            for step in range(1, nc):
                arrived(turn(z, k, nz), turn(x, j, nx), turn(c, step, nc))
    for item in sent:
        item.wait_send()
    keep.wait()
    if with_ids:
        for step in range(1, nz):
            zs = turn(z, step, nz)
            pltpu.make_async_remote_copy(
                src_ref=id_ref,
                dst_ref=ids_ref.at[zs],
                send_sem=id_s.at[step - 1],
                recv_sem=id_r.at[zs],
                device_id={"wide": zs},
                device_id_type=MESH,
            ).wait_recv()
        for item in id_copies:
            item.wait_send()


def run_gather(own, ids, collective):
    nz, nx, nc = (lax.axis_size(a) for a in ALL)
    dma = pltpu.SemaphoreType.DMA
    with_ids = ids is not None
    shape = jax.ShapeDtypeStruct((nz, nc, nx) + own.shape, own.dtype)
    vmem = pl.BlockSpec(memory_space=pltpu.VMEM)
    anywhere = pl.BlockSpec(memory_space=pl.ANY)
    scratch = [
        dma((nz, nc, nx)),
        dma((max(nz - 1, 1),)),
        dma((nz, max(nx - 1, 1))),
        dma((nz, nx, max(nc - 1, 1))),
        dma((1,)),
    ]
    if with_ids:
        scratch += [dma((nz,)), dma((max(nz - 1, 1),))]
    out = pl.pallas_call(
        functools.partial(gather_kernel, with_ids),
        in_specs=[vmem, vmem] if with_ids else [vmem],
        out_specs=[anywhere, vmem] if with_ids else anywhere,
        out_shape=[shape, jax.ShapeDtypeStruct((nz,) + ids.shape, ids.dtype)] if with_ids else shape,
        scratch_shapes=scratch,
        compiler_params=pltpu.CompilerParams(collective_id=collective, has_side_effects=True),
    )(*([own, ids] if with_ids else [own]))
    depth = own.shape[1]
    if with_ids:
        return out[0].reshape(-1, depth), out[1].reshape(1, -1)
    return out.reshape(-1, depth)


def reduce_kernel(
    part_ref, gain_ref, out_ref, mine, core_in, x_out, x_in, z_out, z_in,
    local_sem, core_s, core_r, x_s, x_r, z_s, z_r,
):
    (z, x, c), (nz, nx, nc) = place()
    f32 = jnp.float32
    greet()
    other = turn(c, 1, nc)
    core, kept = [], []
    for k in range(nz):
        s = turn(z, k + 1, nz)
        item = pltpu.make_async_remote_copy(
            src_ref=part_ref.at[s, other],
            dst_ref=core_in.at[k],
            send_sem=core_s.at[k],
            recv_sem=core_r.at[k],
            device_id={"inner": other},
            device_id_type=MESH,
        )
        item.start()
        core.append(item)
        stay = pltpu.make_async_copy(part_ref.at[s, c], mine.at[k], local_sem.at[k])
        stay.start()
        kept.append(stay)

    def pair(k, xs):
        return mine[k, xs].astype(f32) + core_in[k, xs].astype(f32)

    across, along = [], []

    def finish(k):
        total = pair(k, x)
        for step in range(1, nx):
            across[k][step - 1].wait_recv()
            total = total + x_in[k, step - 1].astype(f32)
        if k == nz - 1:
            return total
        z_out[k] = total.astype(z_out.dtype)
        item = pltpu.make_async_remote_copy(
            src_ref=z_out.at[k],
            dst_ref=z_in.at[k],
            send_sem=z_s.at[k],
            recv_sem=z_r.at[k],
            device_id={"wide": turn(z, k + 1, nz)},
            device_id_type=MESH,
        )
        item.start()
        along.append(item)

    for k in range(nz):
        kept[k].wait()
        core[k].wait_recv()
        items = []
        for step in range(1, nx):
            xs = turn(x, step, nx)
            x_out[k, step - 1] = pair(k, xs).astype(x_out.dtype)
            item = pltpu.make_async_remote_copy(
                src_ref=x_out.at[k, step - 1],
                dst_ref=x_in.at[k, step - 1],
                send_sem=x_s.at[k, step - 1],
                recv_sem=x_r.at[k, step - 1],
                device_id={"expert": xs},
                device_id_type=MESH,
            )
            item.start()
            items.append(item)
        across.append(items)
        if k > 0:
            finish(k - 1)
    total = finish(nz - 1)
    for k in range(nz - 1):
        along[k].wait_recv()
        total = total + z_in[k].astype(f32)
    center = jnp.mean(total, axis=1, keepdims=True)
    spread = jnp.mean(jnp.square(total - center), axis=1, keepdims=True)
    normed = (total - center) * lax.rsqrt(spread + 1e-05) * gain_ref[...].astype(f32)
    out_ref[...] = normed.astype(out_ref.dtype)
    for item in core + along + [i for items in across for i in items]:
        item.wait_send()


def run_reduce(part, gain, share, collective):
    nz, nx, nc = (lax.axis_size(a) for a in ALL)
    width = part.shape[1]
    dma = pltpu.SemaphoreType.DMA
    kind = part.dtype
    part = part.reshape(nz, nc, nx, share, width)
    few = max(nx - 1, 1)
    vmem = pl.BlockSpec(memory_space=pltpu.VMEM)
    return pl.pallas_call(
        reduce_kernel,
        in_specs=[pl.BlockSpec(memory_space=pl.ANY), vmem],
        out_specs=vmem,
        out_shape=jax.ShapeDtypeStruct((share, width), kind),
        scratch_shapes=[
            pltpu.VMEM((nz, nx, share, width), kind),
            pltpu.VMEM((nz, nx, share, width), kind),
            pltpu.VMEM((nz, few, share, width), kind),
            pltpu.VMEM((nz, few, share, width), kind),
            pltpu.VMEM((nz, share, width), kind),
            pltpu.VMEM((nz, share, width), kind),
            dma((nz,)),
            dma((nz,)),
            dma((nz,)),
            dma((nz, few)),
            dma((nz, few)),
            dma((nz,)),
            dma((nz,)),
        ],
        compiler_params=pltpu.CompilerParams(
            collective_id=collective, has_side_effects=True, vmem_limit_bytes=VMEM_LIMIT
        ),
    )(part, gain)


def expert_kernel(tasks, x_ref, gate_ref, win_ref, wout_ref, out_ref, acc_ref):
    rows = x_ref.shape[0]
    columns = gate_ref.shape[1]
    experts_all = columns // tasks
    held, _, _ = win_ref.shape
    width = wout_ref.shape[1]
    x = x_ref[...]
    logits = jnp.dot(x, gate_ref[...], preferred_element_type=jnp.float32)
    task = lax.broadcasted_iota(jnp.int32, (rows, columns), 1) // experts_all
    top = jnp.zeros_like(logits)
    for t in range(tasks):
        high = jnp.max(jnp.where(task == t, logits, -jnp.inf), axis=1, keepdims=True)
        top = jnp.where(task == t, high, top)
    powers = jnp.exp(logits - top)
    total = jnp.ones_like(logits)
    for t in range(tasks):
        part = jnp.sum(jnp.where(task == t, powers, 0.0), axis=1, keepdims=True)
        total = jnp.where(task == t, part, total)
    gates = powers / total
    shift = lax.rem(columns - lax.axis_index("expert") * held, columns)
    gates = pltpu.roll(gates, shift, 1)
    together = min(4, held)
    for first in range(0, held, together):
        made = []
        for e in range(first, first + together):
            hidden = jnp.maximum(
                jnp.dot(x, win_ref[e], preferred_element_type=jnp.float32), 0.0
            ).astype(jnp.bfloat16)
            made.append(
                lax.dot_general(
                    hidden,
                    wout_ref[e],
                    (((1,), (1,)), ((), ())),
                    preferred_element_type=jnp.float32,
                )
            )
        for t in range(tasks):
            piece = None
            for j, output in enumerate(made):
                lane = t * experts_all + first + j
                term = gates[:, lane : lane + 1] * output
                piece = term if piece is None else piece + term
            span = slice(t * width, (t + 1) * width)
            if first > 0:
                piece = piece + acc_ref[:, span]
            if first + together < held:
                acc_ref[:, span] = piece
            else:
                out_ref[:, span] = piece.astype(out_ref.dtype)


def run_experts(x, gate_weight, expert_in, expert_out, tasks):
    rows, depth = x.shape
    held, _, units = expert_in.shape
    width = expert_out.shape[1]
    block = min(512, rows)
    return pl.pallas_call(
        functools.partial(expert_kernel, tasks),
        grid=(rows // block,),
        in_specs=[
            pl.BlockSpec((block, depth), lambda i: (i, 0)),
            pl.BlockSpec(gate_weight.shape, lambda i: (0, 0)),
            pl.BlockSpec(expert_in.shape, lambda i: (0, 0, 0), pipeline_mode=pl.Buffered(1)),
            pl.BlockSpec(expert_out.shape, lambda i: (0, 0, 0), pipeline_mode=pl.Buffered(1)),
        ],
        out_specs=pl.BlockSpec((block, tasks * width), lambda i: (i, 0)),
        out_shape=jax.ShapeDtypeStruct((rows, tasks * width), jnp.bfloat16),
        scratch_shapes=[pltpu.VMEM((block, tasks * width), jnp.float32)],
        compiler_params=pltpu.CompilerParams(vmem_limit_bytes=VMEM_LIMIT),
    )(x, gate_weight, expert_in, expert_out)


def attention_kernel(q_ref, k_ref, v_ref, own_ref, all_ref, weight_ref, out_ref):
    same = own_ref[...] == all_ref[...]
    factor = 1.0 / math.sqrt(HD)
    result = None
    for first in range(0, q_ref.shape[1], HD):
        span = slice(first, first + HD)
        affinity = (
            lax.dot_general(
                q_ref[:, span],
                k_ref[:, span],
                (((1,), (1,)), ((), ())),
                preferred_element_type=jnp.float32,
            )
            * factor
        )
        affinity = jnp.where(same, affinity, -1e30)
        highest = jnp.max(affinity, axis=1, keepdims=True)
        powers = jnp.exp(affinity - highest)
        total = jnp.sum(powers, axis=1, keepdims=True)
        context = jnp.dot(
            powers.astype(jnp.bfloat16), v_ref[:, span], preferred_element_type=jnp.float32
        )
        context = (context / total).astype(jnp.bfloat16)
        term = jnp.dot(context, weight_ref[span, :], preferred_element_type=jnp.float32)
        result = term if result is None else result + term
    out_ref[...] = result


def run_attention(q, k, v, own, every, weight):
    rows, width = q.shape
    keys = k.shape[0]
    tasks = weight.shape[1]
    block = min(128, rows)
    return pl.pallas_call(
        attention_kernel,
        grid=(rows // block,),
        in_specs=[
            pl.BlockSpec((block, width), lambda i: (i, 0)),
            pl.BlockSpec((keys, width), lambda i: (0, 0)),
            pl.BlockSpec((keys, width), lambda i: (0, 0)),
            pl.BlockSpec((block, 1), lambda i: (i, 0)),
            pl.BlockSpec((1, keys), lambda i: (0, 0)),
            pl.BlockSpec((width, tasks), lambda i: (0, 0)),
        ],
        out_specs=pl.BlockSpec((block, tasks), lambda i: (i, 0)),
        out_shape=jax.ShapeDtypeStruct((rows, tasks), jnp.float32),
        compiler_params=pltpu.CompilerParams(vmem_limit_bytes=VMEM_LIMIT),
    )(q, k, v, own, every, weight)


def flip(position, step):
    low = lax.rem(position, 2)
    high = position // 2
    return (high + (step // 2) * (1 - 2 * high)) * 2 + low + lax.rem(step, 2) * (1 - 2 * low)


def remote(src, dst, send, recv, **where):
    return pltpu.make_async_remote_copy(
        src_ref=src, dst_ref=dst, send_sem=send, recv_sem=recv, device_id=where,
        device_id_type=MESH,
    )


TOGETHER = 2


def mix_part(
    tasks, cand_ref, gate_ref, win_hbm, wout_hbm, gain_ref, nb,
    xbuf, win, wout, gates_all, gates, hidden, made, acc, part, core_in, x_out, x_in, z_out, z_in,
    load_sem, up_s, down_s, z_r, x_s, x_r, c_s, c_r, core_s, core_r, rx_s, rx_r, rz_s, rz_r,
):
    (z, x, c), (nz, nx, nc) = place()
    f32, bf = jnp.float32, jnp.bfloat16
    other_x, other_c = 1 - x, 1 - c
    held = win.shape[0]
    quarters, share, depth = xbuf.shape[1:]
    rows = quarters * share
    width = wout.shape[1]
    spot = c * nx + x
    loads = [
        pltpu.make_async_copy(cand_ref, xbuf.at[z], load_sem.at[0]),
        pltpu.make_async_copy(win_hbm, win, load_sem.at[1]),
        pltpu.make_async_copy(wout_hbm, wout, load_sem.at[2]),
    ]
    for item in loads:
        item.start()
    greet_all()

    piece_rows = share // 2
    half_model = part.shape[2] // 2

    def rows_of(h):
        return pl.ds(h * piece_rows, piece_rows)

    def features(f):
        return pl.ds(f * half_model, half_model)

    def upward(src, slab, d, h):
        return remote(
            src.at[rows_of(h)], xbuf.at[slab, spot, rows_of(h)], up_s.at[d, h], z_r.at[slab, h],
            wide=z + 1,
        )

    def downward(src, slab, d, h):
        return remote(
            src.at[rows_of(h)], xbuf.at[slab, spot, rows_of(h)], down_s.at[d, h],
            z_r.at[slab, h], wide=z - 1,
        )

    def sideways(slab, q, h):
        piece = xbuf.at[slab, q, rows_of(h)]
        return remote(piece, piece, x_s.at[slab, h], x_r.at[slab, h], expert=other_x)

    def corewise(slab, j, q):
        piece = xbuf.at[slab, q]
        return remote(piece, piece, c_s.at[slab, j], c_r.at[slab, j], inner=other_c)

    for h in range(2):

        @pl.when(z < nz - 1)
        def _():
            upward(cand_ref.at[spot], z, 0, h).start()

        @pl.when(z > 0)
        def _():
            downward(cand_ref.at[spot], z, 0, h).start()

    for item in loads:
        item.wait()

    def arrive_z(d, h):
        below, above = z - d, z + d

        @pl.when(below >= 0)
        def _():
            upward(xbuf.at[below, spot], below, 0, h).wait_recv()

            @pl.when(z < nz - 1)
            def _():
                upward(xbuf.at[below, spot], below, d, h).start()

        @pl.when(above < nz)
        def _():
            downward(xbuf.at[above, spot], above, 0, h).wait_recv()

            @pl.when(z > 0)
            def _():
                downward(xbuf.at[above, spot], above, d, h).start()

        slab = flip(z, d)
        sideways(slab, spot, h).start()
        if h == 1:
            corewise(slab, 0, spot).start()

    def arrive_x(slab):
        q = c * nx + other_x
        for h in range(2):
            sideways(slab, q, h).wait_recv()
        corewise(slab, 1, q).start()

    def arrive_c(slab):
        for j, q in ((0, other_c * nx + x), (1, other_c * nx + other_x)):
            corewise(slab, j, q).wait_recv()

    def to_core(k):
        return remote(
            part.at[k, pl.ds(other_c * nx, nx)], core_in.at[k], core_s.at[k], core_r.at[k],
            inner=other_c,
        )

    def to_x(k, f):
        return remote(
            x_out.at[k, features(f)], x_in.at[k, features(f)], rx_s.at[k, f], rx_r.at[k, f],
            expert=other_x,
        )

    def to_z(k, f):
        return remote(
            z_out.at[k, features(f)], z_in.at[k, features(f)], rz_s.at[k, f], rz_r.at[k, f],
            wide=flip(z, k),
        )

    def reduce_core(k):
        to_core(k).wait_recv()
        for f in range(2):
            x_out[k, features(f)] = (
                part[k, c * nx + other_x, features(f)].astype(f32)
                + core_in[k, other_x, features(f)].astype(f32)
            ).astype(bf)
            to_x(k, f).start()

    def total_of(k, f):
        return (
            part[k, c * nx + x, features(f)].astype(f32)
            + core_in[k, x, features(f)].astype(f32)
            + x_in[k, features(f)].astype(f32)
        )

    def reduce_x(k, f):
        to_x(k, f).wait_recv()
        z_out[k, features(f)] = total_of(k, f).astype(bf)
        to_z(k, f).start()

    groups = held // TOGETHER

    def gating(i, k):
        side = (i % 2) * TOGETHER
        for q in range(quarters):
            lanes = slice(q * share, (q + 1) * share)
            weights = [
                [
                    gates[t * held + i * TOGETHER + j : t * held + i * TOGETHER + j + 1, lanes]
                    for j in range(TOGETHER)
                ]
                for t in range(tasks)
            ]
            for f in range(0, width, 16):
                outs = [made[side + j, f : f + 16, lanes] for j in range(TOGETHER)]
                for t in range(tasks):
                    span = slice(t * width + f, t * width + f + 16)
                    piece = weights[t][0] * outs[0]
                    for j in range(1, TOGETHER):
                        piece = piece + weights[t][j] * outs[j]
                    if i > 0:
                        piece = piece + acc[q, span, :]
                    if i < groups - 1:
                        acc[q, span, :] = piece
                    else:
                        part[k, q, span, :] = piece.astype(bf)

    def stage(i, data, k):
        if i < groups:
            for j in range(TOGETHER):
                e = i * TOGETHER + j
                hidden[(i % 2) * TOGETHER + j] = jnp.maximum(
                    jnp.dot(data, win[e], preferred_element_type=f32), 0.0
                ).astype(bf)
        if 0 < i <= groups:
            side = ((i - 1) % 2) * TOGETHER
            for j in range(TOGETHER):
                e = (i - 1) * TOGETHER + j
                made[side + j] = lax.dot_general(
                    wout[e], hidden[side + j], (((1,), (1,)), ((), ())),
                    preferred_element_type=f32,
                )
        if i > 1:
            gating(i - 2, k)

    agenda = (
        (0, 0, lambda: arrive_z(1, 0)),
        (0, 4, lambda: arrive_z(1, 1)),
        (0, 7, lambda: arrive_z(2, 0)),
        (1, 4, lambda: arrive_z(3, 0)),
        (1, 7, lambda: arrive_z(3, 1)),
        (1, 8, lambda: reduce_core(0)),
        (1, 9, lambda: arrive_x(flip(z, 2))),
        (2, 2, lambda: reduce_core(1)),
        (2, 6, lambda: arrive_x(flip(z, 3))),
        (3, 2, lambda: reduce_core(2)),
        (3, 4, lambda: reduce_x(1, 0)),
        (3, 5, lambda: reduce_x(1, 1)),
        (3, 9, lambda: reduce_x(2, 0)),
    )

    def step(k, carry):
        slab = flip(z, k)
        data = xbuf[slab].reshape(rows, depth)
        logits = lax.dot_general(
            gate_ref[...], data, (((0,), (1,)), ((), ())), preferred_element_type=f32
        )
        logits = logits.reshape(tasks, logits.shape[0] // tasks, rows)
        powers = jnp.exp(logits - jnp.max(logits, axis=1, keepdims=True))
        gates_all[...] = powers / jnp.sum(powers, axis=1, keepdims=True)
        for t in range(tasks):
            gates[t * held : (t + 1) * held, :] = gates_all[
                t, pl.ds(pl.multiple_of(x * held, held), held), :
            ]
        after = flip(z, k + 1)
        for i in range(groups + 2):
            for moment, boundary, action in agenda:
                if boundary == i:
                    pl.when(k == moment)(action)
            if i > 0:
                data = xbuf[slab].reshape(rows, depth)
            stage(i, data, k)
        to_core(k).start()

        @pl.when(k == 0)
        def _():
            arrive_z(2, 1)
            arrive_x(after)

        @pl.when(k < nz - 1)
        def _():
            arrive_c(after)

        return carry

    lax.fori_loop(0, nz, step, 0)
    reduce_x(2, 1)
    reduce_core(3)
    for f in range(2):
        reduce_x(3, f)
    totals = []
    for f in range(2):
        to_x(0, f).wait_recv()
        total = total_of(0, f)
        for k in range(1, nz):
            to_z(k, f).wait_recv()
            total = total + z_in[k, features(f)].astype(f32)
        totals.append(total)
    total = jnp.concatenate(totals, axis=0)
    total = total.T
    center = jnp.mean(total, axis=1, keepdims=True)
    spread = jnp.mean(jnp.square(total - center), axis=1, keepdims=True)
    gain = gain_ref[...].astype(f32)
    gain = jnp.concatenate([gain[i : i + 1, :] for i in range(gain.shape[0])], axis=1)
    normed = (total - center) * lax.rsqrt(spread + 1e-05) * gain
    nb[x, c] = normed.astype(bf)
    yield
    for d in range(nz - 1):
        for h in range(2):

            @pl.when((z < nz - 1) & (z - d >= 0))
            def _():
                upward(xbuf.at[z, spot], z, d, h).wait_send()

            @pl.when((z > 0) & (z + d < nz))
            def _():
                downward(xbuf.at[z, spot], z, d, h).wait_send()

    for k in range(1, nz):
        slab = flip(z, k)
        corewise(slab, 0, spot).wait_send()
        corewise(slab, 1, spot).wait_send()
        for h in range(2):
            sideways(slab, spot, h).wait_send()
            to_z(k, h).wait_send()
    for k in range(nz):
        to_core(k).wait_send()
        for f in range(2):
            to_x(k, f).wait_send()


def greet_all():
    (z, x, c), (nz, nx, nc) = place()
    barrier = pltpu.get_barrier_semaphore()
    pl.semaphore_signal(
        barrier, inc=1, device_id={"expert": 1 - x, "inner": 1 - c}, device_id_type=MESH
    )
    for axis, here, size in zip(ALL, (z, x, c), (nz, nx, nc)):
        for turned in range(1, size):
            pl.semaphore_signal(
                barrier, inc=1, device_id={axis: turn(here, turned, size)}, device_id_type=MESH
            )
    pl.semaphore_wait(barrier, nz + nx + nc - 2)


def whole_kernel(
    tasks, mix_count, cand_ref, gate_ref, win_hbm, wout_hbm, gain_ref,
    q_hbm, k_hbm, v_hbm, task_ref, attn_ref, id_ref, out_ref, *scratch
):
    nb = scratch[mix_count]
    mix = mix_part(
        tasks, cand_ref, gate_ref, win_hbm, wout_hbm, gain_ref, nb, *scratch[:mix_count]
    )
    score = score_part(
        q_hbm, k_hbm, v_hbm, task_ref, attn_ref, id_ref, out_ref, *scratch[mix_count:]
    )
    next(score)
    next(mix)
    next(score, None)
    next(mix, None)


def score_part(
    q_hbm, k_hbm, v_hbm, task_ref, attn_ref, id_ref, out_ref,
    nb, q_ref, k_ref, v_ref, keys, extra, ids, queries, powers, high, sums, partial,
    load_sem, n_s, n_r, id_s, id_r, up_s, down_s, key_r, p_s, p_r,
):
    (z, x, c), (nz, nx, nc) = place()
    f32, bf = jnp.float32, jnp.bfloat16
    other_x, other_c = 1 - x, 1 - c
    _, _, share, depth = nb.shape
    rows = nx * nc * share
    both = nc * share
    heads = queries.shape[0]
    tasks = task_ref.shape[0]
    loads = [
        pltpu.make_async_copy(k_hbm, k_ref, load_sem.at[0]),
        pltpu.make_async_copy(v_hbm, v_ref, load_sem.at[1]),
        pltpu.make_async_copy(q_hbm, q_ref, load_sem.at[2]),
    ]
    for item in loads:
        item.start()
    yield

    def give(side, core, j, **where):
        return remote(nb.at[side, core], nb.at[side, core], n_s.at[j], n_r.at[j], **where)

    first = give(x, c, 0, expert=other_x)
    second = give(x, c, 1, inner=other_c)
    third = give(other_x, c, 2, inner=other_c)
    first.start()
    second.start()
    id_copies = []
    for turned in range(1, nz):
        target = turn(z, turned, nz)
        item = remote(id_ref, ids.at[z], id_s.at[turned], id_r.at[z], wide=target)
        item.start()
        id_copies.append(item)
    ids[z] = id_ref[...]
    for item in loads:
        item.wait()
    own = jnp.concatenate([id_ref[q] for q in range(nx * nc)], axis=1).astype(f32)
    lifted = heads * tasks
    extra[:, :, lifted:, :] = jnp.ones((nz, nx, 16, both), bf)
    shape = (lifted, heads * HD)
    row = lax.broadcasted_iota(jnp.int32, shape, 0) // tasks
    column = lax.broadcasted_iota(jnp.int32, shape, 1) // HD
    stacked = jnp.concatenate([attn_ref[...].astype(f32)] * heads, axis=0)
    blocks = jnp.where(row == column, stacked, 0.0).astype(bf)
    sides = (x, other_x)

    def parts(slab, m):
        return [keys.at[slab, sides[m]], extra.at[slab, sides[m], pl.ds(0, lifted)]]

    def upward(slab, d, m, j):
        piece = parts(slab, m)[j]
        return remote(piece, piece, up_s.at[d, m, j], key_r.at[slab, m, j], wide=z + 1)

    def downward(slab, d, m, j):
        piece = parts(slab, m)[j]
        return remote(piece, piece, down_s.at[d, m, j], key_r.at[slab, m, j], wide=z - 1)

    def announce(m, j):
        @pl.when(z < nz - 1)
        def _():
            upward(z, 0, m, j).start()

        @pl.when(z > 0)
        def _():
            downward(z, 0, m, j).start()

    def pass_on(d, m):
        for slab, here, further, way in (
            (z - d, z - d >= 0, z < nz - 1, upward),
            (z + d, z + d < nz, z > 0, downward),
        ):

            @pl.when(here)
            def _():
                for j in range(2):
                    way(slab, 0, m, j).wait_recv()

                    @pl.when(further)
                    def _():
                        way(slab, d, m, j).start()

    def make(m):
        data = nb[sides[m]].reshape(both, depth)
        keys[z, sides[m]] = jnp.dot(data, k_ref[...], preferred_element_type=f32).astype(bf)
        announce(m, 0)
        values = jnp.dot(data, v_ref[...], preferred_element_type=f32).astype(bf)
        extra[z, sides[m], :lifted, :] = lax.dot_general(
            blocks, values, (((1,), (1,)), ((), ())), preferred_element_type=f32
        ).astype(bf)
        announce(m, 1)

    give(x, other_c, 1, inner=other_c).wait_recv()
    make(0)
    give(other_x, c, 0, expert=other_x).wait_recv()
    third.start()
    pass_on(1, 0)
    give(other_x, other_c, 2, inner=other_c).wait_recv()
    make(1)
    data = jnp.concatenate([nb[q % nx, q // nx] for q in range(nx * nc)], axis=0)
    made = jnp.dot(data, q_ref[...], preferred_element_type=f32) * (1.0 / math.sqrt(HD))
    lane = lax.broadcasted_iota(jnp.int32, (rows, 2 * HD), 1)
    for h in range(heads):
        pair = made[:, h // 2 * 2 * HD : (h // 2 + 1) * 2 * HD]
        queries[h] = jnp.where(lane // HD == h % 2, pair, 0.0).astype(bf)
    for item in id_copies:
        item.wait_send()
    for turned in range(1, nz):
        source = turn(z, turned, nz)
        remote(id_ref, ids.at[source], id_s.at[turned], id_r.at[source], wide=source).wait_recv()

    def attend(slab, m, fresh=False):
        side = sides[m]
        theirs = jnp.concatenate([ids[slab, side], ids[slab, nx + side]], axis=1).astype(f32)
        same = jnp.broadcast_to(theirs, (8, both)).T[:, :1] == own
        tops = []
        for h in range(heads):
            pair = slice(h // 2 * 2 * HD, (h // 2 + 1) * 2 * HD)
            affinity = lax.dot_general(
                keys[slab, side][:, pair], queries[h], (((1,), (1,)), ((), ())),
                preferred_element_type=f32,
            )
            affinity = jnp.where(same, affinity, -1e30)
            top = jnp.max(affinity, axis=0, keepdims=True)
            powers[h] = jnp.exp(affinity - top).astype(bf)
            tops.append(top)
        for h in range(heads):
            got = jnp.dot(extra[slab, side], powers[h], preferred_element_type=f32)
            if fresh:
                high[h] = tops[h]
                sums[h] = got
            else:
                peak = jnp.maximum(high[h], tops[h])
                sums[h] = sums[h] * jnp.exp(high[h] - peak) + got * jnp.exp(tops[h] - peak)
                high[h] = peak

    attend(z, 0, True)
    attend(z, 1)
    pass_on(1, 1)
    attend(flip(z, 1), 0)
    pass_on(2, 0)
    attend(flip(z, 1), 1)
    pass_on(2, 1)
    attend(flip(z, 2), 0)
    attend(flip(z, 2), 1)
    pass_on(3, 0)
    attend(flip(z, 3), 0)
    pass_on(3, 1)
    attend(flip(z, 3), 1)
    result = None
    for h in range(heads):
        term = sums[h, h * tasks : (h + 1) * tasks] / sums[h, lifted : lifted + 1]
        result = term if result is None else result + term
    partial[0] = jnp.concatenate([result, jnp.zeros((8 - tasks, rows), f32)], axis=0)
    sends = []
    for j, where in enumerate(
        ({"inner": other_c}, {"expert": other_x}, {"expert": other_x, "inner": other_c})
    ):
        item = remote(partial.at[0], partial.at[j + 1], p_s.at[j], p_r.at[j], **where)
        item.start()
        sends.append(item)
    base = lax.dot_general(
        task_ref[...], data, (((1,), (1,)), ((), ())), preferred_element_type=f32
    )
    for item in sends:
        item.wait()
    everything = (partial[0] + partial[1]) + (partial[2] + partial[3])
    out_ref[...] = everything[:tasks, :] + base
    first.wait_send()
    second.wait_send()
    third.wait_send()
    for d in range(nz - 1):
        for m in range(2):
            for j in range(2):

                @pl.when((z < nz - 1) & (z - d >= 0))
                def _():
                    upward(z, d, m, j).wait_send()

                @pl.when((z > 0) & (z + d < nz))
                def _():
                    downward(z, d, m, j).wait_send()


def run_whole(
    cand, gate_weight, expert_in, expert_out, gain, query, key, value, task, attn, request_of,
    collective,
):
    nz, nx, nc = (lax.axis_size(a) for a in ALL)
    rows, depth = cand.shape
    quarters = nx * nc
    share = rows // quarters
    held, _, units = expert_in.shape
    width = expert_out.shape[1]
    tasks = task.shape[1]
    dma = pltpu.SemaphoreType.DMA
    f32, bf = jnp.float32, jnp.bfloat16
    vmem = pl.BlockSpec(memory_space=pltpu.VMEM)
    anywhere = pl.BlockSpec(memory_space=pl.ANY)
    model = tasks * width
    experts_all = gate_weight.shape[1] // tasks
    lanes = query.shape[1]
    heads = lanes // HD
    mix_scratch = [
        pltpu.VMEM((nz, quarters, share, depth), bf),
        pltpu.VMEM(expert_in.shape, bf),
        pltpu.VMEM(expert_out.shape, bf),
        pltpu.VMEM((tasks, experts_all, rows), f32),
        pltpu.VMEM((tasks * held, rows), f32),
        pltpu.VMEM((2 * TOGETHER, rows, units), bf),
        pltpu.VMEM((2 * TOGETHER, width, rows), f32),
        pltpu.VMEM((quarters, model, share), f32),
        pltpu.VMEM((nz, quarters, model, share), bf),
        pltpu.VMEM((nz, nx, model, share), bf),
        pltpu.VMEM((nz, model, share), bf),
        pltpu.VMEM((nz, model, share), bf),
        pltpu.VMEM((nz, model, share), bf),
        pltpu.VMEM((nz, model, share), bf),
        dma((3,)),
        dma((nz, 2)),
        dma((nz, 2)),
        dma((nz, 2)),
        dma((nz, 2)),
        dma((nz, 2)),
        dma((nz, 2)),
        dma((nz, 2)),
        dma((nz,)),
        dma((nz,)),
        dma((nz, 2)),
        dma((nz, 2)),
        dma((nz, 2)),
        dma((nz, 2)),
    ]
    columns = heads * tasks + 16
    score_scratch = [
        pltpu.VMEM((nx, nc, share, model), bf),
        pltpu.VMEM(query.shape, bf),
        pltpu.VMEM(key.shape, bf),
        pltpu.VMEM(value.shape, bf),
        pltpu.VMEM((nz, nx, nc * share, lanes), bf),
        pltpu.VMEM((nz, nx, columns, nc * share), bf),
        pltpu.VMEM((nz, quarters, 1, share), jnp.int32),
        pltpu.VMEM((heads, rows, 2 * HD), bf),
        pltpu.VMEM((heads, nc * share, rows), bf),
        pltpu.VMEM((heads, 1, rows), f32),
        pltpu.VMEM((heads, columns, rows), f32),
        pltpu.VMEM((nx * nc, 8, rows), f32),
        dma((3,)),
        dma((3,)),
        dma((3,)),
        dma((nz,)),
        dma((nz,)),
        dma((nz, 2, 2)),
        dma((nz, 2, 2)),
        dma((nz, 2, 2)),
        dma((3,)),
        dma((3,)),
    ]
    return pl.pallas_call(
        functools.partial(whole_kernel, tasks, len(mix_scratch)),
        in_specs=[anywhere, vmem, anywhere, anywhere, vmem, anywhere, anywhere, anywhere]
        + [vmem] * 3,
        out_specs=vmem,
        out_shape=jax.ShapeDtypeStruct((tasks, rows), f32),
        scratch_shapes=mix_scratch + score_scratch,
        compiler_params=pltpu.CompilerParams(
            collective_id=collective, has_side_effects=True, vmem_limit_bytes=VMEM_LIMIT
        ),
    )(
        cand.reshape(quarters, share, depth), gate_weight, expert_in, expert_out,
        gain.reshape(-1, 128), query, key, value, task.T, attn.T,
        request_of.reshape(quarters, 1, share),
    ).T


def fused(sizes, rows, heads, held):
    return sizes == (4, 2, 2) and rows % 512 == 0 and heads == 4 and held == 8 * TOGETHER


def local(
    candidates,
    gate_weight,
    expert_in,
    expert_out,
    norm_gain,
    query_weight,
    key_weight,
    value_weight,
    task_weight,
    attn_weight,
    request_of,
):
    rows = candidates.shape[0]
    tasks = task_weight.shape[1]
    nz, nx, nc = (lax.axis_size(a) for a in ALL)
    if fused((nz, nx, nc), rows, query_weight.shape[1] // HD, expert_in.shape[0]):
        return run_whole(
            candidates, gate_weight, expert_in, expert_out, norm_gain, query_weight, key_weight,
            value_weight, task_weight, attn_weight, request_of, 3,
        )
    share = rows // (nx * nc)
    spot = lax.axis_index("inner") * nx + lax.axis_index("expert")
    wide = lax.axis_index("wide")
    quarter = lax.dynamic_slice_in_dim(candidates, spot * share, share, 0)
    everyone, requests = run_gather(quarter, request_of[None, :], 0)
    partial_mix = run_experts(everyone, gate_weight, expert_in, expert_out, tasks)
    normed = run_reduce(partial_mix, norm_gain[None, :], share, 1)
    normed_all = run_gather(normed, None, 2)
    own = lax.dynamic_slice_in_dim(normed_all, wide * rows, rows, 0)
    queries = jnp.dot(own, query_weight, preferred_element_type=jnp.float32).astype(jnp.bfloat16)
    keys = jnp.dot(normed_all, key_weight, preferred_element_type=jnp.float32).astype(jnp.bfloat16)
    values = jnp.dot(normed_all, value_weight, preferred_element_type=jnp.float32).astype(
        jnp.bfloat16
    )
    term = run_attention(
        queries, keys, values, request_of[:, None], requests, attn_weight
    )
    attention = lax.psum(term.T, ("expert", "inner")).T
    return jnp.dot(own, task_weight, preferred_element_type=jnp.float32) + attention


def solution(mesh):
    return jax.shard_map(
        local,
        mesh=mesh,
        in_specs=(
            P(("groups", "wide"), None),
            P(),
            P("expert", None, ("wide", "inner")),
            P("expert", None, ("wide", "inner")),
            P(),
            P(None, ("expert", "inner")),
            P(None, ("expert", "inner")),
            P(None, ("expert", "inner")),
            P(),
            P(("expert", "inner"), None),
            P(("groups", "wide")),
        ),
        out_specs=P(("groups", "wide"), None),
        check_vma=False,
    )
```

```python
import functools
import math

import jax
import jax.numpy as jnp
from jax import lax
from jax.experimental import pallas as pl
from jax.experimental.pallas import tpu as pltpu
from jax.sharding import PartitionSpec as P

HD = 64
ALL = ("wide", "expert", "inner")
VMEM_LIMIT = 60 * 1024 * 1024


MESH = pl.DeviceIdType.MESH


def place():
    return tuple(lax.axis_index(a) for a in ALL), tuple(lax.axis_size(a) for a in ALL)


def turn(start, step, size):
    return lax.rem(start + step, size)


def greet():
    mine, sizes = place()
    barrier = pltpu.get_barrier_semaphore()
    for axis, here, size in zip(ALL, mine, sizes):
        for step in range(1, size):
            pl.semaphore_signal(
                barrier, inc=1, device_id={axis: turn(here, step, size)}, device_id_type=MESH
            )
    pl.semaphore_wait(barrier, sum(sizes) - len(sizes))


def gather_kernel(with_ids, *refs):
    if with_ids:
        own_ref, id_ref, out_ref, ids_ref, recv, send_z, send_x, send_c, local_sem, id_r, id_s = refs
    else:
        own_ref, out_ref, recv, send_z, send_x, send_c, local_sem = refs
    (z, x, c), (nz, nx, nc) = place()
    greet()

    def copy(src, zs, xs, cs, sem, axis, target):
        return pltpu.make_async_remote_copy(
            src_ref=src,
            dst_ref=out_ref.at[zs, cs, xs],
            send_sem=sem,
            recv_sem=recv.at[zs, cs, xs],
            device_id={axis: target},
            device_id_type=MESH,
        )

    def arrived(zs, xs, cs):
        copy(out_ref.at[zs, cs, xs], zs, xs, cs, send_z.at[0], "inner", turn(c, 1, nc)).wait_recv()

    sent = []

    def push(*what):
        item = copy(*what)
        item.start()
        sent.append(item)

    def spread_x(src, k, zs):
        for step in range(1, nx):
            push(src, zs, x, c, send_x.at[k, step - 1], "expert", turn(x, step, nx))

    def spread_c(src, k, j, zs, xs):
        for step in range(1, nc):
            push(src, zs, xs, c, send_c.at[k, j, step - 1], "inner", turn(c, step, nc))

    for step in range(1, nz):
        push(own_ref, z, x, c, send_z.at[step - 1], "wide", turn(z, step, nz))
    spread_x(own_ref, 0, z)
    spread_c(own_ref, 0, 0, z, x)
    keep = pltpu.make_async_copy(own_ref, out_ref.at[z, c, x], local_sem.at[0])
    keep.start()
    if with_ids:
        id_copies = []
        for step in range(1, nz):
            item = pltpu.make_async_remote_copy(
                src_ref=id_ref,
                dst_ref=ids_ref.at[z],
                send_sem=id_s.at[step - 1],
                recv_sem=id_r.at[z],
                device_id={"wide": turn(z, step, nz)},
                device_id_type=MESH,
            )
            item.start()
            id_copies.append(item)
        ids_ref[z] = id_ref[...]

    def pass_x(k):
        zs = turn(z, k, nz)
        for step in range(1, nx):
            xs = turn(x, step, nx)
            arrived(zs, xs, c)
            spread_c(out_ref.at[zs, c, xs], k, step, zs, xs)

    for k in range(1, nz):
        zs = turn(z, k, nz)
        arrived(zs, x, c)
        spread_x(out_ref.at[zs, c, x], k, zs)
        spread_c(out_ref.at[zs, c, x], k, 0, zs, x)
        pass_x(k - 1)
    pass_x(nz - 1)
    for k in range(nz):
        for j in range(nx):
            for step in range(1, nc):
                arrived(turn(z, k, nz), turn(x, j, nx), turn(c, step, nc))
    for item in sent:
        item.wait_send()
    keep.wait()
    if with_ids:
        for step in range(1, nz):
            zs = turn(z, step, nz)
            pltpu.make_async_remote_copy(
                src_ref=id_ref,
                dst_ref=ids_ref.at[zs],
                send_sem=id_s.at[step - 1],
                recv_sem=id_r.at[zs],
                device_id={"wide": zs},
                device_id_type=MESH,
            ).wait_recv()
        for item in id_copies:
            item.wait_send()


def run_gather(own, ids, collective):
    nz, nx, nc = (lax.axis_size(a) for a in ALL)
    dma = pltpu.SemaphoreType.DMA
    with_ids = ids is not None
    shape = jax.ShapeDtypeStruct((nz, nc, nx) + own.shape, own.dtype)
    vmem = pl.BlockSpec(memory_space=pltpu.VMEM)
    anywhere = pl.BlockSpec(memory_space=pl.ANY)
    scratch = [
        dma((nz, nc, nx)),
        dma((max(nz - 1, 1),)),
        dma((nz, max(nx - 1, 1))),
        dma((nz, nx, max(nc - 1, 1))),
        dma((1,)),
    ]
    if with_ids:
        scratch += [dma((nz,)), dma((max(nz - 1, 1),))]
    out = pl.pallas_call(
        functools.partial(gather_kernel, with_ids),
        in_specs=[vmem, vmem] if with_ids else [vmem],
        out_specs=[anywhere, vmem] if with_ids else anywhere,
        out_shape=[shape, jax.ShapeDtypeStruct((nz,) + ids.shape, ids.dtype)] if with_ids else shape,
        scratch_shapes=scratch,
        compiler_params=pltpu.CompilerParams(collective_id=collective, has_side_effects=True),
    )(*([own, ids] if with_ids else [own]))
    depth = own.shape[1]
    if with_ids:
        return out[0].reshape(-1, depth), out[1].reshape(1, -1)
    return out.reshape(-1, depth)


def reduce_kernel(
    part_ref, gain_ref, out_ref, mine, core_in, x_out, x_in, z_out, z_in,
    local_sem, core_s, core_r, x_s, x_r, z_s, z_r,
):
    (z, x, c), (nz, nx, nc) = place()
    f32 = jnp.float32
    greet()
    other = turn(c, 1, nc)
    core, kept = [], []
    for k in range(nz):
        s = turn(z, k + 1, nz)
        item = pltpu.make_async_remote_copy(
            src_ref=part_ref.at[s, other],
            dst_ref=core_in.at[k],
            send_sem=core_s.at[k],
            recv_sem=core_r.at[k],
            device_id={"inner": other},
            device_id_type=MESH,
        )
        item.start()
        core.append(item)
        stay = pltpu.make_async_copy(part_ref.at[s, c], mine.at[k], local_sem.at[k])
        stay.start()
        kept.append(stay)

    def pair(k, xs):
        return mine[k, xs].astype(f32) + core_in[k, xs].astype(f32)

    across, along = [], []

    def finish(k):
        total = pair(k, x)
        for step in range(1, nx):
            across[k][step - 1].wait_recv()
            total = total + x_in[k, step - 1].astype(f32)
        if k == nz - 1:
            return total
        z_out[k] = total.astype(z_out.dtype)
        item = pltpu.make_async_remote_copy(
            src_ref=z_out.at[k],
            dst_ref=z_in.at[k],
            send_sem=z_s.at[k],
            recv_sem=z_r.at[k],
            device_id={"wide": turn(z, k + 1, nz)},
            device_id_type=MESH,
        )
        item.start()
        along.append(item)

    for k in range(nz):
        kept[k].wait()
        core[k].wait_recv()
        items = []
        for step in range(1, nx):
            xs = turn(x, step, nx)
            x_out[k, step - 1] = pair(k, xs).astype(x_out.dtype)
            item = pltpu.make_async_remote_copy(
                src_ref=x_out.at[k, step - 1],
                dst_ref=x_in.at[k, step - 1],
                send_sem=x_s.at[k, step - 1],
                recv_sem=x_r.at[k, step - 1],
                device_id={"expert": xs},
                device_id_type=MESH,
            )
            item.start()
            items.append(item)
        across.append(items)
        if k > 0:
            finish(k - 1)
    total = finish(nz - 1)
    for k in range(nz - 1):
        along[k].wait_recv()
        total = total + z_in[k].astype(f32)
    center = jnp.mean(total, axis=1, keepdims=True)
    spread = jnp.mean(jnp.square(total - center), axis=1, keepdims=True)
    normed = (total - center) * lax.rsqrt(spread + 1e-05) * gain_ref[...].astype(f32)
    out_ref[...] = normed.astype(out_ref.dtype)
    for item in core + along + [i for items in across for i in items]:
        item.wait_send()


def run_reduce(part, gain, share, collective):
    nz, nx, nc = (lax.axis_size(a) for a in ALL)
    width = part.shape[1]
    dma = pltpu.SemaphoreType.DMA
    kind = part.dtype
    part = part.reshape(nz, nc, nx, share, width)
    few = max(nx - 1, 1)
    vmem = pl.BlockSpec(memory_space=pltpu.VMEM)
    return pl.pallas_call(
        reduce_kernel,
        in_specs=[pl.BlockSpec(memory_space=pl.ANY), vmem],
        out_specs=vmem,
        out_shape=jax.ShapeDtypeStruct((share, width), kind),
        scratch_shapes=[
            pltpu.VMEM((nz, nx, share, width), kind),
            pltpu.VMEM((nz, nx, share, width), kind),
            pltpu.VMEM((nz, few, share, width), kind),
            pltpu.VMEM((nz, few, share, width), kind),
            pltpu.VMEM((nz, share, width), kind),
            pltpu.VMEM((nz, share, width), kind),
            dma((nz,)),
            dma((nz,)),
            dma((nz,)),
            dma((nz, few)),
            dma((nz, few)),
            dma((nz,)),
            dma((nz,)),
        ],
        compiler_params=pltpu.CompilerParams(
            collective_id=collective, has_side_effects=True, vmem_limit_bytes=VMEM_LIMIT
        ),
    )(part, gain)


def expert_kernel(tasks, x_ref, gate_ref, win_ref, wout_ref, out_ref, acc_ref):
    rows = x_ref.shape[0]
    columns = gate_ref.shape[1]
    experts_all = columns // tasks
    held, _, _ = win_ref.shape
    width = wout_ref.shape[1]
    x = x_ref[...]
    logits = jnp.dot(x, gate_ref[...], preferred_element_type=jnp.float32)
    task = lax.broadcasted_iota(jnp.int32, (rows, columns), 1) // experts_all
    top = jnp.zeros_like(logits)
    for t in range(tasks):
        high = jnp.max(jnp.where(task == t, logits, -jnp.inf), axis=1, keepdims=True)
        top = jnp.where(task == t, high, top)
    powers = jnp.exp(logits - top)
    total = jnp.ones_like(logits)
    for t in range(tasks):
        part = jnp.sum(jnp.where(task == t, powers, 0.0), axis=1, keepdims=True)
        total = jnp.where(task == t, part, total)
    gates = powers / total
    shift = lax.rem(columns - lax.axis_index("expert") * held, columns)
    gates = pltpu.roll(gates, shift, 1)
    together = min(4, held)
    for first in range(0, held, together):
        made = []
        for e in range(first, first + together):
            hidden = jnp.maximum(
                jnp.dot(x, win_ref[e], preferred_element_type=jnp.float32), 0.0
            ).astype(jnp.bfloat16)
            made.append(
                lax.dot_general(
                    hidden,
                    wout_ref[e],
                    (((1,), (1,)), ((), ())),
                    preferred_element_type=jnp.float32,
                )
            )
        for t in range(tasks):
            piece = None
            for j, output in enumerate(made):
                lane = t * experts_all + first + j
                term = gates[:, lane : lane + 1] * output
                piece = term if piece is None else piece + term
            span = slice(t * width, (t + 1) * width)
            if first > 0:
                piece = piece + acc_ref[:, span]
            if first + together < held:
                acc_ref[:, span] = piece
            else:
                out_ref[:, span] = piece.astype(out_ref.dtype)


def run_experts(x, gate_weight, expert_in, expert_out, tasks):
    rows, depth = x.shape
    held, _, units = expert_in.shape
    width = expert_out.shape[1]
    block = min(512, rows)
    return pl.pallas_call(
        functools.partial(expert_kernel, tasks),
        grid=(rows // block,),
        in_specs=[
            pl.BlockSpec((block, depth), lambda i: (i, 0)),
            pl.BlockSpec(gate_weight.shape, lambda i: (0, 0)),
            pl.BlockSpec(expert_in.shape, lambda i: (0, 0, 0), pipeline_mode=pl.Buffered(1)),
            pl.BlockSpec(expert_out.shape, lambda i: (0, 0, 0), pipeline_mode=pl.Buffered(1)),
        ],
        out_specs=pl.BlockSpec((block, tasks * width), lambda i: (i, 0)),
        out_shape=jax.ShapeDtypeStruct((rows, tasks * width), jnp.bfloat16),
        scratch_shapes=[pltpu.VMEM((block, tasks * width), jnp.float32)],
        compiler_params=pltpu.CompilerParams(vmem_limit_bytes=VMEM_LIMIT),
    )(x, gate_weight, expert_in, expert_out)


def attention_kernel(q_ref, k_ref, v_ref, own_ref, all_ref, weight_ref, out_ref):
    same = own_ref[...] == all_ref[...]
    factor = 1.0 / math.sqrt(HD)
    result = None
    for first in range(0, q_ref.shape[1], HD):
        span = slice(first, first + HD)
        affinity = (
            lax.dot_general(
                q_ref[:, span],
                k_ref[:, span],
                (((1,), (1,)), ((), ())),
                preferred_element_type=jnp.float32,
            )
            * factor
        )
        affinity = jnp.where(same, affinity, -1e30)
        highest = jnp.max(affinity, axis=1, keepdims=True)
        powers = jnp.exp(affinity - highest)
        total = jnp.sum(powers, axis=1, keepdims=True)
        context = jnp.dot(
            powers.astype(jnp.bfloat16), v_ref[:, span], preferred_element_type=jnp.float32
        )
        context = (context / total).astype(jnp.bfloat16)
        term = jnp.dot(context, weight_ref[span, :], preferred_element_type=jnp.float32)
        result = term if result is None else result + term
    out_ref[...] = result


def run_attention(q, k, v, own, every, weight):
    rows, width = q.shape
    keys = k.shape[0]
    tasks = weight.shape[1]
    block = min(128, rows)
    return pl.pallas_call(
        attention_kernel,
        grid=(rows // block,),
        in_specs=[
            pl.BlockSpec((block, width), lambda i: (i, 0)),
            pl.BlockSpec((keys, width), lambda i: (0, 0)),
            pl.BlockSpec((keys, width), lambda i: (0, 0)),
            pl.BlockSpec((block, 1), lambda i: (i, 0)),
            pl.BlockSpec((1, keys), lambda i: (0, 0)),
            pl.BlockSpec((width, tasks), lambda i: (0, 0)),
        ],
        out_specs=pl.BlockSpec((block, tasks), lambda i: (i, 0)),
        out_shape=jax.ShapeDtypeStruct((rows, tasks), jnp.float32),
        compiler_params=pltpu.CompilerParams(vmem_limit_bytes=VMEM_LIMIT),
    )(q, k, v, own, every, weight)


def flip(position, step):
    low = lax.rem(position, 2)
    high = position // 2
    return (high + (step // 2) * (1 - 2 * high)) * 2 + low + lax.rem(step, 2) * (1 - 2 * low)


def remote(src, dst, send, recv, **where):
    return pltpu.make_async_remote_copy(
        src_ref=src, dst_ref=dst, send_sem=send, recv_sem=recv, device_id=where,
        device_id_type=MESH,
    )


TOGETHER = 2
CUTS = 4


def mix_part(
    tasks, cand_ref, gate_ref, win_hbm, wout_hbm, gain_ref, nb,
    xbuf, win, wout, gates_all, gates, hidden, made, acc, part, core_in, x_out, x_in, z_out, z_in,
    load_sem, up_s, down_s, z_r, x_s, x_r, c_s, c_r, core_s, core_r, rx_s, rx_r, rz_s, rz_r,
):
    (z, x, c), (nz, nx, nc) = place()
    f32, bf = jnp.float32, jnp.bfloat16
    other_x, other_c = 1 - x, 1 - c
    held = win.shape[0]
    quarters, share, depth = xbuf.shape[1:]
    rows = quarters * share
    width = wout.shape[1]
    spot = c * nx + x
    loads = [
        pltpu.make_async_copy(cand_ref, xbuf.at[z], load_sem.at[0]),
        pltpu.make_async_copy(win_hbm, win, load_sem.at[1]),
        pltpu.make_async_copy(wout_hbm, wout, load_sem.at[2]),
    ]
    for item in loads:
        item.start()
    greet_all()

    piece_rows = share // 2
    some = part.shape[2] // CUTS

    def rows_of(h):
        return pl.ds(h * piece_rows, piece_rows)

    def features(f):
        return pl.ds(f * some, some)

    def upward(src, slab, d, h):
        return remote(
            src.at[rows_of(h)], xbuf.at[slab, spot, rows_of(h)], up_s.at[d, h], z_r.at[slab, h],
            wide=z + 1,
        )

    def downward(src, slab, d, h):
        return remote(
            src.at[rows_of(h)], xbuf.at[slab, spot, rows_of(h)], down_s.at[d, h],
            z_r.at[slab, h], wide=z - 1,
        )

    def sideways(slab, q, h):
        piece = xbuf.at[slab, q, rows_of(h)]
        return remote(piece, piece, x_s.at[slab, h], x_r.at[slab, h], expert=other_x)

    def corewise(slab, j, q):
        piece = xbuf.at[slab, q]
        return remote(piece, piece, c_s.at[slab, j], c_r.at[slab, j], inner=other_c)

    for h in range(2):

        @pl.when(z < nz - 1)
        def _():
            upward(cand_ref.at[spot], z, 0, h).start()

        @pl.when(z > 0)
        def _():
            downward(cand_ref.at[spot], z, 0, h).start()

    for item in loads:
        item.wait()

    def arrive_z(d, h):
        below, above = z - d, z + d

        @pl.when(below >= 0)
        def _():
            upward(xbuf.at[below, spot], below, 0, h).wait_recv()

            @pl.when(z < nz - 1)
            def _():
                upward(xbuf.at[below, spot], below, d, h).start()

        @pl.when(above < nz)
        def _():
            downward(xbuf.at[above, spot], above, 0, h).wait_recv()

            @pl.when(z > 0)
            def _():
                downward(xbuf.at[above, spot], above, d, h).start()

        slab = flip(z, d)
        sideways(slab, spot, h).start()
        if h == 1:
            corewise(slab, 0, spot).start()

    def arrive_x(slab):
        q = c * nx + other_x
        for h in range(2):
            sideways(slab, q, h).wait_recv()
        corewise(slab, 1, q).start()

    def arrive_c(slab):
        for j, q in ((0, other_c * nx + x), (1, other_c * nx + other_x)):
            corewise(slab, j, q).wait_recv()

    def to_core(k):
        return remote(
            part.at[k, pl.ds(other_c * nx, nx)], core_in.at[k], core_s.at[k], core_r.at[k],
            inner=other_c,
        )

    def to_x(k, f):
        return remote(
            x_out.at[k, features(f)], x_in.at[k, features(f)], rx_s.at[k, f], rx_r.at[k, f],
            expert=other_x,
        )

    def to_z(k, f):
        return remote(
            z_out.at[k, features(f)], z_in.at[k, features(f)], rz_s.at[k, f], rz_r.at[k, f],
            wide=flip(z, 1 if k == 2 else k),
        )

    def reduce_core(k):
        to_core(k).wait_recv()
        for f in range(CUTS):
            x_out[k, features(f)] = (
                part[k, c * nx + other_x, features(f)].astype(f32)
                + core_in[k, other_x, features(f)].astype(f32)
            ).astype(bf)
            to_x(k, f).start()

    def total_of(k, f):
        return (
            part[k, c * nx + x, features(f)].astype(f32)
            + core_in[k, x, features(f)].astype(f32)
            + x_in[k, features(f)].astype(f32)
        )

    def reduce_x(k, f):
        to_x(k, f).wait_recv()
        total = total_of(k, f)
        if k == 3:
            to_z(2, f).wait_recv()
            total = total + z_in[2, features(f)].astype(f32)
        z_out[k, features(f)] = total.astype(bf)
        to_z(k, f).start()

    groups = held // TOGETHER

    def gating(i, k):
        side = (i % 2) * TOGETHER
        for q in range(quarters):
            lanes = slice(q * share, (q + 1) * share)
            weights = [
                [
                    gates[t * held + i * TOGETHER + j : t * held + i * TOGETHER + j + 1, lanes]
                    for j in range(TOGETHER)
                ]
                for t in range(tasks)
            ]
            for f in range(0, width, 16):
                outs = [made[side + j, f : f + 16, lanes] for j in range(TOGETHER)]
                for t in range(tasks):
                    span = slice(t * width + f, t * width + f + 16)
                    piece = weights[t][0] * outs[0]
                    for j in range(1, TOGETHER):
                        piece = piece + weights[t][j] * outs[j]
                    if i > 0:
                        piece = piece + acc[q, span, :]
                    if i < groups - 1:
                        acc[q, span, :] = piece
                    else:
                        part[k, q, span, :] = piece.astype(bf)

    def stage(i, data, k):
        if i < groups:
            for j in range(TOGETHER):
                e = i * TOGETHER + j
                hidden[(i % 2) * TOGETHER + j] = jnp.maximum(
                    jnp.dot(data, win[e], preferred_element_type=f32), 0.0
                ).astype(bf)
        if 0 < i <= groups:
            side = ((i - 1) % 2) * TOGETHER
            for j in range(TOGETHER):
                e = (i - 1) * TOGETHER + j
                made[side + j] = lax.dot_general(
                    wout[e], hidden[side + j], (((1,), (1,)), ((), ())),
                    preferred_element_type=f32,
                )
        if i > 1:
            gating(i - 2, k)

    agenda = (
        (0, 0, lambda: arrive_z(1, 0)),
        (0, 4, lambda: arrive_z(1, 1)),
        (0, 7, lambda: arrive_z(2, 0)),
        (1, 4, lambda: arrive_z(3, 0)),
        (1, 7, lambda: arrive_z(3, 1)),
        (1, 8, lambda: reduce_core(0)),
        (1, 9, lambda: arrive_x(flip(z, 2))),
        (2, 2, lambda: reduce_core(1)),
        (2, 6, lambda: arrive_x(flip(z, 3))),
        (3, 2, lambda: reduce_core(2)),
        (3, 4, lambda: reduce_x(1, 0)),
        (3, 4, lambda: reduce_x(1, 1)),
        (3, 5, lambda: reduce_x(1, 2)),
        (3, 6, lambda: reduce_x(1, 3)),
        (3, 8, lambda: reduce_x(2, 0)),
        (3, 9, lambda: reduce_x(2, 1)),
    )

    def step(k, carry):
        slab = flip(z, k)
        data = xbuf[slab].reshape(rows, depth)
        logits = lax.dot_general(
            gate_ref[...], data, (((0,), (1,)), ((), ())), preferred_element_type=f32
        )
        logits = logits.reshape(tasks, logits.shape[0] // tasks, rows)
        powers = jnp.exp(logits - jnp.max(logits, axis=1, keepdims=True))
        gates_all[...] = powers / jnp.sum(powers, axis=1, keepdims=True)
        for t in range(tasks):
            gates[t * held : (t + 1) * held, :] = gates_all[
                t, pl.ds(pl.multiple_of(x * held, held), held), :
            ]
        after = flip(z, k + 1)
        for i in range(groups + 2):
            for moment, boundary, action in agenda:
                if boundary == i:
                    pl.when(k == moment)(action)
            if i > 0:
                data = xbuf[slab].reshape(rows, depth)
            stage(i, data, k)
        to_core(k).start()

        @pl.when(k == 0)
        def _():
            arrive_z(2, 1)
            arrive_x(after)

        @pl.when(k < nz - 1)
        def _():
            arrive_c(after)

        return carry

    lax.fori_loop(0, nz, step, 0)
    reduce_x(2, 2)
    reduce_core(3)
    reduce_x(2, 3)
    for f in range(CUTS):
        reduce_x(3, f)
    totals = []
    for f in range(CUTS):
        to_x(0, f).wait_recv()
        total = total_of(0, f)
        for k in (1, 3):
            to_z(k, f).wait_recv()
            total = total + z_in[k, features(f)].astype(f32)
        totals.append(total)
    total = jnp.concatenate(totals, axis=0)
    total = total.T
    center = jnp.mean(total, axis=1, keepdims=True)
    spread = jnp.mean(jnp.square(total - center), axis=1, keepdims=True)
    gain = gain_ref[...].astype(f32)
    gain = jnp.concatenate([gain[i : i + 1, :] for i in range(gain.shape[0])], axis=1)
    normed = (total - center) * lax.rsqrt(spread + 1e-05) * gain
    nb[x, c] = normed.astype(bf)
    yield
    for d in range(nz - 1):
        for h in range(2):

            @pl.when((z < nz - 1) & (z - d >= 0))
            def _():
                upward(xbuf.at[z, spot], z, d, h).wait_send()

            @pl.when((z > 0) & (z + d < nz))
            def _():
                downward(xbuf.at[z, spot], z, d, h).wait_send()

    for k in range(1, nz):
        slab = flip(z, k)
        corewise(slab, 0, spot).wait_send()
        corewise(slab, 1, spot).wait_send()
        for h in range(2):
            sideways(slab, spot, h).wait_send()
        for f in range(CUTS):
            to_z(k, f).wait_send()
    for k in range(nz):
        to_core(k).wait_send()
        for f in range(CUTS):
            to_x(k, f).wait_send()


def greet_all():
    (z, x, c), (nz, nx, nc) = place()
    barrier = pltpu.get_barrier_semaphore()
    pl.semaphore_signal(
        barrier, inc=1, device_id={"expert": 1 - x, "inner": 1 - c}, device_id_type=MESH
    )
    for axis, here, size in zip(ALL, (z, x, c), (nz, nx, nc)):
        for turned in range(1, size):
            pl.semaphore_signal(
                barrier, inc=1, device_id={axis: turn(here, turned, size)}, device_id_type=MESH
            )
    pl.semaphore_wait(barrier, nz + nx + nc - 2)


def whole_kernel(
    tasks, mix_count, cand_ref, gate_ref, win_hbm, wout_hbm, gain_ref,
    q_hbm, k_hbm, v_hbm, task_ref, attn_ref, id_ref, out_ref, *scratch
):
    nb = scratch[mix_count]
    mix = mix_part(
        tasks, cand_ref, gate_ref, win_hbm, wout_hbm, gain_ref, nb, *scratch[:mix_count]
    )
    score = score_part(
        q_hbm, k_hbm, v_hbm, task_ref, attn_ref, id_ref, out_ref, *scratch[mix_count:]
    )
    next(score)
    next(mix)
    next(score, None)
    next(mix, None)


def score_part(
    q_hbm, k_hbm, v_hbm, task_ref, attn_ref, id_ref, out_ref,
    nb, q_ref, k_ref, v_ref, keys, extra, ids, queries, powers, high, sums, partial,
    load_sem, n_s, n_r, id_s, id_r, up_s, down_s, key_r, p_s, p_r,
):
    (z, x, c), (nz, nx, nc) = place()
    f32, bf = jnp.float32, jnp.bfloat16
    other_x, other_c = 1 - x, 1 - c
    _, _, share, depth = nb.shape
    rows = nx * nc * share
    both = nc * share
    heads = queries.shape[0]
    tasks = task_ref.shape[0]
    loads = [
        pltpu.make_async_copy(k_hbm, k_ref, load_sem.at[0]),
        pltpu.make_async_copy(v_hbm, v_ref, load_sem.at[1]),
        pltpu.make_async_copy(q_hbm, q_ref, load_sem.at[2]),
    ]
    for item in loads:
        item.start()
    yield

    def give(side, core, j, **where):
        return remote(nb.at[side, core], nb.at[side, core], n_s.at[j], n_r.at[j], **where)

    first = give(x, c, 0, expert=other_x)
    second = give(x, c, 1, inner=other_c)
    third = give(other_x, c, 2, inner=other_c)
    first.start()
    second.start()
    id_copies = []
    for turned in range(1, nz):
        target = turn(z, turned, nz)
        item = remote(id_ref, ids.at[z], id_s.at[turned], id_r.at[z], wide=target)
        item.start()
        id_copies.append(item)
    ids[z] = id_ref[...]
    for item in loads:
        item.wait()
    own = jnp.concatenate([id_ref[q] for q in range(nx * nc)], axis=1).astype(f32)
    lifted = heads * tasks
    extra[:, :, lifted:, :] = jnp.ones((nz, nx, 16, both), bf)
    shape = (lifted, heads * HD)
    row = lax.broadcasted_iota(jnp.int32, shape, 0) // tasks
    column = lax.broadcasted_iota(jnp.int32, shape, 1) // HD
    stacked = jnp.concatenate([attn_ref[...].astype(f32)] * heads, axis=0)
    blocks = jnp.where(row == column, stacked, 0.0).astype(bf)
    sides = (x, other_x)

    def parts(slab, m):
        return [keys.at[slab, sides[m]], extra.at[slab, sides[m], pl.ds(0, lifted)]]

    def upward(slab, d, m, j):
        piece = parts(slab, m)[j]
        return remote(piece, piece, up_s.at[d, m, j], key_r.at[slab, m, j], wide=z + 1)

    def downward(slab, d, m, j):
        piece = parts(slab, m)[j]
        return remote(piece, piece, down_s.at[d, m, j], key_r.at[slab, m, j], wide=z - 1)

    def announce(m, j):
        @pl.when(z < nz - 1)
        def _():
            upward(z, 0, m, j).start()

        @pl.when(z > 0)
        def _():
            downward(z, 0, m, j).start()

    def pass_on(d, m):
        for slab, here, further, way in (
            (z - d, z - d >= 0, z < nz - 1, upward),
            (z + d, z + d < nz, z > 0, downward),
        ):

            @pl.when(here)
            def _():
                for j in range(2):
                    way(slab, 0, m, j).wait_recv()

                    @pl.when(further)
                    def _():
                        way(slab, d, m, j).start()

    def make(m):
        data = nb[sides[m]].reshape(both, depth)
        keys[z, sides[m]] = jnp.dot(data, k_ref[...], preferred_element_type=f32).astype(bf)
        announce(m, 0)
        values = jnp.dot(data, v_ref[...], preferred_element_type=f32).astype(bf)
        extra[z, sides[m], :lifted, :] = lax.dot_general(
            blocks, values, (((1,), (1,)), ((), ())), preferred_element_type=f32
        ).astype(bf)
        announce(m, 1)

    give(x, other_c, 1, inner=other_c).wait_recv()
    make(0)
    give(other_x, c, 0, expert=other_x).wait_recv()
    third.start()
    pass_on(1, 0)
    give(other_x, other_c, 2, inner=other_c).wait_recv()
    make(1)
    data = jnp.concatenate([nb[q % nx, q // nx] for q in range(nx * nc)], axis=0)
    made = jnp.dot(data, q_ref[...], preferred_element_type=f32) * (1.0 / math.sqrt(HD))
    lane = lax.broadcasted_iota(jnp.int32, (rows, 2 * HD), 1)
    for h in range(heads):
        pair = made[:, h // 2 * 2 * HD : (h // 2 + 1) * 2 * HD]
        queries[h] = jnp.where(lane // HD == h % 2, pair, 0.0).astype(bf)
    for item in id_copies:
        item.wait_send()
    for turned in range(1, nz):
        source = turn(z, turned, nz)
        remote(id_ref, ids.at[source], id_s.at[turned], id_r.at[source], wide=source).wait_recv()

    def attend(slab, m, fresh=False):
        side = sides[m]
        theirs = jnp.concatenate([ids[slab, side], ids[slab, nx + side]], axis=1).astype(f32)
        same = jnp.broadcast_to(theirs, (8, both)).T[:, :1] == own
        tops = []
        for h in range(heads):
            pair = slice(h // 2 * 2 * HD, (h // 2 + 1) * 2 * HD)
            affinity = lax.dot_general(
                keys[slab, side][:, pair], queries[h], (((1,), (1,)), ((), ())),
                preferred_element_type=f32,
            )
            affinity = jnp.where(same, affinity, -1e30)
            top = jnp.max(affinity, axis=0, keepdims=True)
            powers[h] = jnp.exp(affinity - top).astype(bf)
            tops.append(top)
        for h in range(heads):
            got = jnp.dot(extra[slab, side], powers[h], preferred_element_type=f32)
            if fresh:
                high[h] = tops[h]
                sums[h] = got
            else:
                peak = jnp.maximum(high[h], tops[h])
                sums[h] = sums[h] * jnp.exp(high[h] - peak) + got * jnp.exp(tops[h] - peak)
                high[h] = peak

    attend(z, 0, True)
    attend(z, 1)
    pass_on(1, 1)
    attend(flip(z, 1), 0)
    pass_on(2, 0)
    attend(flip(z, 1), 1)
    pass_on(2, 1)
    attend(flip(z, 2), 0)
    attend(flip(z, 2), 1)
    pass_on(3, 0)
    attend(flip(z, 3), 0)
    pass_on(3, 1)
    attend(flip(z, 3), 1)
    result = None
    for h in range(heads):
        term = sums[h, h * tasks : (h + 1) * tasks] / sums[h, lifted : lifted + 1]
        result = term if result is None else result + term
    partial[0] = jnp.concatenate([result, jnp.zeros((8 - tasks, rows), f32)], axis=0)
    sends = []
    for j, where in enumerate(
        ({"inner": other_c}, {"expert": other_x}, {"expert": other_x, "inner": other_c})
    ):
        item = remote(partial.at[0], partial.at[j + 1], p_s.at[j], p_r.at[j], **where)
        item.start()
        sends.append(item)
    base = lax.dot_general(
        task_ref[...], data, (((1,), (1,)), ((), ())), preferred_element_type=f32
    )
    for item in sends:
        item.wait()
    everything = (partial[0] + partial[1]) + (partial[2] + partial[3])
    out_ref[...] = everything[:tasks, :] + base
    first.wait_send()
    second.wait_send()
    third.wait_send()
    for d in range(nz - 1):
        for m in range(2):
            for j in range(2):

                @pl.when((z < nz - 1) & (z - d >= 0))
                def _():
                    upward(z, d, m, j).wait_send()

                @pl.when((z > 0) & (z + d < nz))
                def _():
                    downward(z, d, m, j).wait_send()


def run_whole(
    cand, gate_weight, expert_in, expert_out, gain, query, key, value, task, attn, request_of,
    collective,
):
    nz, nx, nc = (lax.axis_size(a) for a in ALL)
    rows, depth = cand.shape
    quarters = nx * nc
    share = rows // quarters
    held, _, units = expert_in.shape
    width = expert_out.shape[1]
    tasks = task.shape[1]
    dma = pltpu.SemaphoreType.DMA
    f32, bf = jnp.float32, jnp.bfloat16
    vmem = pl.BlockSpec(memory_space=pltpu.VMEM)
    anywhere = pl.BlockSpec(memory_space=pl.ANY)
    model = tasks * width
    experts_all = gate_weight.shape[1] // tasks
    lanes = query.shape[1]
    heads = lanes // HD
    mix_scratch = [
        pltpu.VMEM((nz, quarters, share, depth), bf),
        pltpu.VMEM(expert_in.shape, bf),
        pltpu.VMEM(expert_out.shape, bf),
        pltpu.VMEM((tasks, experts_all, rows), f32),
        pltpu.VMEM((tasks * held, rows), f32),
        pltpu.VMEM((2 * TOGETHER, rows, units), bf),
        pltpu.VMEM((2 * TOGETHER, width, rows), f32),
        pltpu.VMEM((quarters, model, share), f32),
        pltpu.VMEM((nz, quarters, model, share), bf),
        pltpu.VMEM((nz, nx, model, share), bf),
        pltpu.VMEM((nz, model, share), bf),
        pltpu.VMEM((nz, model, share), bf),
        pltpu.VMEM((nz, model, share), bf),
        pltpu.VMEM((nz, model, share), bf),
        dma((3,)),
        dma((nz, 2)),
        dma((nz, 2)),
        dma((nz, 2)),
        dma((nz, 2)),
        dma((nz, 2)),
        dma((nz, 2)),
        dma((nz, 2)),
        dma((nz,)),
        dma((nz,)),
        dma((nz, CUTS)),
        dma((nz, CUTS)),
        dma((nz, CUTS)),
        dma((nz, CUTS)),
    ]
    columns = heads * tasks + 16
    score_scratch = [
        pltpu.VMEM((nx, nc, share, model), bf),
        pltpu.VMEM(query.shape, bf),
        pltpu.VMEM(key.shape, bf),
        pltpu.VMEM(value.shape, bf),
        pltpu.VMEM((nz, nx, nc * share, lanes), bf),
        pltpu.VMEM((nz, nx, columns, nc * share), bf),
        pltpu.VMEM((nz, quarters, 1, share), jnp.int32),
        pltpu.VMEM((heads, rows, 2 * HD), bf),
        pltpu.VMEM((heads, nc * share, rows), bf),
        pltpu.VMEM((heads, 1, rows), f32),
        pltpu.VMEM((heads, columns, rows), f32),
        pltpu.VMEM((nx * nc, 8, rows), f32),
        dma((3,)),
        dma((3,)),
        dma((3,)),
        dma((nz,)),
        dma((nz,)),
        dma((nz, 2, 2)),
        dma((nz, 2, 2)),
        dma((nz, 2, 2)),
        dma((3,)),
        dma((3,)),
    ]
    return pl.pallas_call(
        functools.partial(whole_kernel, tasks, len(mix_scratch)),
        in_specs=[anywhere, vmem, anywhere, anywhere, vmem, anywhere, anywhere, anywhere]
        + [vmem] * 3,
        out_specs=vmem,
        out_shape=jax.ShapeDtypeStruct((tasks, rows), f32),
        scratch_shapes=mix_scratch + score_scratch,
        compiler_params=pltpu.CompilerParams(
            collective_id=collective, has_side_effects=True, vmem_limit_bytes=VMEM_LIMIT
        ),
    )(
        cand.reshape(quarters, share, depth), gate_weight, expert_in, expert_out,
        gain.reshape(-1, 128), query, key, value, task.T, attn.T,
        request_of.reshape(quarters, 1, share),
    ).T


def fused(sizes, rows, heads, held):
    return sizes == (4, 2, 2) and rows % 512 == 0 and heads == 4 and held == 8 * TOGETHER


def local(
    candidates,
    gate_weight,
    expert_in,
    expert_out,
    norm_gain,
    query_weight,
    key_weight,
    value_weight,
    task_weight,
    attn_weight,
    request_of,
):
    rows = candidates.shape[0]
    tasks = task_weight.shape[1]
    nz, nx, nc = (lax.axis_size(a) for a in ALL)
    if fused((nz, nx, nc), rows, query_weight.shape[1] // HD, expert_in.shape[0]):
        return run_whole(
            candidates, gate_weight, expert_in, expert_out, norm_gain, query_weight, key_weight,
            value_weight, task_weight, attn_weight, request_of, 3,
        )
    share = rows // (nx * nc)
    spot = lax.axis_index("inner") * nx + lax.axis_index("expert")
    wide = lax.axis_index("wide")
    quarter = lax.dynamic_slice_in_dim(candidates, spot * share, share, 0)
    everyone, requests = run_gather(quarter, request_of[None, :], 0)
    partial_mix = run_experts(everyone, gate_weight, expert_in, expert_out, tasks)
    normed = run_reduce(partial_mix, norm_gain[None, :], share, 1)
    normed_all = run_gather(normed, None, 2)
    own = lax.dynamic_slice_in_dim(normed_all, wide * rows, rows, 0)
    queries = jnp.dot(own, query_weight, preferred_element_type=jnp.float32).astype(jnp.bfloat16)
    keys = jnp.dot(normed_all, key_weight, preferred_element_type=jnp.float32).astype(jnp.bfloat16)
    values = jnp.dot(normed_all, value_weight, preferred_element_type=jnp.float32).astype(
        jnp.bfloat16
    )
    term = run_attention(
        queries, keys, values, request_of[:, None], requests, attn_weight
    )
    attention = lax.psum(term.T, ("expert", "inner")).T
    return jnp.dot(own, task_weight, preferred_element_type=jnp.float32) + attention


def solution(mesh):
    return jax.shard_map(
        local,
        mesh=mesh,
        in_specs=(
            P(("groups", "wide"), None),
            P(),
            P("expert", None, ("wide", "inner")),
            P("expert", None, ("wide", "inner")),
            P(),
            P(None, ("expert", "inner")),
            P(None, ("expert", "inner")),
            P(None, ("expert", "inner")),
            P(),
            P(("expert", "inner"), None),
            P(("groups", "wide")),
        ),
        out_specs=P(("groups", "wide"), None),
        check_vma=False,
    )
```

```python
import functools
import math

import jax
import jax.numpy as jnp
from jax import lax
from jax.experimental import pallas as pl
from jax.experimental.pallas import tpu as pltpu
from jax.sharding import PartitionSpec as P

HD = 64
ALL = ("wide", "expert", "inner")
VMEM_LIMIT = 60 * 1024 * 1024


MESH = pl.DeviceIdType.MESH


def place():
    return tuple(lax.axis_index(a) for a in ALL), tuple(lax.axis_size(a) for a in ALL)


def turn(start, step, size):
    return lax.rem(start + step, size)


def greet():
    mine, sizes = place()
    barrier = pltpu.get_barrier_semaphore()
    for axis, here, size in zip(ALL, mine, sizes):
        for step in range(1, size):
            pl.semaphore_signal(
                barrier, inc=1, device_id={axis: turn(here, step, size)}, device_id_type=MESH
            )
    pl.semaphore_wait(barrier, sum(sizes) - len(sizes))


def gather_kernel(with_ids, *refs):
    if with_ids:
        own_ref, id_ref, out_ref, ids_ref, recv, send_z, send_x, send_c, local_sem, id_r, id_s = refs
    else:
        own_ref, out_ref, recv, send_z, send_x, send_c, local_sem = refs
    (z, x, c), (nz, nx, nc) = place()
    greet()

    def copy(src, zs, xs, cs, sem, axis, target):
        return pltpu.make_async_remote_copy(
            src_ref=src,
            dst_ref=out_ref.at[zs, cs, xs],
            send_sem=sem,
            recv_sem=recv.at[zs, cs, xs],
            device_id={axis: target},
            device_id_type=MESH,
        )

    def arrived(zs, xs, cs):
        copy(out_ref.at[zs, cs, xs], zs, xs, cs, send_z.at[0], "inner", turn(c, 1, nc)).wait_recv()

    sent = []

    def push(*what):
        item = copy(*what)
        item.start()
        sent.append(item)

    def spread_x(src, k, zs):
        for step in range(1, nx):
            push(src, zs, x, c, send_x.at[k, step - 1], "expert", turn(x, step, nx))

    def spread_c(src, k, j, zs, xs):
        for step in range(1, nc):
            push(src, zs, xs, c, send_c.at[k, j, step - 1], "inner", turn(c, step, nc))

    for step in range(1, nz):
        push(own_ref, z, x, c, send_z.at[step - 1], "wide", turn(z, step, nz))
    spread_x(own_ref, 0, z)
    spread_c(own_ref, 0, 0, z, x)
    keep = pltpu.make_async_copy(own_ref, out_ref.at[z, c, x], local_sem.at[0])
    keep.start()
    if with_ids:
        id_copies = []
        for step in range(1, nz):
            item = pltpu.make_async_remote_copy(
                src_ref=id_ref,
                dst_ref=ids_ref.at[z],
                send_sem=id_s.at[step - 1],
                recv_sem=id_r.at[z],
                device_id={"wide": turn(z, step, nz)},
                device_id_type=MESH,
            )
            item.start()
            id_copies.append(item)
        ids_ref[z] = id_ref[...]

    def pass_x(k):
        zs = turn(z, k, nz)
        for step in range(1, nx):
            xs = turn(x, step, nx)
            arrived(zs, xs, c)
            spread_c(out_ref.at[zs, c, xs], k, step, zs, xs)

    for k in range(1, nz):
        zs = turn(z, k, nz)
        arrived(zs, x, c)
        spread_x(out_ref.at[zs, c, x], k, zs)
        spread_c(out_ref.at[zs, c, x], k, 0, zs, x)
        pass_x(k - 1)
    pass_x(nz - 1)
    for k in range(nz):
        for j in range(nx):
            for step in range(1, nc):
                arrived(turn(z, k, nz), turn(x, j, nx), turn(c, step, nc))
    for item in sent:
        item.wait_send()
    keep.wait()
    if with_ids:
        for step in range(1, nz):
            zs = turn(z, step, nz)
            pltpu.make_async_remote_copy(
                src_ref=id_ref,
                dst_ref=ids_ref.at[zs],
                send_sem=id_s.at[step - 1],
                recv_sem=id_r.at[zs],
                device_id={"wide": zs},
                device_id_type=MESH,
            ).wait_recv()
        for item in id_copies:
            item.wait_send()


def run_gather(own, ids, collective):
    nz, nx, nc = (lax.axis_size(a) for a in ALL)
    dma = pltpu.SemaphoreType.DMA
    with_ids = ids is not None
    shape = jax.ShapeDtypeStruct((nz, nc, nx) + own.shape, own.dtype)
    vmem = pl.BlockSpec(memory_space=pltpu.VMEM)
    anywhere = pl.BlockSpec(memory_space=pl.ANY)
    scratch = [
        dma((nz, nc, nx)),
        dma((max(nz - 1, 1),)),
        dma((nz, max(nx - 1, 1))),
        dma((nz, nx, max(nc - 1, 1))),
        dma((1,)),
    ]
    if with_ids:
        scratch += [dma((nz,)), dma((max(nz - 1, 1),))]
    out = pl.pallas_call(
        functools.partial(gather_kernel, with_ids),
        in_specs=[vmem, vmem] if with_ids else [vmem],
        out_specs=[anywhere, vmem] if with_ids else anywhere,
        out_shape=[shape, jax.ShapeDtypeStruct((nz,) + ids.shape, ids.dtype)] if with_ids else shape,
        scratch_shapes=scratch,
        compiler_params=pltpu.CompilerParams(collective_id=collective, has_side_effects=True),
    )(*([own, ids] if with_ids else [own]))
    depth = own.shape[1]
    if with_ids:
        return out[0].reshape(-1, depth), out[1].reshape(1, -1)
    return out.reshape(-1, depth)


def reduce_kernel(
    part_ref, gain_ref, out_ref, mine, core_in, x_out, x_in, z_out, z_in,
    local_sem, core_s, core_r, x_s, x_r, z_s, z_r,
):
    (z, x, c), (nz, nx, nc) = place()
    f32 = jnp.float32
    greet()
    other = turn(c, 1, nc)
    core, kept = [], []
    for k in range(nz):
        s = turn(z, k + 1, nz)
        item = pltpu.make_async_remote_copy(
            src_ref=part_ref.at[s, other],
            dst_ref=core_in.at[k],
            send_sem=core_s.at[k],
            recv_sem=core_r.at[k],
            device_id={"inner": other},
            device_id_type=MESH,
        )
        item.start()
        core.append(item)
        stay = pltpu.make_async_copy(part_ref.at[s, c], mine.at[k], local_sem.at[k])
        stay.start()
        kept.append(stay)

    def pair(k, xs):
        return mine[k, xs].astype(f32) + core_in[k, xs].astype(f32)

    across, along = [], []

    def finish(k):
        total = pair(k, x)
        for step in range(1, nx):
            across[k][step - 1].wait_recv()
            total = total + x_in[k, step - 1].astype(f32)
        if k == nz - 1:
            return total
        z_out[k] = total.astype(z_out.dtype)
        item = pltpu.make_async_remote_copy(
            src_ref=z_out.at[k],
            dst_ref=z_in.at[k],
            send_sem=z_s.at[k],
            recv_sem=z_r.at[k],
            device_id={"wide": turn(z, k + 1, nz)},
            device_id_type=MESH,
        )
        item.start()
        along.append(item)

    for k in range(nz):
        kept[k].wait()
        core[k].wait_recv()
        items = []
        for step in range(1, nx):
            xs = turn(x, step, nx)
            x_out[k, step - 1] = pair(k, xs).astype(x_out.dtype)
            item = pltpu.make_async_remote_copy(
                src_ref=x_out.at[k, step - 1],
                dst_ref=x_in.at[k, step - 1],
                send_sem=x_s.at[k, step - 1],
                recv_sem=x_r.at[k, step - 1],
                device_id={"expert": xs},
                device_id_type=MESH,
            )
            item.start()
            items.append(item)
        across.append(items)
        if k > 0:
            finish(k - 1)
    total = finish(nz - 1)
    for k in range(nz - 1):
        along[k].wait_recv()
        total = total + z_in[k].astype(f32)
    center = jnp.mean(total, axis=1, keepdims=True)
    spread = jnp.mean(jnp.square(total - center), axis=1, keepdims=True)
    normed = (total - center) * lax.rsqrt(spread + 1e-05) * gain_ref[...].astype(f32)
    out_ref[...] = normed.astype(out_ref.dtype)
    for item in core + along + [i for items in across for i in items]:
        item.wait_send()


def run_reduce(part, gain, share, collective):
    nz, nx, nc = (lax.axis_size(a) for a in ALL)
    width = part.shape[1]
    dma = pltpu.SemaphoreType.DMA
    kind = part.dtype
    part = part.reshape(nz, nc, nx, share, width)
    few = max(nx - 1, 1)
    vmem = pl.BlockSpec(memory_space=pltpu.VMEM)
    return pl.pallas_call(
        reduce_kernel,
        in_specs=[pl.BlockSpec(memory_space=pl.ANY), vmem],
        out_specs=vmem,
        out_shape=jax.ShapeDtypeStruct((share, width), kind),
        scratch_shapes=[
            pltpu.VMEM((nz, nx, share, width), kind),
            pltpu.VMEM((nz, nx, share, width), kind),
            pltpu.VMEM((nz, few, share, width), kind),
            pltpu.VMEM((nz, few, share, width), kind),
            pltpu.VMEM((nz, share, width), kind),
            pltpu.VMEM((nz, share, width), kind),
            dma((nz,)),
            dma((nz,)),
            dma((nz,)),
            dma((nz, few)),
            dma((nz, few)),
            dma((nz,)),
            dma((nz,)),
        ],
        compiler_params=pltpu.CompilerParams(
            collective_id=collective, has_side_effects=True, vmem_limit_bytes=VMEM_LIMIT
        ),
    )(part, gain)


def expert_kernel(tasks, x_ref, gate_ref, win_ref, wout_ref, out_ref, acc_ref):
    rows = x_ref.shape[0]
    columns = gate_ref.shape[1]
    experts_all = columns // tasks
    held, _, _ = win_ref.shape
    width = wout_ref.shape[1]
    x = x_ref[...]
    logits = jnp.dot(x, gate_ref[...], preferred_element_type=jnp.float32)
    task = lax.broadcasted_iota(jnp.int32, (rows, columns), 1) // experts_all
    top = jnp.zeros_like(logits)
    for t in range(tasks):
        high = jnp.max(jnp.where(task == t, logits, -jnp.inf), axis=1, keepdims=True)
        top = jnp.where(task == t, high, top)
    powers = jnp.exp(logits - top)
    total = jnp.ones_like(logits)
    for t in range(tasks):
        part = jnp.sum(jnp.where(task == t, powers, 0.0), axis=1, keepdims=True)
        total = jnp.where(task == t, part, total)
    gates = powers / total
    shift = lax.rem(columns - lax.axis_index("expert") * held, columns)
    gates = pltpu.roll(gates, shift, 1)
    together = min(4, held)
    for first in range(0, held, together):
        made = []
        for e in range(first, first + together):
            hidden = jnp.maximum(
                jnp.dot(x, win_ref[e], preferred_element_type=jnp.float32), 0.0
            ).astype(jnp.bfloat16)
            made.append(
                lax.dot_general(
                    hidden,
                    wout_ref[e],
                    (((1,), (1,)), ((), ())),
                    preferred_element_type=jnp.float32,
                )
            )
        for t in range(tasks):
            piece = None
            for j, output in enumerate(made):
                lane = t * experts_all + first + j
                term = gates[:, lane : lane + 1] * output
                piece = term if piece is None else piece + term
            span = slice(t * width, (t + 1) * width)
            if first > 0:
                piece = piece + acc_ref[:, span]
            if first + together < held:
                acc_ref[:, span] = piece
            else:
                out_ref[:, span] = piece.astype(out_ref.dtype)


def run_experts(x, gate_weight, expert_in, expert_out, tasks):
    rows, depth = x.shape
    held, _, units = expert_in.shape
    width = expert_out.shape[1]
    block = min(512, rows)
    return pl.pallas_call(
        functools.partial(expert_kernel, tasks),
        grid=(rows // block,),
        in_specs=[
            pl.BlockSpec((block, depth), lambda i: (i, 0)),
            pl.BlockSpec(gate_weight.shape, lambda i: (0, 0)),
            pl.BlockSpec(expert_in.shape, lambda i: (0, 0, 0), pipeline_mode=pl.Buffered(1)),
            pl.BlockSpec(expert_out.shape, lambda i: (0, 0, 0), pipeline_mode=pl.Buffered(1)),
        ],
        out_specs=pl.BlockSpec((block, tasks * width), lambda i: (i, 0)),
        out_shape=jax.ShapeDtypeStruct((rows, tasks * width), jnp.bfloat16),
        scratch_shapes=[pltpu.VMEM((block, tasks * width), jnp.float32)],
        compiler_params=pltpu.CompilerParams(vmem_limit_bytes=VMEM_LIMIT),
    )(x, gate_weight, expert_in, expert_out)


def attention_kernel(q_ref, k_ref, v_ref, own_ref, all_ref, weight_ref, out_ref):
    same = own_ref[...] == all_ref[...]
    factor = 1.0 / math.sqrt(HD)
    result = None
    for first in range(0, q_ref.shape[1], HD):
        span = slice(first, first + HD)
        affinity = (
            lax.dot_general(
                q_ref[:, span],
                k_ref[:, span],
                (((1,), (1,)), ((), ())),
                preferred_element_type=jnp.float32,
            )
            * factor
        )
        affinity = jnp.where(same, affinity, -1e30)
        highest = jnp.max(affinity, axis=1, keepdims=True)
        powers = jnp.exp(affinity - highest)
        total = jnp.sum(powers, axis=1, keepdims=True)
        context = jnp.dot(
            powers.astype(jnp.bfloat16), v_ref[:, span], preferred_element_type=jnp.float32
        )
        context = (context / total).astype(jnp.bfloat16)
        term = jnp.dot(context, weight_ref[span, :], preferred_element_type=jnp.float32)
        result = term if result is None else result + term
    out_ref[...] = result


def run_attention(q, k, v, own, every, weight):
    rows, width = q.shape
    keys = k.shape[0]
    tasks = weight.shape[1]
    block = min(128, rows)
    return pl.pallas_call(
        attention_kernel,
        grid=(rows // block,),
        in_specs=[
            pl.BlockSpec((block, width), lambda i: (i, 0)),
            pl.BlockSpec((keys, width), lambda i: (0, 0)),
            pl.BlockSpec((keys, width), lambda i: (0, 0)),
            pl.BlockSpec((block, 1), lambda i: (i, 0)),
            pl.BlockSpec((1, keys), lambda i: (0, 0)),
            pl.BlockSpec((width, tasks), lambda i: (0, 0)),
        ],
        out_specs=pl.BlockSpec((block, tasks), lambda i: (i, 0)),
        out_shape=jax.ShapeDtypeStruct((rows, tasks), jnp.float32),
        compiler_params=pltpu.CompilerParams(vmem_limit_bytes=VMEM_LIMIT),
    )(q, k, v, own, every, weight)


def flip(position, step):
    low = lax.rem(position, 2)
    high = position // 2
    return (high + (step // 2) * (1 - 2 * high)) * 2 + low + lax.rem(step, 2) * (1 - 2 * low)


def remote(src, dst, send, recv, **where):
    return pltpu.make_async_remote_copy(
        src_ref=src, dst_ref=dst, send_sem=send, recv_sem=recv, device_id=where,
        device_id_type=MESH,
    )


TOGETHER = 2
CUTS = 4
PIECES = 4


def mix_part(
    tasks, cand_ref, gate_ref, win_hbm, wout_hbm, gain_ref, nb,
    xbuf, win, wout, gates_all, gates, hidden, made, acc, part, core_in, x_out, x_in, z_out, z_in,
    load_sem, up_s, down_s, z_r, x_s, x_r, c_s, c_r, core_s, core_r, rx_s, rx_r, rz_s, rz_r,
):
    (z, x, c), (nz, nx, nc) = place()
    f32, bf = jnp.float32, jnp.bfloat16
    other_x, other_c = 1 - x, 1 - c
    held = win.shape[0]
    quarters, share, depth = xbuf.shape[1:]
    rows = quarters * share
    width = wout.shape[1]
    spot = c * nx + x
    loads = [
        pltpu.make_async_copy(cand_ref, xbuf.at[z], load_sem.at[0]),
        pltpu.make_async_copy(win_hbm, win, load_sem.at[1]),
        pltpu.make_async_copy(wout_hbm, wout, load_sem.at[2]),
    ]
    for item in loads:
        item.start()
    greet_all()

    piece_rows = share // PIECES
    some = part.shape[2] // CUTS

    def rows_of(h):
        return pl.ds(h * piece_rows, piece_rows)

    def features(f):
        return pl.ds(f * some, some)

    def upward(src, slab, d, h):
        return remote(
            src.at[rows_of(h)], xbuf.at[slab, spot, rows_of(h)], up_s.at[d, h], z_r.at[slab, h],
            wide=z + 1,
        )

    def downward(src, slab, d, h):
        return remote(
            src.at[rows_of(h)], xbuf.at[slab, spot, rows_of(h)], down_s.at[d, h],
            z_r.at[slab, h], wide=z - 1,
        )

    def sideways(slab, q, h):
        piece = xbuf.at[slab, q, rows_of(h)]
        return remote(piece, piece, x_s.at[slab, h], x_r.at[slab, h], expert=other_x)

    def corewise(slab, j, q):
        piece = xbuf.at[slab, q]
        return remote(piece, piece, c_s.at[slab, j], c_r.at[slab, j], inner=other_c)

    for h in range(PIECES):

        @pl.when(z < nz - 1)
        def _():
            upward(cand_ref.at[spot], z, 0, h).start()

        @pl.when(z > 0)
        def _():
            downward(cand_ref.at[spot], z, 0, h).start()

    for item in loads:
        item.wait()

    def arrive_z(d, h):
        below, above = z - d, z + d

        @pl.when(below >= 0)
        def _():
            upward(xbuf.at[below, spot], below, 0, h).wait_recv()

            @pl.when(z < nz - 1)
            def _():
                upward(xbuf.at[below, spot], below, d, h).start()

        @pl.when(above < nz)
        def _():
            downward(xbuf.at[above, spot], above, 0, h).wait_recv()

            @pl.when(z > 0)
            def _():
                downward(xbuf.at[above, spot], above, d, h).start()

        slab = flip(z, d)
        sideways(slab, spot, h).start()
        if h == PIECES - 1:
            corewise(slab, 0, spot).start()

    def arrive_x(slab):
        q = c * nx + other_x
        for h in range(PIECES):
            sideways(slab, q, h).wait_recv()
        corewise(slab, 1, q).start()

    def arrive_c(slab):
        for j, q in ((0, other_c * nx + x), (1, other_c * nx + other_x)):
            corewise(slab, j, q).wait_recv()

    def to_core(k):
        return remote(
            part.at[k, pl.ds(other_c * nx, nx)], core_in.at[k], core_s.at[k], core_r.at[k],
            inner=other_c,
        )

    def to_x(k, f):
        return remote(
            x_out.at[k, features(f)], x_in.at[k, features(f)], rx_s.at[k, f], rx_r.at[k, f],
            expert=other_x,
        )

    def to_z(k, f):
        return remote(
            z_out.at[k, features(f)], z_in.at[k, features(f)], rz_s.at[k, f], rz_r.at[k, f],
            wide=flip(z, 1 if k == 2 else k),
        )

    def reduce_core(k):
        to_core(k).wait_recv()
        for f in range(CUTS):
            x_out[k, features(f)] = (
                part[k, c * nx + other_x, features(f)].astype(f32)
                + core_in[k, other_x, features(f)].astype(f32)
            ).astype(bf)
            to_x(k, f).start()

    def total_of(k, f):
        return (
            part[k, c * nx + x, features(f)].astype(f32)
            + core_in[k, x, features(f)].astype(f32)
            + x_in[k, features(f)].astype(f32)
        )

    def reduce_x(k, f):
        to_x(k, f).wait_recv()
        total = total_of(k, f)
        if k == 3:
            to_z(2, f).wait_recv()
            total = total + z_in[2, features(f)].astype(f32)
        z_out[k, features(f)] = total.astype(bf)
        to_z(k, f).start()

    groups = held // TOGETHER

    def gating(i, k):
        side = (i % 2) * TOGETHER
        for q in range(quarters):
            lanes = slice(q * share, (q + 1) * share)
            weights = [
                [
                    gates[t * held + i * TOGETHER + j : t * held + i * TOGETHER + j + 1, lanes]
                    for j in range(TOGETHER)
                ]
                for t in range(tasks)
            ]
            for f in range(0, width, 16):
                outs = [made[side + j, f : f + 16, lanes] for j in range(TOGETHER)]
                for t in range(tasks):
                    span = slice(t * width + f, t * width + f + 16)
                    piece = weights[t][0] * outs[0]
                    for j in range(1, TOGETHER):
                        piece = piece + weights[t][j] * outs[j]
                    if i > 0:
                        piece = piece + acc[q, span, :]
                    if i < groups - 1:
                        acc[q, span, :] = piece
                    else:
                        part[k, q, span, :] = piece.astype(bf)

    def stage(i, data, k):
        if i < groups:
            for j in range(TOGETHER):
                e = i * TOGETHER + j
                hidden[(i % 2) * TOGETHER + j] = jnp.maximum(
                    jnp.dot(data, win[e], preferred_element_type=f32), 0.0
                ).astype(bf)
        if 0 < i <= groups:
            side = ((i - 1) % 2) * TOGETHER
            for j in range(TOGETHER):
                e = (i - 1) * TOGETHER + j
                made[side + j] = lax.dot_general(
                    wout[e], hidden[side + j], (((1,), (1,)), ((), ())),
                    preferred_element_type=f32,
                )
        if i > 1:
            gating(i - 2, k)

    agenda = (
        (0, 2, lambda: arrive_z(1, 0)),
        (0, 4, lambda: arrive_z(1, 1)),
        (0, 6, lambda: arrive_z(1, 2)),
        (0, 8, lambda: arrive_z(1, 3)),
        (0, 9, lambda: arrive_z(2, 0)),
        (1, 1, lambda: arrive_z(3, 0)),
        (1, 2, lambda: arrive_z(3, 1)),
        (1, 4, lambda: arrive_z(3, 2)),
        (1, 6, lambda: arrive_z(3, 3)),
        (1, 8, lambda: reduce_core(0)),
        (1, 9, lambda: arrive_x(flip(z, 2))),
        (2, 2, lambda: reduce_core(1)),
        (2, 6, lambda: arrive_x(flip(z, 3))),
        (3, 2, lambda: reduce_core(2)),
        (3, 4, lambda: reduce_x(1, 0)),
        (3, 4, lambda: reduce_x(1, 1)),
        (3, 5, lambda: reduce_x(1, 2)),
        (3, 6, lambda: reduce_x(1, 3)),
        (3, 8, lambda: reduce_x(2, 0)),
        (3, 9, lambda: reduce_x(2, 1)),
    )

    def step(k, carry):
        slab = flip(z, k)
        data = xbuf[slab].reshape(rows, depth)
        logits = lax.dot_general(
            gate_ref[...], data, (((0,), (1,)), ((), ())), preferred_element_type=f32
        )
        logits = logits.reshape(tasks, logits.shape[0] // tasks, rows)
        powers = jnp.exp(logits - jnp.max(logits, axis=1, keepdims=True))
        gates_all[...] = powers / jnp.sum(powers, axis=1, keepdims=True)
        for t in range(tasks):
            gates[t * held : (t + 1) * held, :] = gates_all[
                t, pl.ds(pl.multiple_of(x * held, held), held), :
            ]
        after = flip(z, k + 1)
        for i in range(groups + 2):
            for moment, boundary, action in agenda:
                if boundary == i:
                    pl.when(k == moment)(action)
            if i > 0:
                data = xbuf[slab].reshape(rows, depth)
            stage(i, data, k)
        to_core(k).start()

        @pl.when(k == 0)
        def _():
            for h in range(1, PIECES):
                arrive_z(2, h)
            arrive_x(after)

        @pl.when(k < nz - 1)
        def _():
            arrive_c(after)

        return carry

    lax.fori_loop(0, nz, step, 0)
    reduce_x(2, 2)
    reduce_core(3)
    reduce_x(2, 3)
    for f in range(CUTS):
        reduce_x(3, f)
    totals = []
    for f in range(CUTS):
        to_x(0, f).wait_recv()
        total = total_of(0, f)
        for k in (1, 3):
            to_z(k, f).wait_recv()
            total = total + z_in[k, features(f)].astype(f32)
        totals.append(total)
    total = jnp.concatenate(totals, axis=0)
    total = total.T
    center = jnp.mean(total, axis=1, keepdims=True)
    spread = jnp.mean(jnp.square(total - center), axis=1, keepdims=True)
    gain = gain_ref[...].astype(f32)
    gain = jnp.concatenate([gain[i : i + 1, :] for i in range(gain.shape[0])], axis=1)
    normed = (total - center) * lax.rsqrt(spread + 1e-05) * gain
    nb[x, c] = normed.astype(bf)
    yield
    for d in range(nz - 1):
        for h in range(PIECES):

            @pl.when((z < nz - 1) & (z - d >= 0))
            def _():
                upward(xbuf.at[z, spot], z, d, h).wait_send()

            @pl.when((z > 0) & (z + d < nz))
            def _():
                downward(xbuf.at[z, spot], z, d, h).wait_send()

    for k in range(1, nz):
        slab = flip(z, k)
        corewise(slab, 0, spot).wait_send()
        corewise(slab, 1, spot).wait_send()
        for h in range(PIECES):
            sideways(slab, spot, h).wait_send()
        for f in range(CUTS):
            to_z(k, f).wait_send()
    for k in range(nz):
        to_core(k).wait_send()
        for f in range(CUTS):
            to_x(k, f).wait_send()


def greet_all():
    (z, x, c), (nz, nx, nc) = place()
    barrier = pltpu.get_barrier_semaphore()
    pl.semaphore_signal(
        barrier, inc=1, device_id={"expert": 1 - x, "inner": 1 - c}, device_id_type=MESH
    )
    for axis, here, size in zip(ALL, (z, x, c), (nz, nx, nc)):
        for turned in range(1, size):
            pl.semaphore_signal(
                barrier, inc=1, device_id={axis: turn(here, turned, size)}, device_id_type=MESH
            )
    pl.semaphore_wait(barrier, nz + nx + nc - 2)


def whole_kernel(
    tasks, mix_count, cand_ref, gate_ref, win_hbm, wout_hbm, gain_ref,
    q_hbm, k_hbm, v_hbm, task_ref, attn_ref, id_ref, out_ref, *scratch
):
    nb = scratch[mix_count]
    mix = mix_part(
        tasks, cand_ref, gate_ref, win_hbm, wout_hbm, gain_ref, nb, *scratch[:mix_count]
    )
    score = score_part(
        q_hbm, k_hbm, v_hbm, task_ref, attn_ref, id_ref, out_ref, *scratch[mix_count:]
    )
    next(score)
    next(mix)
    next(score, None)
    next(mix, None)


def score_part(
    q_hbm, k_hbm, v_hbm, task_ref, attn_ref, id_ref, out_ref,
    nb, q_ref, k_ref, v_ref, keys, extra, ids, queries, powers, high, sums, partial,
    load_sem, n_s, n_r, id_s, id_r, up_s, down_s, key_r, p_s, p_r,
):
    (z, x, c), (nz, nx, nc) = place()
    f32, bf = jnp.float32, jnp.bfloat16
    other_x, other_c = 1 - x, 1 - c
    _, _, share, depth = nb.shape
    rows = nx * nc * share
    both = nc * share
    heads = queries.shape[0]
    tasks = task_ref.shape[0]
    loads = [
        pltpu.make_async_copy(k_hbm, k_ref, load_sem.at[0]),
        pltpu.make_async_copy(v_hbm, v_ref, load_sem.at[1]),
        pltpu.make_async_copy(q_hbm, q_ref, load_sem.at[2]),
    ]
    for item in loads:
        item.start()
    yield

    def give(side, core, j, **where):
        return remote(nb.at[side, core], nb.at[side, core], n_s.at[j], n_r.at[j], **where)

    first = give(x, c, 0, expert=other_x)
    second = give(x, c, 1, inner=other_c)
    third = give(other_x, c, 2, inner=other_c)
    first.start()
    second.start()
    id_copies = []
    for turned in range(1, nz):
        target = turn(z, turned, nz)
        item = remote(id_ref, ids.at[z], id_s.at[turned], id_r.at[z], wide=target)
        item.start()
        id_copies.append(item)
    ids[z] = id_ref[...]
    for item in loads:
        item.wait()
    own = jnp.concatenate([id_ref[q] for q in range(nx * nc)], axis=1).astype(f32)
    lifted = heads * tasks
    extra[:, :, lifted:, :] = jnp.ones((nz, nx, 16, both), bf)
    shape = (lifted, heads * HD)
    row = lax.broadcasted_iota(jnp.int32, shape, 0) // tasks
    column = lax.broadcasted_iota(jnp.int32, shape, 1) // HD
    stacked = jnp.concatenate([attn_ref[...].astype(f32)] * heads, axis=0)
    blocks = jnp.where(row == column, stacked, 0.0).astype(bf)
    sides = (x, other_x)

    def parts(slab, m):
        return [keys.at[slab, sides[m]], extra.at[slab, sides[m], pl.ds(0, lifted)]]

    def upward(slab, d, m, j):
        piece = parts(slab, m)[j]
        return remote(piece, piece, up_s.at[d, m, j], key_r.at[slab, m, j], wide=z + 1)

    def downward(slab, d, m, j):
        piece = parts(slab, m)[j]
        return remote(piece, piece, down_s.at[d, m, j], key_r.at[slab, m, j], wide=z - 1)

    def announce(m, j):
        @pl.when(z < nz - 1)
        def _():
            upward(z, 0, m, j).start()

        @pl.when(z > 0)
        def _():
            downward(z, 0, m, j).start()

    def pass_on(d, m):
        for slab, here, further, way in (
            (z - d, z - d >= 0, z < nz - 1, upward),
            (z + d, z + d < nz, z > 0, downward),
        ):

            @pl.when(here)
            def _():
                for j in range(2):
                    way(slab, 0, m, j).wait_recv()

                    @pl.when(further)
                    def _():
                        way(slab, d, m, j).start()

    def make(m):
        data = nb[sides[m]].reshape(both, depth)
        keys[z, sides[m]] = jnp.dot(data, k_ref[...], preferred_element_type=f32).astype(bf)
        announce(m, 0)
        values = jnp.dot(data, v_ref[...], preferred_element_type=f32).astype(bf)
        extra[z, sides[m], :lifted, :] = lax.dot_general(
            blocks, values, (((1,), (1,)), ((), ())), preferred_element_type=f32
        ).astype(bf)
        announce(m, 1)

    give(x, other_c, 1, inner=other_c).wait_recv()
    make(0)
    give(other_x, c, 0, expert=other_x).wait_recv()
    third.start()
    pass_on(1, 0)
    give(other_x, other_c, 2, inner=other_c).wait_recv()
    make(1)
    data = jnp.concatenate([nb[q % nx, q // nx] for q in range(nx * nc)], axis=0)
    made = jnp.dot(data, q_ref[...], preferred_element_type=f32) * (1.0 / math.sqrt(HD))
    lane = lax.broadcasted_iota(jnp.int32, (rows, 2 * HD), 1)
    for h in range(heads):
        pair = made[:, h // 2 * 2 * HD : (h // 2 + 1) * 2 * HD]
        queries[h] = jnp.where(lane // HD == h % 2, pair, 0.0).astype(bf)
    for item in id_copies:
        item.wait_send()
    for turned in range(1, nz):
        source = turn(z, turned, nz)
        remote(id_ref, ids.at[source], id_s.at[turned], id_r.at[source], wide=source).wait_recv()

    def attend(slab, m, fresh=False):
        side = sides[m]
        theirs = jnp.concatenate([ids[slab, side], ids[slab, nx + side]], axis=1).astype(f32)
        same = jnp.broadcast_to(theirs, (8, both)).T[:, :1] == own
        tops = []
        for h in range(heads):
            pair = slice(h // 2 * 2 * HD, (h // 2 + 1) * 2 * HD)
            affinity = lax.dot_general(
                keys[slab, side][:, pair], queries[h], (((1,), (1,)), ((), ())),
                preferred_element_type=f32,
            )
            affinity = jnp.where(same, affinity, -1e30)
            top = jnp.max(affinity, axis=0, keepdims=True)
            powers[h] = jnp.exp(affinity - top).astype(bf)
            tops.append(top)
        for h in range(heads):
            got = jnp.dot(extra[slab, side], powers[h], preferred_element_type=f32)
            if fresh:
                high[h] = tops[h]
                sums[h] = got
            else:
                peak = jnp.maximum(high[h], tops[h])
                sums[h] = sums[h] * jnp.exp(high[h] - peak) + got * jnp.exp(tops[h] - peak)
                high[h] = peak

    attend(z, 0, True)
    attend(z, 1)
    pass_on(1, 1)
    attend(flip(z, 1), 0)
    pass_on(2, 0)
    attend(flip(z, 1), 1)
    pass_on(2, 1)
    attend(flip(z, 2), 0)
    attend(flip(z, 2), 1)
    pass_on(3, 0)
    attend(flip(z, 3), 0)
    pass_on(3, 1)
    attend(flip(z, 3), 1)
    result = None
    for h in range(heads):
        term = sums[h, h * tasks : (h + 1) * tasks] / sums[h, lifted : lifted + 1]
        result = term if result is None else result + term
    partial[0] = jnp.concatenate([result, jnp.zeros((8 - tasks, rows), f32)], axis=0)
    sends = []
    for j, where in enumerate(
        ({"inner": other_c}, {"expert": other_x}, {"expert": other_x, "inner": other_c})
    ):
        item = remote(partial.at[0], partial.at[j + 1], p_s.at[j], p_r.at[j], **where)
        item.start()
        sends.append(item)
    base = lax.dot_general(
        task_ref[...], data, (((1,), (1,)), ((), ())), preferred_element_type=f32
    )
    for item in sends:
        item.wait()
    everything = (partial[0] + partial[1]) + (partial[2] + partial[3])
    out_ref[...] = everything[:tasks, :] + base
    first.wait_send()
    second.wait_send()
    third.wait_send()
    for d in range(nz - 1):
        for m in range(2):
            for j in range(2):

                @pl.when((z < nz - 1) & (z - d >= 0))
                def _():
                    upward(z, d, m, j).wait_send()

                @pl.when((z > 0) & (z + d < nz))
                def _():
                    downward(z, d, m, j).wait_send()


def run_whole(
    cand, gate_weight, expert_in, expert_out, gain, query, key, value, task, attn, request_of,
    collective,
):
    nz, nx, nc = (lax.axis_size(a) for a in ALL)
    rows, depth = cand.shape
    quarters = nx * nc
    share = rows // quarters
    held, _, units = expert_in.shape
    width = expert_out.shape[1]
    tasks = task.shape[1]
    dma = pltpu.SemaphoreType.DMA
    f32, bf = jnp.float32, jnp.bfloat16
    vmem = pl.BlockSpec(memory_space=pltpu.VMEM)
    anywhere = pl.BlockSpec(memory_space=pl.ANY)
    model = tasks * width
    experts_all = gate_weight.shape[1] // tasks
    lanes = query.shape[1]
    heads = lanes // HD
    mix_scratch = [
        pltpu.VMEM((nz, quarters, share, depth), bf),
        pltpu.VMEM(expert_in.shape, bf),
        pltpu.VMEM(expert_out.shape, bf),
        pltpu.VMEM((tasks, experts_all, rows), f32),
        pltpu.VMEM((tasks * held, rows), f32),
        pltpu.VMEM((2 * TOGETHER, rows, units), bf),
        pltpu.VMEM((2 * TOGETHER, width, rows), f32),
        pltpu.VMEM((quarters, model, share), f32),
        pltpu.VMEM((nz, quarters, model, share), bf),
        pltpu.VMEM((nz, nx, model, share), bf),
        pltpu.VMEM((nz, model, share), bf),
        pltpu.VMEM((nz, model, share), bf),
        pltpu.VMEM((nz, model, share), bf),
        pltpu.VMEM((nz, model, share), bf),
        dma((3,)),
        dma((nz, PIECES)),
        dma((nz, PIECES)),
        dma((nz, PIECES)),
        dma((nz, PIECES)),
        dma((nz, PIECES)),
        dma((nz, 2)),
        dma((nz, 2)),
        dma((nz,)),
        dma((nz,)),
        dma((nz, CUTS)),
        dma((nz, CUTS)),
        dma((nz, CUTS)),
        dma((nz, CUTS)),
    ]
    columns = heads * tasks + 16
    score_scratch = [
        pltpu.VMEM((nx, nc, share, model), bf),
        pltpu.VMEM(query.shape, bf),
        pltpu.VMEM(key.shape, bf),
        pltpu.VMEM(value.shape, bf),
        pltpu.VMEM((nz, nx, nc * share, lanes), bf),
        pltpu.VMEM((nz, nx, columns, nc * share), bf),
        pltpu.VMEM((nz, quarters, 1, share), jnp.int32),
        pltpu.VMEM((heads, rows, 2 * HD), bf),
        pltpu.VMEM((heads, nc * share, rows), bf),
        pltpu.VMEM((heads, 1, rows), f32),
        pltpu.VMEM((heads, columns, rows), f32),
        pltpu.VMEM((nx * nc, 8, rows), f32),
        dma((3,)),
        dma((3,)),
        dma((3,)),
        dma((nz,)),
        dma((nz,)),
        dma((nz, 2, 2)),
        dma((nz, 2, 2)),
        dma((nz, 2, 2)),
        dma((3,)),
        dma((3,)),
    ]
    return pl.pallas_call(
        functools.partial(whole_kernel, tasks, len(mix_scratch)),
        in_specs=[anywhere, vmem, anywhere, anywhere, vmem, anywhere, anywhere, anywhere]
        + [vmem] * 3,
        out_specs=vmem,
        out_shape=jax.ShapeDtypeStruct((tasks, rows), f32),
        scratch_shapes=mix_scratch + score_scratch,
        compiler_params=pltpu.CompilerParams(
            collective_id=collective, has_side_effects=True, vmem_limit_bytes=VMEM_LIMIT
        ),
    )(
        cand.reshape(quarters, share, depth), gate_weight, expert_in, expert_out,
        gain.reshape(-1, 128), query, key, value, task.T, attn.T,
        request_of.reshape(quarters, 1, share),
    ).T


def fused(sizes, rows, heads, held):
    return sizes == (4, 2, 2) and rows % 512 == 0 and heads == 4 and held == 8 * TOGETHER


def local(
    candidates,
    gate_weight,
    expert_in,
    expert_out,
    norm_gain,
    query_weight,
    key_weight,
    value_weight,
    task_weight,
    attn_weight,
    request_of,
):
    rows = candidates.shape[0]
    tasks = task_weight.shape[1]
    nz, nx, nc = (lax.axis_size(a) for a in ALL)
    if fused((nz, nx, nc), rows, query_weight.shape[1] // HD, expert_in.shape[0]):
        return run_whole(
            candidates, gate_weight, expert_in, expert_out, norm_gain, query_weight, key_weight,
            value_weight, task_weight, attn_weight, request_of, 3,
        )
    share = rows // (nx * nc)
    spot = lax.axis_index("inner") * nx + lax.axis_index("expert")
    wide = lax.axis_index("wide")
    quarter = lax.dynamic_slice_in_dim(candidates, spot * share, share, 0)
    everyone, requests = run_gather(quarter, request_of[None, :], 0)
    partial_mix = run_experts(everyone, gate_weight, expert_in, expert_out, tasks)
    normed = run_reduce(partial_mix, norm_gain[None, :], share, 1)
    normed_all = run_gather(normed, None, 2)
    own = lax.dynamic_slice_in_dim(normed_all, wide * rows, rows, 0)
    queries = jnp.dot(own, query_weight, preferred_element_type=jnp.float32).astype(jnp.bfloat16)
    keys = jnp.dot(normed_all, key_weight, preferred_element_type=jnp.float32).astype(jnp.bfloat16)
    values = jnp.dot(normed_all, value_weight, preferred_element_type=jnp.float32).astype(
        jnp.bfloat16
    )
    term = run_attention(
        queries, keys, values, request_of[:, None], requests, attn_weight
    )
    attention = lax.psum(term.T, ("expert", "inner")).T
    return jnp.dot(own, task_weight, preferred_element_type=jnp.float32) + attention


def solution(mesh):
    return jax.shard_map(
        local,
        mesh=mesh,
        in_specs=(
            P(("groups", "wide"), None),
            P(),
            P("expert", None, ("wide", "inner")),
            P("expert", None, ("wide", "inner")),
            P(),
            P(None, ("expert", "inner")),
            P(None, ("expert", "inner")),
            P(None, ("expert", "inner")),
            P(),
            P(("expert", "inner"), None),
            P(("groups", "wide")),
        ),
        out_specs=P(("groups", "wide"), None),
        check_vma=False,
    )
```
